256 devices in a mesh: dom: 32 (over z, x), head: 8 (over y, core).
Axes of the slice: x: 4, y: 4, z: 8, core: 2. Of those that a mesh axis runs over, the one named last changes fastest.
Arguments:
- node_feats: float32 [32768, 512], P('dom')
- order: int32 [32768], P('dom'), may hold values from 0 to 32767, as said below
- node_count: int32 [256], replicated, may hold values from 32 to 128
- local_blocks: int32 [256, 3], P('dom'), may hold values from 0 to 255, as said below
- exp_blocks: int32 [256, 6], P('dom'), may hold values from 0 to 255, as said below
- virt_blocks: int32 [256], P('dom'), may hold values from 0 to 3
- virt_feats: float32 [512, 512], replicated, may hold values from -6 to 6
- w_query: float32 [512, 512], P(None, 'head'), may hold values from -0.25 to 0.25
- w_key: float32 [512, 512], P(None, 'head'), may hold values from -0.25 to 0.25
- w_value: float32 [512, 512], P(None, 'head'), may hold values from -0.25 to 0.25
- w_out: float32 [512, 512], P(None, 'head'), may hold values from -2 to 2
- w_up: float32 [512, 1024], P(None, 'head'), may hold values from -0.25 to 0.25
- w_down: float32 [1024, 512], P('head'), may hold values from -0.1875 to 0.1875
Outputs:
- refined: float32 [32768, 512], P('dom', 'head')
The draws below stay inside these ranges and needn't reach their ends.
Inputs may be any that keep to these rules, and one draw needn't show every extreme that they name: `order`: each device's 8 * 128 entries are a permutation of that device's own node numbers (the rows it holds). `local_blocks`: every entry lies within 2 clusters of its own cluster; column 1 is exactly 2 away unless that leaves the grid, where it is clipped to the end. `exp_blocks`: call id // 8 the owner of a cluster id. Among the 48 entries of one device's clusters, at most 3 have any one owner, and for every device some owner has exactly 3.
All inputs are finite; a program needn't handle non-finite values.
Results may differ from the reference program's by a relative error of at most 0.0003.
Values sent between devices are 32-bit elements; how exact they have to be, the bound alone decides.
No kernel may reach another device: no remote copies, remote signals or barrier semaphores. Data moves between devices by JAX's collectives and lax.ppermute only.
A program may use at most 128 MiB of HBM per device.

```python
import math
import jax
import jax.numpy as jnp
from jax import lax

D = 512
HEADS = 8
HD = 64
FF = 1024
CL = 128
C_DEV = 8
NE = 6
LW = 2
VB = 4
VN = 512
CLUSTERS = 256
NODES = 32768
CAP = 3
N_DOM = 32


def draw_node_feats(key, part):
    first_key = jax.random.fold_in(key, 0)
    return jax.random.normal(first_key, (NODES, D), jnp.float32)


def draw_order(key, part):
    device_keys = jax.random.split(key, N_DOM)

    def one_device(device_key, device):
        return jax.random.permutation(device_key, C_DEV * CL).astype(jnp.int32) + device * (C_DEV * CL)
    return jax.vmap(one_device)(device_keys, jnp.arange(N_DOM, dtype=jnp.int32)).reshape(-1).astype(jnp.int32)


def draw_local_blocks(key, part):
    first_key, second_key, third_key = jax.random.split(key, 3)
    own_ids = jnp.arange(CLUSTERS, dtype=jnp.int32)
    close_ids = own_ids + jax.random.randint(first_key, (CLUSTERS,), -1, 2)
    signs = jax.random.randint(second_key, (CLUSTERS,), 0, 2) * 2 - 1
    far_ids = own_ids + signs * LW
    other_ids = own_ids + jax.random.randint(third_key, (CLUSTERS,), -LW, LW + 1)
    stacked = jnp.stack([close_ids, far_ids, other_ids], 1)
    return jnp.clip(stacked, 0, CLUSTERS - 1).astype(jnp.int32)


def draw_exp_blocks(key, part):
    device_keys = jax.random.split(key, N_DOM)
    entries = C_DEV * NE

    def one_device(device_key):
        hot_key, pool_key, mix_key, inner_key = jax.random.split(device_key, 4)
        hot_owner = jax.random.randint(hot_key, (), 0, N_DOM)
        others = jnp.arange(N_DOM - 1, dtype=jnp.int32)
        others = others + (others >= hot_owner).astype(jnp.int32)
        pool_ids = jax.random.permutation(pool_key, jnp.repeat(others, CAP))[:entries - CAP]
        owners = jnp.concatenate([jnp.full((CAP,), hot_owner, jnp.int32), pool_ids.astype(jnp.int32)])
        owners = jax.random.permutation(mix_key, owners)
        inside = jax.random.randint(inner_key, (entries,), 0, C_DEV)
        return owners * C_DEV + inside
    return jax.vmap(one_device)(device_keys).reshape(CLUSTERS, NE).astype(jnp.int32)


def place_ends(array, key, least, high):
    index_at = [jax.random.randint(jax.random.fold_in(key, axis), (), 0, length) for axis, length in enumerate(array.shape)]
    widest = array.shape.index(max(array.shape))
    neighbour = index_at[:widest] + [(index_at[widest] + 1) % array.shape[widest]] + index_at[widest + 1:]
    return array.at[tuple(index_at)].set(least).at[tuple(neighbour)].set(high)


def levels(own_key, dims, cuts, smallest, high):
    level = 1.0
    for dim, parts in cuts:
        draws = jax.random.uniform(jax.random.fold_in(jax.random.fold_in(own_key, 6), dim), (parts,), jnp.float32, smallest / len(cuts), high / len(cuts))
        level = level * jnp.repeat(jnp.exp(draws), dims[dim] // parts).reshape((-1,) + (1,) * (len(dims) - 1 - dim))
    return level


def centred(own_key, extent, spread, limit, cuts=(), kind=jnp.bfloat16):
    drawn = spread * jax.random.normal(own_key, extent, jnp.float32)
    if cuts:
        drawn = drawn * levels(own_key, extent, cuts, -0.22, 0.18)
    return jnp.clip(drawn, -limit, limit).astype(kind)


def setup_inputs(seed: int = 0) -> dict:
    seeds = jax.random.split(jax.random.key(seed), 14)
    node_feats = draw_node_feats(jax.random.fold_in(seeds[13], 71), 0)
    order = draw_order(jax.random.fold_in(seeds[13], 71), 0)
    node_count = place_ends(jax.random.randint(seeds[2], (CLUSTERS,), CL // 4, CL + 1), jax.random.fold_in(seeds[2], 1), CL // 4, CL).astype(jnp.int32)
    local_blocks = draw_local_blocks(jax.random.fold_in(seeds[13], 71), 0)
    exp_blocks = draw_exp_blocks(jax.random.fold_in(seeds[13], 71), 0)
    virt_blocks = place_ends(jax.random.randint(seeds[5], (CLUSTERS,), 0, VB), jax.random.fold_in(seeds[5], 1), 0, VB - 1).astype(jnp.int32)
    virt_feats = centred(seeds[6], (VN, D), 1.0, 6.0, (), jnp.float32)
    w_query = centred(seeds[7], (D, D), D ** -0.5, 0.25, ((1, 8),), jnp.float32)
    w_key = centred(seeds[8], (D, D), D ** -0.5, 0.25, ((1, 8),), jnp.float32)
    w_value = centred(seeds[9], (D, D), D ** -0.5, 0.25, ((1, 8),), jnp.float32)
    w_out = centred(seeds[10], (D, D), (D // 64) ** -0.5, 2.0, ((1, 8),), jnp.float32)
    w_up = centred(seeds[11], (D, FF), D ** -0.5, 0.25, ((1, 8),), jnp.float32)
    w_down = centred(seeds[12], (FF, D), FF ** -0.5, 0.1875, ((0, 8),), jnp.float32)
    return {"node_feats": node_feats, "order": order, "node_count": node_count, "local_blocks": local_blocks, "exp_blocks": exp_blocks, "virt_blocks": virt_blocks, "virt_feats": virt_feats, "w_query": w_query, "w_key": w_key, "w_value": w_value, "w_out": w_out, "w_up": w_up, "w_down": w_down}


highest = lax.Precision.HIGHEST

def matmul(left, right):
    return jnp.dot(left, right, preferred_element_type=jnp.float32, precision=highest)

def reference(node_feats, order, node_count, local_blocks, exp_blocks, virt_blocks, virt_feats, w_query, w_key, w_value, w_out, w_up, w_down):
    ordered = node_feats[order]
    queries = matmul(ordered, w_query).reshape(CLUSTERS, CL, HEADS, HD)
    key_rows = matmul(ordered, w_key).reshape(CLUSTERS, CL, HEADS, HD)
    value_rows = matmul(ordered, w_value).reshape(CLUSTERS, CL, HEADS, HD)
    virt_keys = matmul(virt_feats, w_key).reshape(VB, CL, HEADS, HD)
    virt_values = matmul(virt_feats, w_value).reshape(VB, CL, HEADS, HD)
    positions = jnp.arange(CL)

    def attend(cluster):
        block_ids = jnp.concatenate([local_blocks[cluster], exp_blocks[cluster]])
        chosen = virt_blocks[cluster]
        block_keys = jnp.concatenate([key_rows[block_ids], virt_keys[chosen][None]], 0).reshape(-1, HEADS, HD)
        block_values = jnp.concatenate([value_rows[block_ids], virt_values[chosen][None]], 0).reshape(-1, HEADS, HD)
        usable = jnp.concatenate([positions[None, :] < node_count[block_ids][:, None], jnp.ones((1, CL), bool)], 0).reshape(-1)
        scores = jnp.einsum('qhd,khd->hqk', queries[cluster], block_keys, precision=highest) / math.sqrt(HD)
        scores = jnp.where(usable[None, None, :], scores, -1e+30)
        peaks = lax.optimization_barrier(jnp.max(scores, axis=2, keepdims=True))
        weights = jnp.where(usable[None, None, :], jnp.exp(scores - peaks), 0.0)
        totals = lax.optimization_barrier(jnp.sum(weights, axis=2))
        weighted = jnp.einsum('hqk,khd->qhd', weights, block_values, precision=highest)
        return weighted / jnp.transpose(totals)[..., None]
    attention = lax.map(attend, jnp.arange(CLUSTERS)).reshape(NODES, D)
    residual = ordered + matmul(attention, w_out)
    row_mean = lax.optimization_barrier(jnp.mean(residual, axis=1))
    row_square = lax.optimization_barrier(jnp.mean(residual * residual, axis=1))
    row_var = row_square - row_mean * row_mean
    normed = (residual - row_mean[:, None]) * lax.rsqrt(row_var + 1e-05)[:, None]
    hidden = jax.nn.gelu(matmul(normed, w_up), approximate=False)
    result = residual + matmul(hidden, w_down)
    return jnp.zeros_like(result).at[order].set(result)
```

```python
import math

import jax
import jax.numpy as jnp
from jax import lax
from jax.experimental import pallas as pl
from jax.experimental.pallas import tpu as pltpu
from jax.sharding import Mesh, PartitionSpec as P

D = 512
HD = 64
FF = 1024
CL = 128
CD = 8
NE = 6
NL = 3
CAP = 3
NZ, NX, NY, NC = 8, 4, 4, 2
PR = CL // (NY * NC)
EK = NE * CL
LK = (NL + 1) * CL
NEG = -1e30
BF = jnp.bfloat16
F32 = jnp.float32
NT = (((1,), (1,)), ((), ()))
NN = (((1,), (0,)), ((), ()))

GROUPS = ((0, 1, 7), (2, 6), (3, 5, 4))


def split2(v):
    hi = v.astype(BF)
    return hi, (v - hi.astype(F32)).astype(BF)


def mm(a, b, dims):
    return lax.dot_general(a, b, dims, preferred_element_type=F32)


def dot3(ah, al, bh, bl, dims):
    return mm(ah, bh, dims) + (mm(ah, bl, dims) + mm(al, bh, dims))


def vspec():
    return pl.BlockSpec(memory_space=pltpu.VMEM)


def sspec():
    return pl.BlockSpec(memory_space=pltpu.SMEM)


def params(mb=56):
    return pltpu.CompilerParams(vmem_limit_bytes=mb << 20)


def pair_halves(a, b, c, low):
    first = jnp.where(c == 0, a, b)
    second = jnp.where(c == 0, b, a)
    left = jnp.where(low, first, pltpu.roll(second, HD, 1))
    right = jnp.where(low, pltpu.roll(first, HD, 1), second)
    return left, right


def near_kernel(pos, x_ref, xl_ref, bias_ref, *rest):
    w = rest[:16]
    qh, ql, vh, vl, oh, ol, o_out, m_out, l_out, kh, kl = rest[16:]
    y, c = pos[0], pos[1]
    low = lax.broadcasted_iota(jnp.int32, (D, 2 * HD), 1) < HD
    lowq = lax.broadcasted_iota(jnp.int32, (CL, 2 * HD), 1) < HD
    xh, xl = split2(x_ref[...])
    hi, lo = split2(xl_ref[...])
    kh[...] = hi
    kl[...] = lo
    for dy in range(NY):
        qka, voa, qkb, vob = (w[4 * dy + i] for i in range(4))
        at = lax.rem(y - dy + NY, NY)
        wq, wk = pair_halves(qka[...], qkb[...], c, low)
        wv, wo = pair_halves(voa[...], vob[...], c, low)
        q = dot3(xh, xl, *split2(wq), NN) * (1.0 / math.sqrt(HD))
        both = jnp.concatenate([jnp.where(lowq, q, 0.0), jnp.where(lowq, 0.0, q)], 0)
        t = dot3(*split2(both), *split2(wk), NT)
        th, tl = split2(t)
        qh[at] = th
        ql[at] = tl
        wvh, wvl = split2(wv)
        vh[at] = wvh
        vl[at] = wvl
        woh, wol = split2(wo)
        oh[at] = woh
        ol[at] = wol

    def body(p, carry):
        s = dot3(qh[p], ql[p], kh[...], kl[...], NT) + bias_ref[...]
        m = jnp.max(s, axis=1, keepdims=True)
        e = jnp.exp(s - m)
        m_out[p] = m
        l_out[p] = jnp.sum(e, axis=1, keepdims=True)
        a = dot3(*split2(e), kh[...], kl[...], NN)
        o_out[p] = dot3(*split2(a), vh[p], vl[p], NN)
        return carry

    lax.fori_loop(0, NY, body, 0)


def near_call(pos, x_own, xl, bias, weights):
    shapes = [
        ((NY, 2 * CL, D), BF), ((NY, 2 * CL, D), BF),
        ((NY, D, 2 * HD), BF), ((NY, D, 2 * HD), BF),
        ((NY, D, 2 * HD), BF), ((NY, D, 2 * HD), BF),
        ((NY, 2 * CL, 2 * HD), F32), ((NY, 2 * CL, 1), F32), ((NY, 2 * CL, 1), F32),
    ]
    return pl.pallas_call(
        near_kernel,
        out_shape=[jax.ShapeDtypeStruct(s, t) for s, t in shapes],
        in_specs=[sspec()] + [vspec()] * (3 + len(weights)),
        out_specs=[vspec()] * len(shapes),
        scratch_shapes=[pltpu.VMEM((LK, D), BF), pltpu.VMEM((LK, D), BF)],
        compiler_params=params(),
        cost_estimate=pl.CostEstimate(flops=6 * 10**9, bytes_accessed=16 << 20, transcendentals=1 << 20),
        name="near",
    )(pos, x_own, xl, bias, *weights)


def prep_kernel(*refs):
    w = refs[:16]
    uh, ul, dh, dl = refs[16:]
    for i in range(8):
        up, dn = w[2 * i], w[2 * i + 1]
        cols = slice(i * CL, (i + 1) * CL)
        hi, lo = split2(up[...])
        uh[:, cols] = hi
        ul[:, cols] = lo
        for j in range(4):
            hi, lo = split2(dn[j * CL:(j + 1) * CL, :])
            dh[cols, j * CL:(j + 1) * CL] = hi
            dl[cols, j * CL:(j + 1) * CL] = lo


def prep_call(weights):
    shapes = [((D, FF), BF), ((D, FF), BF), ((FF, D), BF), ((FF, D), BF)]
    return pl.pallas_call(
        prep_kernel,
        out_shape=[jax.ShapeDtypeStruct(s, t) for s, t in shapes],
        in_specs=[vspec()] * len(weights),
        out_specs=[vspec()] * len(shapes),
        compiler_params=params(),
        cost_estimate=pl.CostEstimate(flops=10**7, bytes_accessed=8 << 20, transcendentals=0),
        name="prep",
    )(*weights)


def far_kernel(x_ref, xe_ref, bias_ref, qh, ql, vh, vl, oh, ol, o_in, m_in, l_in,
               uh, ul, dh, dl, out_ref, kh, kl, att, res):
    hi, lo = split2(xe_ref[...])
    kh[...] = hi
    kl[...] = lo
    lowq = lax.broadcasted_iota(jnp.int32, (CL, 2 * HD), 1) < HD

    def body(p, carry):
        s = dot3(qh[p], ql[p], kh[...], kl[...], NT) + bias_ref[...]
        m_near = m_in[p]
        m = jnp.maximum(m_near, jnp.max(s, axis=1, keepdims=True))
        e = jnp.exp(s - m)
        scale = jnp.exp(m_near - m)
        total = jnp.sum(e, axis=1, keepdims=True) + l_in[p] * scale
        a = dot3(*split2(e), kh[...], kl[...], NN)
        o = dot3(*split2(a), vh[p], vl[p], NN) + o_in[p] * scale
        o = o / total
        att[p] = jnp.where(lowq, o[:CL], o[CL:])
        return carry

    lax.fori_loop(0, NY, body, 0)
    ah, al = split2(jnp.concatenate([att[p] for p in range(NY)], 1))

    def project(p, carry):
        res[p] = dot3(ah, al, oh[p], ol[p], NN)
        return carry

    lax.fori_loop(0, NY, project, 0)
    r = x_ref[...] + jnp.concatenate([res[p] for p in range(NY)], 1)
    mean = jnp.sum(r, axis=1, keepdims=True) * (1.0 / D)
    square = jnp.sum(r * r, axis=1, keepdims=True) * (1.0 / D)
    normed = (r - mean) * lax.rsqrt(square - mean * mean + 1e-05)
    hid = dot3(*split2(normed), uh[...], ul[...], NN)
    act = 0.5 * hid * (1.0 + lax.erf(hid * math.sqrt(0.5)))
    y = r + dot3(*split2(act), dh[...], dl[...], NN)
    out_ref[...] = y.T


def far_call(x_own, xe, bias, near, ffw):
    args = (x_own, xe, bias) + tuple(near) + tuple(ffw)
    return pl.pallas_call(
        far_kernel,
        out_shape=jax.ShapeDtypeStruct((D, CL), F32),
        in_specs=[vspec()] * len(args),
        out_specs=vspec(),
        scratch_shapes=[pltpu.VMEM((EK, D), BF), pltpu.VMEM((EK, D), BF),
                        pltpu.VMEM((NY, CL, 2 * HD), F32), pltpu.VMEM((NY, CL, 2 * HD), F32)],
        compiler_params=params(),
        cost_estimate=pl.CostEstimate(flops=6 * 10**9, bytes_accessed=16 << 20, transcendentals=1 << 20),
        name="far",
    )(*args)


def place_kernel(r_ref, order_ref, out_ref):
    full = jnp.concatenate([r_ref[i * HD:(i + 1) * HD, :] for i in range(CD)], 1)
    hi = full.astype(BF)
    rest = full - hi.astype(F32)
    mid = rest.astype(BF)
    low = (rest - mid.astype(F32)).astype(BF)
    parts = jnp.concatenate([hi, mid, low], 0)
    step = 256
    for j in range(CD * CL // step):
        nodes = lax.broadcasted_iota(jnp.int32, (step, CD * CL), 0) + j * step
        pick = jnp.where(nodes == order_ref[...], 1.0, 0.0).astype(BF)
        t = mm(parts, pick, NT)
        t = t[:HD] + (t[HD:2 * HD] + t[2 * HD:])
        out_ref[j * step:(j + 1) * step, :] = t.T


def place_call(received, lorder):
    return pl.pallas_call(
        place_kernel,
        out_shape=jax.ShapeDtypeStruct((CD * CL, HD), F32),
        in_specs=[vspec(), vspec()],
        out_specs=vspec(),
        compiler_params=params(),
        cost_estimate=pl.CostEstimate(flops=4 * 10**8, bytes_accessed=1 << 20, transcendentals=0),
        name="place",
    )(received, lorder)


def pick_kernel(n, idx, *refs):
    srcs, outs = refs[:n], refs[n:]
    for k in range(NX):
        for s in range(n):
            for j in range(CAP):
                b = idx[k * n * CAP + s * CAP + j]
                at = pl.multiple_of(b * PR, PR)
                outs[k][(s * CAP + j) * PR:(s * CAP + j + 1) * PR, :] = srcs[s][pl.ds(at, PR), :]


def pick_call(idx, srcs):
    n = len(srcs)
    rows = n * CAP * PR
    return pl.pallas_call(
        lambda *refs: pick_kernel(n, *refs),
        out_shape=[jax.ShapeDtypeStruct((rows, D), F32)] * NX,
        in_specs=[sspec()] + [vspec()] * n,
        out_specs=[vspec()] * NX,
        compiler_params=params(),
        cost_estimate=pl.CostEstimate(flops=0, bytes_accessed=NX * rows * D * 8, transcendentals=0),
        name="pick",
    )(idx, *srcs)


def send_kernel(which, row, *refs):
    srcs, out = refs[:-1], refs[-1]

    def body(i, carry):
        w = which[i]
        at = pl.multiple_of(row[i], PR)
        to = pl.multiple_of(i * PR, PR)
        for n, src in enumerate(srcs):
            @pl.when(w == n)
            def _(src=src):
                out[pl.ds(to, PR), :] = src[pl.ds(at, PR), :]
        return carry

    lax.fori_loop(0, CD * NE, body, 0)


def send_call(which, row, srcs):
    return pl.pallas_call(
        send_kernel,
        out_shape=jax.ShapeDtypeStruct((CD * NE * PR, D), F32),
        in_specs=[sspec()] * 2 + [vspec()] * len(srcs),
        out_specs=vspec(),
        compiler_params=params(),
        cost_estimate=pl.CostEstimate(flops=0, bytes_accessed=6 << 20, transcendentals=0),
        name="send",
    )(which, row, *srcs)


def ring(size, step):
    return [(i, (i + step) % size) for i in range(size)]


def shards(node_feats, order, node_count, local_blocks, exp_blocks, virt_blocks, virt_feats,
           w_query, w_key, w_value, w_out, w_up, w_down):
    z, x, y, c = (lax.axis_index(a) for a in ("z", "x", "y", "c"))
    dom = z * NX + x
    head = y * NC + c
    first = dom * CD
    lorder = (order - dom * (CD * CL)).reshape(CD, CL)

    def rows_of(index):
        return node_feats.at[index].get(mode="promise_in_bounds", unique_indices=True)

    piece_rows = lax.dynamic_index_in_dim(lorder.reshape(CD, NY * NC, PR), head, 1, False).reshape(-1)
    edge = jnp.where(head < NY, CD - NC + c, c)
    edge_rows = lax.dynamic_index_in_dim(lorder, edge, 0, False)
    piece = rows_of(piece_rows)
    edge_feats = rows_of(edge_rows)

    flat = exp_blocks.reshape(-1)
    owner = flat // CD
    inside = flat % CD
    n_req = CD * NE
    earlier = jnp.arange(n_req)[:, None] > jnp.arange(n_req)[None, :]
    rank = jnp.sum(jnp.where(earlier & (owner[:, None] == owner[None, :]), 1, 0), 1)
    slot = owner * CAP + rank
    table = jnp.sum(
        jnp.where(slot[None, :] == jnp.arange(NZ * NX * CAP)[:, None], inside[None, :], 0), 1
    ).reshape(NZ, NX, CAP)
    asked = [lax.dynamic_index_in_dim(table, x, 1, False)]
    for k in range(1, NX):
        mine = lax.dynamic_index_in_dim(table, (x - k) % NX, 1, False)
        asked.append(lax.ppermute(mine, "x", ring(NX, -k)))
    asked = jnp.roll(jnp.stack(asked, 0), -z, axis=1)

    half = CD // 2 * PR
    ups = [piece[:half], piece[half:]]
    downs = [piece[:half], piece[half:]]
    held = {0: [piece[:half], piece[half:]]}
    for step in range(1, 4):
        for i in range(2):
            ups[i] = lax.ppermute(ups[i], "z", ring(NZ, 1))
            downs[i] = lax.ppermute(downs[i], "z", ring(NZ, -1))
        held[NZ - step] = list(ups)
        held[step] = list(downs)
    held[4] = [lax.ppermute(ups[0], "z", ring(NZ, 1)), lax.ppermute(downs[1], "z", ring(NZ, -1))]

    picked = []
    for group in GROUPS:
        idx = asked[:, jnp.array(group), :].reshape(-1)
        outs = pick_call(idx, [jnp.concatenate(held[s], 0) for s in group])
        picked.append([outs[0]] + [lax.ppermute(outs[k], "x", ring(NX, k)) for k in range(1, NX)])

    def gather_weights(v):
        n = v.shape[0] // 2
        u = lax.ppermute(v, "y", ring(NY, 1))
        d = lax.ppermute(v, "y", ring(NY, -1))
        e = lax.ppermute(u[:n], "y", ring(NY, 1))
        f = lax.ppermute(d[n:], "y", ring(NY, -1))
        mine = [v, u, d, e, f]
        other = [lax.ppermute(t, "c", [(0, 1), (1, 0)]) for t in mine]
        out = []
        for dy in range(NY):
            for t in (mine, other):
                if dy == 2:
                    out += [t[3], t[4]]
                else:
                    whole = t[(0, 1, None, 2)[dy]]
                    out += [whole[:n], whole[n:]]
        return out

    wa = gather_weights(jnp.concatenate(
        [jnp.concatenate([w_query, w_key], 1), jnp.concatenate([w_value, w_out], 1)], 0))
    wb = gather_weights(jnp.concatenate(
        [w_up] + [w_down[:, j * CL:(j + 1) * CL] for j in range(4)], 0))

    e_in = lax.ppermute(edge_feats, ("z", "x", "y", "c"), [
        (d * CD + h, (d + s) * CD + h)
        for s, hs in ((1, (0, 1)), (-1, (6, 7)))
        for d in range(NZ * NX) if 0 <= d + s < NZ * NX for h in hs])
    e_other = lax.ppermute(e_in, "c", [(0, 1), (1, 0)])
    edges = jnp.stack([jnp.where(c == 0, e_in, e_other), jnp.where(c == 0, e_other, e_in)], 0)
    own_local = lax.dynamic_index_in_dim(local_blocks, head, 0, False)
    own_exp = lax.dynamic_index_in_dim(exp_blocks, head, 0, False)
    rel = own_local - first
    inside_dom = (rel >= 0) & (rel < CD)
    near_rows = jnp.take(lorder, jnp.clip(rel, 0, CD - 1), axis=0, mode="clip").reshape(-1)
    own_rows = lax.dynamic_index_in_dim(lorder, head, 0, False)
    x_own = rows_of(own_rows)
    near_feats = node_feats.at[near_rows].get(mode="promise_in_bounds").reshape(NL, CL, D)
    edge_at = jnp.clip(jnp.where(rel < 0, rel + NC, rel - CD), 0, NC - 1)
    from_edge = jnp.where((edge_at == 0)[:, None, None], edges[0], edges[1])
    near_feats = jnp.where(inside_dom[:, None, None], near_feats, from_edge)
    own_virt = lax.dynamic_index_in_dim(virt_blocks, head, 0, False)
    virt = lax.dynamic_slice_in_dim(virt_feats, own_virt * CL, CL, 0)
    xl = jnp.concatenate([near_feats.reshape(-1, D), virt], 0)
    slots = jnp.arange(CL)

    def bias_of(ids):
        return jnp.where(slots[None, :] < jnp.take(node_count, ids, mode="clip")[:, None], 0.0, NEG)

    near_bias = jnp.concatenate([bias_of(own_local).reshape(-1), jnp.zeros((CL,), F32)])[None, :]
    far_bias = jnp.transpose(bias_of(own_exp).reshape(NE, CD, PR), (1, 0, 2)).reshape(1, EK)

    pos = jnp.stack([y, c]).astype(jnp.int32)
    near = near_call(pos, x_own, xl, near_bias, wa)
    ffw = prep_call(wb)

    rel_z = (owner // NX - z) % NZ
    rel_x = (x - owner % NX) % NX
    group_of = [0] * NZ
    place_of = [0] * NZ
    for g, group in enumerate(GROUPS):
        for p, s in enumerate(group):
            group_of[s], place_of[s] = g, p
    which = jnp.array(group_of)[rel_z] * NX + rel_x
    row = (jnp.array(place_of)[rel_z] * CAP + rank) * PR
    sending = send_call(which.astype(jnp.int32), row.astype(jnp.int32), [t for g in picked for t in g])
    xe = lax.all_to_all(sending, ("y", "c"), 0, 0, tiled=True)

    result = far_call(x_own, xe, far_bias, near, ffw)
    received = lax.all_to_all(result, ("y", "c"), 0, 0, tiled=True)
    return place_call(received, lorder.reshape(1, CD * CL))


def solution(mesh):
    grid = Mesh(mesh.devices.reshape(NZ, NX, NY, NC), ("z", "x", "y", "c"))
    dom, head = ("z", "x"), ("y", "c")
    return jax.shard_map(
        shards,
        mesh=grid,
        in_specs=(P(dom, None), P(dom), P(), P(dom, None), P(dom, None), P(dom), P(),
                  P(None, head), P(None, head), P(None, head), P(None, head), P(None, head),
                  P(head, None)),
        out_specs=P(dom, head),
        check_vma=False,
    )
```

```python
import math

import jax
import jax.numpy as jnp
from jax import lax
from jax.experimental import pallas as pl
from jax.experimental.pallas import tpu as pltpu
from jax.sharding import Mesh, PartitionSpec as P

D = 512
HD = 64
FF = 1024
CL = 128
CD = 8
NE = 6
NL = 3
CAP = 3
NZ, NX, NY, NC = 8, 4, 4, 2
PR = CL // (NY * NC)
EK = NE * CL
LK = (NL + 1) * CL
NEG = -1e30
BF = jnp.bfloat16
F32 = jnp.float32
NT = (((1,), (1,)), ((), ()))
NN = (((1,), (0,)), ((), ()))

GROUPS = ((0, 1, 7, 2, 6), (3, 5, 4))


def split2(v):
    hi = v.astype(BF)
    return hi, (v - hi.astype(F32)).astype(BF)


def mm(a, b, dims):
    return lax.dot_general(a, b, dims, preferred_element_type=F32)


def dot3(ah, al, bh, bl, dims):
    return mm(ah, bh, dims) + (mm(ah, bl, dims) + mm(al, bh, dims))


def vspec():
    return pl.BlockSpec(memory_space=pltpu.VMEM)


def sspec():
    return pl.BlockSpec(memory_space=pltpu.SMEM)


def params(mb):
    return pltpu.CompilerParams(vmem_limit_bytes=mb << 20)


def cost(flops, bytes_accessed, transcendentals=0):
    return pl.CostEstimate(flops=flops, bytes_accessed=bytes_accessed, transcendentals=transcendentals)


def sds(*shape, dtype=F32):
    return jax.ShapeDtypeStruct(shape, dtype)


def columns(row):
    return jnp.broadcast_to(row, (CL, CL)).T


def one_hot(cols):
    lanes = lax.broadcasted_iota(jnp.int32, cols.shape, 1).astype(F32)
    parts = [jnp.where(cols == lanes + float(j * CL), 1.0, 0.0).astype(BF) for j in range(CD)]
    return jnp.concatenate(parts, 1)


def first_kernel(pos, order_ref, nodes_ref, piece_out, edge_out):
    base, head, c = pos[0], pos[1], pos[2]
    order = (order_ref[...] - base).astype(F32)
    mine = pltpu.roll(order, lax.rem(CL - head * PR, CL), 1)
    col = jnp.concatenate([mine] + [jnp.zeros((CL - CD, CL), F32)], 0).T
    pieces = [jnp.broadcast_to(col[:PR, k:k + 1], (PR, CL)) for k in range(CD)]
    edge = jnp.where(head < NY, CD - NC + c, c)
    edge_row = (order_ref[pl.ds(edge, 1), :] - base).astype(F32)
    pick = one_hot(jnp.concatenate(pieces + [columns(edge_row)], 0))
    hi, lo = split2(nodes_ref[...])
    rows = mm(pick, hi, NN) + mm(pick, lo, NN)
    piece_out[...] = rows[:CL]
    edge_out[...] = rows[CL:]


def first_call(pos, order, nodes):
    return pl.pallas_call(
        first_kernel,
        out_shape=[sds(CL, D), sds(CL, D)],
        in_specs=[sspec(), vspec(), vspec()],
        out_specs=[vspec()] * 2,
        compiler_params=params(12),
        cost_estimate=cost(10**9, 3 << 20),
        name="first",
    )(pos, order, nodes)


def index_kernel(pos, exp_ref, t0, t1, t2, t3, row, seen):
    z, x = pos[0], pos[1]
    tables = (t0, t1, t2, t3)

    def clear(i, carry):
        for t in tables:
            t[i] = 0
        return carry

    lax.fori_loop(0, NZ * CAP, clear, 0)

    def unseen(i, carry):
        seen[i] = 0
        return carry

    lax.fori_loop(0, NZ * NX, unseen, 0)

    def place(i, carry):
        for e in range(NE):
            block = exp_ref[i, e]
            owner = lax.shift_right_logical(block, 3)
            inside = lax.bitwise_and(block, CD - 1)
            rank = seen[owner]
            seen[owner] = rank + 1
            oz = lax.shift_right_logical(owner, 2)
            back = lax.bitwise_and(x - lax.bitwise_and(owner, NX - 1), NX - 1)
            for k, t in enumerate(tables):
                @pl.when(back == k)
                def _(t=t):
                    t[oz * CAP + rank] = inside
            off = lax.bitwise_and(oz - z, NZ - 1)
            at = jnp.int32(0)
            base = 0
            for n, group in enumerate(GROUPS):
                for p, s in enumerate(group):
                    at = jnp.where(off == s, base + back * (len(group) * CAP) + p * CAP, at)
                base += NX * len(group) * CAP
            row[i * NE + e] = (at + rank) * PR
        return carry

    lax.fori_loop(0, CD, place, 0)


def index_call(pos, exp_blocks):
    t = sds(NZ * CAP, dtype=jnp.int32)
    return pl.pallas_call(
        index_kernel,
        out_shape=[t] * NX + [sds(CD * NE, dtype=jnp.int32)],
        in_specs=[sspec()] * 2,
        out_specs=[sspec()] * (NX + 1),
        scratch_shapes=[pltpu.SMEM((NZ * NX,), jnp.int32)],
        compiler_params=params(2),
        cost_estimate=cost(1000, 4096),
        name="index",
    )(pos, exp_blocks)


def pack_kernel(q, k, v, o, up, down, out):
    for i, w in enumerate((q, k, v, o)):
        out[i * HD:(i + 1) * HD, :] = w[...]
    out[2 * CL:3 * CL, :] = down[...]
    for j in range(4):
        out[3 * CL:, j * CL:(j + 1) * CL] = up[j * CL:(j + 1) * CL, :]


def pack_call(*w):
    return pl.pallas_call(
        pack_kernel,
        out_shape=sds(D, D),
        in_specs=[vspec()] * 6,
        out_specs=vspec(),
        compiler_params=params(5),
        cost_estimate=cost(0, 2 << 20),
        name="pack",
    )(*w)


def near_kernel(pos, local_ref, virt_ref, count_ref, order_ref, nodes_ref, e_in, e_other, virtual_ref, *rest):
    w = rest[:8]
    x_out, qh, ql, vh, vl, oh, ol, o_out, m_out, l_out, kh, kl = rest[8:]
    base, head, c, y = pos[0], pos[1], pos[2], pos[3]
    first = lax.shift_right_logical(base, 7)

    def order_row(r):
        return columns((order_ref[pl.ds(r, 1), :] - base).astype(F32))

    rel = [local_ref[head, j] - first for j in range(NL)]
    rows = [order_row(jnp.clip(r, 0, CD - 1)) for r in rel] + [order_row(head)]
    pick = one_hot(jnp.concatenate(rows, 0))
    nodes = nodes_ref[...]
    hi, lo = split2(nodes)
    got = mm(pick, hi, NN) + mm(pick, lo, NN)
    last = (nodes - hi.astype(F32) - lo.astype(F32)).astype(BF)
    x = got[NL * CL:] + mm(pick[NL * CL:], last, NN)
    x_out[...] = x
    lane = lax.broadcasted_iota(jnp.int32, (1, CL), 1)
    bias = []
    for j in range(NL):
        r = rel[j]
        at = jnp.where(r < 0, r + NC, r - CD)
        edge = jnp.where(at == c, e_in[...], e_other[...])
        keys = jnp.where((r >= 0) & (r < CD), got[j * CL:(j + 1) * CL], edge)
        kh[j * CL:(j + 1) * CL, :], kl[j * CL:(j + 1) * CL, :] = split2(keys)
        bias.append(jnp.where(lane < count_ref[local_ref[head, j]], 0.0, NEG))
    vat = pl.multiple_of(virt_ref[head] * CL, CL)
    kh[NL * CL:, :], kl[NL * CL:, :] = split2(virtual_ref[pl.ds(vat, CL), :])
    bias = jnp.concatenate(bias + [jnp.zeros((1, CL), F32)], 1)

    lowq = lax.broadcasted_iota(jnp.int32, (CL, 2 * HD), 1) < HD
    xh, xl = split2(x)
    for dy in range(NY):
        a, b = w[2 * dy][:2 * CL, :], w[2 * dy + 1][:2 * CL, :]
        at = lax.rem(y - dy + NY, NY)
        left = jnp.where(c == 0, a, b)
        right = jnp.where(c == 0, b, a)
        wq, wk, wv, wo = (
            split2(jnp.concatenate([left[i * HD:(i + 1) * HD], right[i * HD:(i + 1) * HD]], 0))
            for i in range(4))
        q = dot3(xh, xl, *wq, NT) * (1.0 / math.sqrt(HD))
        both = jnp.concatenate([jnp.where(lowq, q, 0.0), jnp.where(lowq, 0.0, q)], 0)
        qh[at], ql[at] = split2(dot3(*split2(both), *wk, NN))
        vh[at], vl[at] = wv
        oh[at], ol[at] = wo

    def body(p, carry):
        s = dot3(qh[p], ql[p], kh[...], kl[...], NT) + bias
        m = jnp.max(s, axis=1, keepdims=True)
        e = jnp.exp(s - m)
        m_out[p] = m
        l_out[p] = jnp.sum(e, axis=1, keepdims=True)
        a = dot3(*split2(e), kh[...], kl[...], NN)
        o_out[p] = dot3(*split2(a), vh[p], vl[p], NT)
        return carry

    lax.fori_loop(0, NY, body, 0)


def near_call(scalars, arrays, weights):
    shapes = [
        sds(CL, D), sds(NY, 2 * CL, D, dtype=BF), sds(NY, 2 * CL, D, dtype=BF),
        sds(NY, 2 * HD, D, dtype=BF), sds(NY, 2 * HD, D, dtype=BF),
        sds(NY, 2 * HD, D, dtype=BF), sds(NY, 2 * HD, D, dtype=BF),
        sds(NY, 2 * CL, 2 * HD), sds(NY, 2 * CL, 1), sds(NY, 2 * CL, 1),
    ]
    return pl.pallas_call(
        near_kernel,
        out_shape=shapes,
        in_specs=[sspec()] * len(scalars) + [vspec()] * len(arrays)
        + [vspec()] * len(weights),
        out_specs=[vspec()] * len(shapes),
        scratch_shapes=[pltpu.VMEM((LK, D), BF), pltpu.VMEM((LK, D), BF)],
        compiler_params=params(32),
        cost_estimate=cost(6 * 10**9, 16 << 20, 1 << 20),
        name="near",
    )(*scalars, *arrays, *weights)


def prep_kernel(*refs):
    w = refs[:8]
    uh, ul, dh, dl = refs[8:]
    for i in range(8):
        rows = slice(i * CL, (i + 1) * CL)
        start = w[i].shape[0] - 2 * CL
        dh[rows, :], dl[rows, :] = split2(w[i][start:start + CL, :])
        hi, lo = split2(w[i][start + CL:, :])
        for j in range(4):
            cols = slice(j * CL, (j + 1) * CL)
            uh[cols, rows] = hi[:, cols]
            ul[cols, rows] = lo[:, cols]


def prep_call(weights):
    return pl.pallas_call(
        prep_kernel,
        out_shape=[sds(D, FF, dtype=BF), sds(D, FF, dtype=BF), sds(FF, D, dtype=BF), sds(FF, D, dtype=BF)],
        in_specs=[vspec()] * len(weights),
        out_specs=[vspec()] * 4,
        compiler_params=params(16),
        cost_estimate=cost(10**7, 8 << 20),
        name="prep",
    )(*weights)


def far_kernel(pos, exp_ref, count_ref, x_ref, xe_ref, qh, ql, vh, vl, oh, ol, o_in, m_in, l_in,
               uh, ul, dh, dl, out_ref, kh, kl):
    head = pos[1]
    hi, lo = split2(xe_ref[...])
    kh[...] = hi
    kl[...] = lo
    lowq = lax.broadcasted_iota(jnp.int32, (CL, 2 * HD), 1) < HD
    n = lax.broadcasted_iota(jnp.int32, (1, EK), 1)

    def steps(v, width, count):
        return sum(jnp.where(v >= width * k, 1, 0) for k in range(1, count))

    piece = steps(n, NE * PR, CD)
    r = n - piece * (NE * PR)
    entry = steps(r, PR, NE)
    slot = piece * PR + r - entry * PR
    bias = jnp.zeros((1, EK), F32)
    for e in range(NE):
        bad = (entry == e) & (slot >= count_ref[exp_ref[head, e]])
        bias = jnp.where(bad, NEG, bias)

    def scores(p):
        return dot3(qh[p], ql[p], kh[...], kl[...], NT) + bias

    att = []
    s_next = scores(0)
    for p in range(NY):
        s = s_next
        if p + 1 < NY:
            s_next = scores(p + 1)
        m_near = m_in[p]
        m = jnp.maximum(m_near, jnp.max(s, axis=1, keepdims=True))
        e = jnp.exp(s - m)
        scale = jnp.exp(m_near - m)
        total = jnp.sum(e, axis=1, keepdims=True) + l_in[p] * scale
        a = dot3(*split2(e), kh[...], kl[...], NN)
        o = dot3(*split2(a), vh[p], vl[p], NT) + o_in[p] * scale
        o = o / total
        att.append(jnp.where(lowq, o[:CL], o[CL:]))

    ah, al = split2(jnp.concatenate(att, 1))
    r = x_ref[...] + dot3(ah, al, oh[...].reshape(D, D), ol[...].reshape(D, D), NT)
    mean = jnp.sum(r, axis=1, keepdims=True) * (1.0 / D)
    square = jnp.sum(r * r, axis=1, keepdims=True) * (1.0 / D)
    normed = (r - mean) * lax.rsqrt(square - mean * mean + 1e-05)
    hid = dot3(*split2(normed), uh[...], ul[...], NN)
    act = 0.5 * hid * (1.0 + lax.erf(hid * math.sqrt(0.5)))
    y = r + dot3(*split2(act), dh[...], dl[...], NN)
    out_ref[...] = y.T


def far_call(scalars, arrays):
    return pl.pallas_call(
        far_kernel,
        out_shape=sds(D, CL),
        in_specs=[sspec()] * len(scalars) + [vspec()] * len(arrays),
        out_specs=vspec(),
        scratch_shapes=[pltpu.VMEM((EK, D), BF), pltpu.VMEM((EK, D), BF)],
        compiler_params=params(32),
        cost_estimate=cost(6 * 10**9, 16 << 20, 1 << 20),
        name="far",
    )(*scalars, *arrays)


def place_kernel(pos, r_ref, order_ref, out_ref):
    full = jnp.concatenate([r_ref[i * HD:(i + 1) * HD, :] for i in range(CD)], 1)
    order = jnp.concatenate([order_ref[i:i + 1, :] for i in range(CD)], 1) - pos[0]
    hi = full.astype(BF)
    rest = full - hi.astype(F32)
    mid = rest.astype(BF)
    low = (rest - mid.astype(F32)).astype(BF)
    parts = jnp.concatenate([hi, mid, low], 0)
    step = 256
    for j in range(CD * CL // step):
        nodes = lax.broadcasted_iota(jnp.int32, (step, CD * CL), 0) + j * step
        pick = jnp.where(nodes == order, 1.0, 0.0).astype(BF)
        t = mm(parts, pick, NT)
        out_ref[:, j * step:(j + 1) * step] = t[:HD] + (t[HD:2 * HD] + t[2 * HD:])


def place_call(pos, received, order):
    return pl.pallas_call(
        place_kernel,
        out_shape=sds(HD, CD * CL),
        in_specs=[sspec(), vspec(), vspec()],
        out_specs=vspec(),
        compiler_params=params(12),
        cost_estimate=cost(4 * 10**8, 1 << 20),
        name="place",
    )(pos, received, order)


def pick_kernel(group, pos, *refs):
    tables, srcs, out = refs[:NX], refs[NX:-1], refs[-1]
    z, x = pos[0], pos[1]
    n = len(group)
    parts, at = [], 0
    for s in group:
        size = 2 if s == NZ // 2 else 1
        parts.append(srcs[at:at + size])
        at += size
    for k in range(NX):
        to = pl.multiple_of(lax.bitwise_and(x + k, NX - 1) * (n * CAP * PR), PR)
        for i, s in enumerate(group):
            src = parts[i]
            for j in range(CAP):
                b = tables[k][lax.bitwise_and(z + s, NZ - 1) * CAP + j]
                if len(src) == 1:
                    v = src[0][pl.ds(pl.multiple_of(b * PR, PR), PR), :]
                else:
                    at = pl.multiple_of(lax.bitwise_and(b, CD // 2 - 1) * PR, PR)
                    v = jnp.where(b < CD // 2, src[0][pl.ds(at, PR), :], src[1][pl.ds(at, PR), :])
                out[pl.ds(pl.multiple_of(to + (i * CAP + j) * PR, PR), PR), :] = v


def pick_call(group, pos, tables, srcs):
    rows = len(group) * CAP * PR
    return pl.pallas_call(
        lambda *refs: pick_kernel(group, *refs),
        out_shape=sds(NX * rows, D),
        in_specs=[sspec()] * (1 + NX) + [vspec()] * len(srcs),
        out_specs=vspec(),
        compiler_params=params(8),
        cost_estimate=cost(0, NX * rows * D * 8),
        name="pick",
    )(pos, *tables, *srcs)


def send_kernel(pos, row, *refs):
    srcs, out, held = refs[:-2], refs[-2], refs[-1]
    x = pos[1]
    at = 0
    for src, group in zip(srcs, GROUPS):
        rows = len(group) * CAP * PR
        for k in range(NX):
            start = pl.multiple_of(lax.bitwise_and(x - k, NX - 1) * rows, PR)
            held[at + k * rows:at + (k + 1) * rows, :] = src[pl.ds(start, rows), :]
        at += NX * rows
    for i in range(CD * NE):
        r = pl.multiple_of(row[i], PR)
        out[i * PR:(i + 1) * PR, :] = held[pl.ds(r, PR), :]


def send_call(pos, row, srcs):
    return pl.pallas_call(
        send_kernel,
        out_shape=sds(CD * NE * PR, D),
        in_specs=[sspec()] * 2 + [vspec()] * len(srcs),
        out_specs=vspec(),
        scratch_shapes=[pltpu.VMEM((NZ * NX * CAP * PR, D), F32)],
        compiler_params=params(12),
        cost_estimate=cost(0, 6 << 20),
        name="send",
    )(pos, row, *srcs)


def ring(size, step):
    return [(i, (i + step) % size) for i in range(size)]


SWAP = [(0, 1), (1, 0)]


def shards(node_feats, order, node_count, local_blocks, exp_blocks, virt_blocks, virt_feats,
           w_query, w_key, w_value, w_out, w_up, w_down):
    z, x, y, c = (lax.axis_index(a) for a in ("z", "x", "y", "c"))
    head = y * NC + c
    pos = jnp.stack([(z * NX + x) * (CD * CL), head, c, y]).astype(jnp.int32)
    zx = jnp.stack([z, x]).astype(jnp.int32)
    order = order.reshape(CD, CL)

    piece, edge = first_call(pos, order, node_feats)

    half = CL // 2
    up = lax.ppermute(piece, "z", ring(NZ, 1))
    down = lax.ppermute(piece, "z", ring(NZ, -1))
    held = {0: (piece,)}

    out = index_call(zx, exp_blocks)
    tables = [out[0]] + [lax.ppermute(out[k], "x", ring(NX, -k)) for k in range(1, NX)]
    row = out[-1]

    v = pack_call(w_query.T, w_key.T, w_value.T, w_out.T, w_up, w_down)
    u = lax.ppermute(v, "y", ring(NY, 1))
    d = lax.ppermute(v, "y", ring(NY, -1))
    e = lax.ppermute(u[:2 * CL], "y", ring(NY, 1))
    f = lax.ppermute(d[2 * CL:], "y", ring(NY, -1))
    mine = [v, u, e, d, f]
    other = [lax.ppermute(t, "c", SWAP) for t in mine]
    wa = [t[i] for i in range(4) for t in (mine, other)]
    wb = [t[i] for i in (0, 1, 4, 3) for t in (mine, other)]

    for step in range(1, 4):
        held[NZ - step] = (up,)
        held[step] = (down,)
        if step < 3:
            up, down = lax.ppermute(up, "z", ring(NZ, 1)), lax.ppermute(down, "z", ring(NZ, -1))
    held[4] = (lax.ppermute(up[:half], "z", ring(NZ, 1)), lax.ppermute(down[half:], "z", ring(NZ, -1)))

    arrived = []
    for group in GROUPS:
        blocks = pick_call(group, zx, tables, [t for s in group for t in held[s]])
        arrived.append(lax.all_to_all(blocks, "x", 0, 0, tiled=True))

    e_in = lax.ppermute(edge, ("z", "x", "y", "c"), [
        (i * CD + h, (i + s) * CD + h)
        for s, hs in ((1, (0, 1)), (-1, (6, 7)))
        for i in range(NZ * NX) if 0 <= i + s < NZ * NX for h in hs])
    e_other = lax.ppermute(e_in, "c", SWAP)

    sending = send_call(zx, row, arrived)
    xe = lax.all_to_all(sending, ("y", "c"), 0, 0, tiled=True)

    near = near_call((pos, local_blocks, virt_blocks, node_count),
                     (order, node_feats, e_in, e_other, virt_feats), wa)
    ffw = prep_call(wb)
    x_own, rest = near[0], near[1:]
    result = far_call((pos, exp_blocks, node_count), (x_own, xe, *rest, *ffw))
    received = lax.all_to_all(result, ("y", "c"), 0, 0, tiled=True)
    return place_call(pos, received, order).T


def solution(mesh):
    grid = Mesh(mesh.devices.reshape(NZ, NX, NY, NC), ("z", "x", "y", "c"))
    dom, head = ("z", "x"), ("y", "c")
    return jax.shard_map(
        shards,
        mesh=grid,
        in_specs=(P(dom, None), P(dom), P(), P(dom, None), P(dom, None), P(dom), P(),
                  P(None, head), P(None, head), P(None, head), P(None, head), P(None, head),
                  P(head, None)),
        out_specs=P(dom, head),
        check_vma=False,
    )
```

```python
import math

import jax
import jax.numpy as jnp
from jax import lax
from jax.experimental import pallas as pl
from jax.experimental.pallas import tpu as pltpu
from jax.sharding import Mesh, PartitionSpec as P

D = 512
HD = 64
FF = 1024
CL = 128
CD = 8
NE = 6
NL = 3
CAP = 3
NZ, NX, NY, NC = 8, 4, 4, 2
PR = CL // (NY * NC)
EK = NE * CL
LK = (NL + 1) * CL
NEG = -1e30
VMEM_BYTES = 67043328
BF = jnp.bfloat16
F32 = jnp.float32
NT = (((1,), (1,)), ((), ()))
NN = (((1,), (0,)), ((), ()))

GROUPS = ((0, 1, 7, 2, 6), (3, 5, 4))


def split2(v):
    hi = v.astype(BF)
    return hi, (v - hi.astype(F32)).astype(BF)


def mm(a, b, dims):
    return lax.dot_general(a, b, dims, preferred_element_type=F32)


def dot3(ah, al, bh, bl, dims):
    return mm(ah, bh, dims) + (mm(ah, bl, dims) + mm(al, bh, dims))


def vspec():
    return pl.BlockSpec(memory_space=pltpu.VMEM)


def hspec():
    return pl.BlockSpec(memory_space=pltpu.HBM)


def sspec():
    return pl.BlockSpec(memory_space=pltpu.SMEM)


def params(mb):
    return pltpu.CompilerParams(vmem_limit_bytes=mb << 20)


def cost(flops, bytes_accessed, transcendentals=0):
    return pl.CostEstimate(flops=flops, bytes_accessed=bytes_accessed, transcendentals=transcendentals)


def sds(*shape, dtype=F32):
    return jax.ShapeDtypeStruct(shape, dtype)


def columns(row):
    return jnp.broadcast_to(row, (CL, CL)).T


def one_hot(cols):
    lanes = lax.broadcasted_iota(jnp.int32, cols.shape, 1).astype(F32)
    parts = [jnp.where(cols == lanes + float(j * CL), 1.0, 0.0).astype(BF) for j in range(CD)]
    return jnp.concatenate(parts, 1)


def first_kernel(pos, order_hbm, nodes_hbm, piece_out, edge_out, order_ref, nodes, sems):
    base, head, c = pos[0], pos[1], pos[2]
    step = 2 * CL
    parts = CD * CL // step
    fetch = [pltpu.make_async_copy(order_hbm, order_ref, sems.at[0])] + [
        pltpu.make_async_copy(nodes_hbm.at[i * step:(i + 1) * step, :], nodes.at[i * step:(i + 1) * step, :],
                              sems.at[i + 1]) for i in range(parts)]
    for copy in fetch:
        copy.start()
    fetch[0].wait()
    order = (order_ref[...] - base).astype(F32)
    mine = pltpu.roll(order, lax.rem(CL - head * PR, CL), 1)
    col = jnp.concatenate([mine] + [jnp.zeros((CL - CD, CL), F32)], 0).T
    pieces = [jnp.broadcast_to(col[:PR, k:k + 1], (PR, CL)) for k in range(CD)]
    edge = jnp.where(head < NY, CD - NC + c, c)
    edge_row = (order_ref[pl.ds(edge, 1), :] - base).astype(F32)
    pick = one_hot(jnp.concatenate(pieces + [columns(edge_row)], 0))
    rows = jnp.zeros((2 * CL, D), F32)
    for i in range(parts):
        fetch[i + 1].wait()
        hi, lo = split2(nodes[i * step:(i + 1) * step, :])
        some = pick[:, i * step:(i + 1) * step]
        rows = rows + (mm(some, hi, NN) + mm(some, lo, NN))
    piece_out[...] = rows[:CL]
    edge_out[...] = rows[CL:]


def first_call(pos, order, nodes):
    return pl.pallas_call(
        first_kernel,
        out_shape=[sds(CL, D), sds(CL, D)],
        in_specs=[sspec(), hspec(), hspec()],
        out_specs=[vspec()] * 2,
        scratch_shapes=[pltpu.VMEM((CD, CL), jnp.int32), pltpu.VMEM((CD * CL, D), F32),
                        pltpu.SemaphoreType.DMA((5,))],
        compiler_params=params(60),
        cost_estimate=cost(10**9, 3 << 20),
        name="first",
    )(pos, order, nodes)


def index_kernel(pos, exp_ref, t0, t1, t2, t3, row, seen):
    z, x = pos[0], pos[1]
    tables = (t0, t1, t2, t3)

    def clear(i, carry):
        for t in tables:
            t[i] = 0
        return carry

    lax.fori_loop(0, NZ * CAP, clear, 0)

    def unseen(i, carry):
        seen[i] = 0
        return carry

    lax.fori_loop(0, NZ * NX, unseen, 0)

    def place(i, carry):
        for e in range(NE):
            block = exp_ref[i, e]
            owner = lax.shift_right_logical(block, 3)
            inside = lax.bitwise_and(block, CD - 1)
            rank = seen[owner]
            seen[owner] = rank + 1
            oz = lax.shift_right_logical(owner, 2)
            back = lax.bitwise_and(x - lax.bitwise_and(owner, NX - 1), NX - 1)
            for k, t in enumerate(tables):
                @pl.when(back == k)
                def _(t=t):
                    t[oz * CAP + rank] = inside
            off = lax.bitwise_and(oz - z, NZ - 1)
            at = jnp.int32(0)
            start = 0
            for group in GROUPS:
                for p, s in enumerate(group):
                    at = jnp.where(off == s, start + back * (len(group) * CAP) + p * CAP, at)
                start += NX * len(group) * CAP
            row[i * NE + e] = (at + rank) * PR
        return carry

    lax.fori_loop(0, CD, place, 0)


def index_call(pos, exp_blocks):
    t = sds(NZ * CAP, dtype=jnp.int32)
    return pl.pallas_call(
        index_kernel,
        out_shape=[t] * NX + [sds(CD * NE, dtype=jnp.int32)],
        in_specs=[sspec()] * 2,
        out_specs=[sspec()] * (NX + 1),
        scratch_shapes=[pltpu.SMEM((NZ * NX,), jnp.int32)],
        compiler_params=params(2),
        cost_estimate=cost(1000, 4096),
        name="index",
    )(pos, exp_blocks)


def pack_kernel(q, k, v, o, up, down, att, ffw, sems):
    pairs = [(w, att.at[i * HD:(i + 1) * HD, :]) for i, w in enumerate((q, k, v, o))]
    pairs.append((down, ffw.at[:CL, :]))
    pairs += [(up.at[j * CL:(j + 1) * CL, :], ffw.at[CL:, j * CL:(j + 1) * CL]) for j in range(4)]
    copies = [pltpu.make_async_copy(src, dst, sems.at[i]) for i, (src, dst) in enumerate(pairs)]
    for copy in copies:
        copy.start()
    for copy in copies:
        copy.wait()


def pack_call(*w):
    return pl.pallas_call(
        pack_kernel,
        out_shape=[sds(2 * CL, D), sds(2 * CL, D)],
        in_specs=[hspec()] * 6,
        out_specs=[vspec()] * 2,
        scratch_shapes=[pltpu.SemaphoreType.DMA((9,))],
        compiler_params=params(60),
        cost_estimate=cost(0, 2 << 20),
        name="pack",
    )(*w)


def near_kernel(pos, local_ref, virt_ref, count_ref, order_ref, nodes_ref, e_in, e_other, virtual_ref, *rest):
    w = rest[:8]
    x_out, q_out, v_out, o_out, state, kh, kl = rest[8:]
    base, head, c, y = pos[0], pos[1], pos[2], pos[3]
    first = lax.shift_right_logical(base, 7)

    def order_row(r):
        return columns((order_ref[pl.ds(r, 1), :] - base).astype(F32))

    rel = [local_ref[head, j] - first for j in range(NL)]
    rows = [order_row(jnp.clip(r, 0, CD - 1)) for r in rel] + [order_row(head)]
    pick = one_hot(jnp.concatenate(rows, 0))
    nodes = nodes_ref[...]
    hi, lo = split2(nodes)
    got = mm(pick, hi, NN) + mm(pick, lo, NN)
    last = (nodes - hi.astype(F32) - lo.astype(F32)).astype(BF)
    x = got[NL * CL:] + mm(pick[NL * CL:], last, NN)
    x_out[...] = x
    lane = lax.broadcasted_iota(jnp.int32, (1, CL), 1)
    bias = []
    for j in range(NL):
        r = rel[j]
        at = jnp.where(r < 0, r + NC, r - CD)
        edge = jnp.where(at == c, e_in[...], e_other[...])
        keys = jnp.where((r >= 0) & (r < CD), got[j * CL:(j + 1) * CL], edge)
        kh[j * CL:(j + 1) * CL, :], kl[j * CL:(j + 1) * CL, :] = split2(keys)
        bias.append(jnp.where(lane < count_ref[local_ref[head, j]], 0.0, NEG))
    vat = pl.multiple_of(virt_ref[head] * CL, CL)
    kh[NL * CL:, :], kl[NL * CL:, :] = split2(virtual_ref[pl.ds(vat, CL), :])
    bias = jnp.concatenate(bias + [jnp.zeros((1, CL), F32)], 1)

    lanes = lax.broadcasted_iota(jnp.int32, (CL, 2 * HD), 1)
    lowq = lanes < HD
    xh, xl = split2(x)
    for dy in range(NY):
        a, b = w[2 * dy][...], w[2 * dy + 1][...]
        at = lax.rem(y - dy + NY, NY)
        left = jnp.where(c == 0, a, b)
        right = jnp.where(c == 0, b, a)
        wq, wk, wv, wo = (
            split2(jnp.concatenate([left[i * HD:(i + 1) * HD], right[i * HD:(i + 1) * HD]], 0))
            for i in range(4))
        q = dot3(xh, xl, *wq, NT) * (1.0 / math.sqrt(HD))
        both = jnp.concatenate([jnp.where(lowq, q, 0.0), jnp.where(lowq, 0.0, q)], 0)
        q_out[0, at], q_out[1, at] = split2(dot3(*split2(both), *wk, NN))
        v_out[0, at], v_out[1, at] = wv
        rows = pl.ds(pl.multiple_of(at * CL, CL), CL)
        o_out[0, rows, :], o_out[1, rows, :] = wo

    def body(p, carry):
        s = dot3(q_out[0, p], q_out[1, p], kh[...], kl[...], NT) + bias
        m = jnp.max(s, axis=1, keepdims=True)
        e = jnp.exp(s - m)
        l = jnp.sum(e, axis=1, keepdims=True)
        a = dot3(*split2(e), kh[...], kl[...], NN)
        o = dot3(*split2(a), v_out[0, p], v_out[1, p], NT)
        state[p, :CL, :] = jnp.where(lowq, o[:CL], jnp.where(lanes < HD + HD // 2, m[:CL], l[:CL]))
        state[p, CL:, :] = jnp.where(lowq, jnp.where(lanes < HD // 2, m[CL:], l[CL:]), o[CL:])
        return carry

    lax.fori_loop(0, NY, body, 0)


def near_call(scalars, arrays, weights):
    shapes = [
        sds(CL, D), sds(2, NY, 2 * CL, D, dtype=BF), sds(2, NY, 2 * HD, D, dtype=BF),
        sds(2, D, D, dtype=BF), sds(NY, 2 * CL, 2 * HD),
    ]
    return pl.pallas_call(
        near_kernel,
        out_shape=shapes,
        in_specs=[sspec()] * len(scalars) + [vspec()] * len(arrays)
        + [vspec()] * len(weights),
        out_specs=[vspec()] * len(shapes),
        scratch_shapes=[pltpu.VMEM((LK, D), BF), pltpu.VMEM((LK, D), BF)],
        compiler_params=params(60),
        cost_estimate=cost(6 * 10**9, 16 << 20, 1 << 20),
        name="near",
    )(*scalars, *arrays, *weights)


def prep_kernel(*refs):
    w = refs[:8]
    u_out, d_out = refs[8:]
    for i in range(8):
        rows = slice(i * CL, (i + 1) * CL)
        d_out[0, rows, :], d_out[1, rows, :] = split2(w[i][:CL, :])
        hi, lo = split2(w[i][CL:, :])
        for j in range(4):
            cols = slice(j * CL, (j + 1) * CL)
            u_out[0, cols, rows] = hi[:, cols]
            u_out[1, cols, rows] = lo[:, cols]


def prep_call(weights):
    return pl.pallas_call(
        prep_kernel,
        out_shape=[sds(2, D, FF, dtype=BF), sds(2, FF, D, dtype=BF)],
        in_specs=[vspec()] * len(weights),
        out_specs=[vspec()] * 2,
        compiler_params=params(60),
        cost_estimate=cost(10**7, 8 << 20),
        name="prep",
    )(*weights)


def far_kernel(pos, exp_ref, count_ref, xe_ref, q_hbm, s_hbm, v_hbm, x_hbm, o_hbm, u_hbm, d_hbm,
               out_ref, kh, kl, q, st, v, x, wo, u, d, sems):
    copies = [pltpu.make_async_copy(src, dst, sems.at[i]) for i, (src, dst) in enumerate(zip(
        (q_hbm, s_hbm, v_hbm, x_hbm, o_hbm, u_hbm, d_hbm), (q, st, v, x, wo, u, d)))]
    for copy in copies:
        copy.start()
    head = pos[1]
    hi, lo = split2(xe_ref[...])
    kh[...] = hi
    kl[...] = lo
    lowq = lax.broadcasted_iota(jnp.int32, (CL, 2 * HD), 1) < HD
    n = lax.broadcasted_iota(jnp.int32, (1, EK), 1)

    def steps(v, width, count):
        return sum(jnp.where(v >= width * k, 1, 0) for k in range(1, count))

    piece = steps(n, NE * PR, CD)
    r = n - piece * (NE * PR)
    entry = steps(r, PR, NE)
    slot = piece * PR + r - entry * PR
    bias = jnp.zeros((1, EK), F32)
    for e in range(NE):
        bad = (entry == e) & (slot >= count_ref[exp_ref[head, e]])
        bias = jnp.where(bad, NEG, bias)

    def scores(p):
        return dot3(q[0, p], q[1, p], kh[...], kl[...], NT) + bias

    att = []
    copies[0].wait()
    s_next = scores(0)
    copies[1].wait()
    copies[2].wait()
    for p in range(NY):
        s = s_next
        if p + 1 < NY:
            s_next = scores(p + 1)
        m_near = jnp.concatenate([st[p, :CL, HD:HD + 1], st[p, CL:, :1]], 0)
        half = HD // 2
        l_near = jnp.concatenate([st[p, :CL, HD + half:HD + half + 1], st[p, CL:, half:half + 1]], 0)
        m = jnp.maximum(m_near, jnp.max(s, axis=1, keepdims=True))
        e = jnp.exp(s - m)
        scale = jnp.exp(m_near - m)
        total = jnp.sum(e, axis=1, keepdims=True) + l_near * scale
        a = dot3(*split2(e), kh[...], kl[...], NN)
        o = dot3(*split2(a), v[0, p], v[1, p], NT) + st[p] * scale
        o = o / total
        att.append(jnp.where(lowq, o[:CL], o[CL:]))

    ah, al = split2(jnp.concatenate(att, 1))
    for copy in copies[3:]:
        copy.wait()
    r = x[...] + dot3(ah, al, wo[0], wo[1], NT)
    mean = jnp.sum(r, axis=1, keepdims=True) * (1.0 / D)
    square = jnp.sum(r * r, axis=1, keepdims=True) * (1.0 / D)
    normed = (r - mean) * lax.rsqrt(square - mean * mean + 1e-05)
    hid = dot3(*split2(normed), u[0], u[1], NN)
    act = 0.5 * hid * (1.0 + lax.erf(hid * math.sqrt(0.5)))
    y = r + dot3(*split2(act), d[0], d[1], NN)
    out_ref[...] = y.T


def far_call(scalars, arrays):
    return pl.pallas_call(
        far_kernel,
        out_shape=sds(D, CL),
        in_specs=[sspec()] * len(scalars) + [vspec()] + [hspec()] * (len(arrays) - 1),
        out_specs=vspec(),
        scratch_shapes=[pltpu.VMEM((EK, D), BF), pltpu.VMEM((EK, D), BF)]
        + [pltpu.VMEM(a.shape, a.dtype) for a in arrays[1:]] + [pltpu.SemaphoreType.DMA((len(arrays) - 1,))],
        compiler_params=params(60),
        cost_estimate=cost(6 * 10**9, 16 << 20, 1 << 20),
        name="far",
    )(*scalars, *arrays)


def place_kernel(pos, r_ref, order_ref, out_ref):
    full = jnp.concatenate([r_ref[i * HD:(i + 1) * HD, :] for i in range(CD)], 1)
    order = jnp.concatenate([order_ref[i:i + 1, :] for i in range(CD)], 1) - pos[0]
    hi = full.astype(BF)
    rest = full - hi.astype(F32)
    mid = rest.astype(BF)
    low = (rest - mid.astype(F32)).astype(BF)
    parts = jnp.concatenate([hi, mid, low], 0)
    step = 256
    for j in range(CD * CL // step):
        nodes = lax.broadcasted_iota(jnp.int32, (step, CD * CL), 0) + j * step
        pick = jnp.where(nodes == order, 1.0, 0.0).astype(BF)
        t = mm(parts, pick, NT)
        out_ref[:, j * step:(j + 1) * step] = t[:HD] + (t[HD:2 * HD] + t[2 * HD:])


def place_call(pos, received, order):
    return pl.pallas_call(
        place_kernel,
        out_shape=sds(HD, CD * CL),
        in_specs=[sspec(), vspec(), vspec()],
        out_specs=vspec(),
        compiler_params=params(12),
        cost_estimate=cost(4 * 10**8, 1 << 20),
        name="place",
    )(pos, received, order)


def pick_kernel(group, pos, *refs):
    tables, srcs, outs, sem = refs[:NX], refs[NX:-NX - 1], refs[-NX - 1:-1], refs[-1]
    z = pos[0]
    parts, at = [], 0
    for s in group:
        size = 2 if s == NZ // 2 else 1
        parts.append(srcs[at:at + size])
        at += size

    def send(src, at, out, to):
        pltpu.make_async_copy(src.at[pl.ds(pl.multiple_of(at, PR), PR), :], out.at[to:to + PR, :], sem).start()

    for k, out in enumerate(outs):
        for i, s in enumerate(group):
            src = parts[i]
            for j in range(CAP):
                b = tables[k][lax.bitwise_and(z + s, NZ - 1) * CAP + j]
                to = (i * CAP + j) * PR
                if len(src) == 1:
                    send(src[0], b * PR, out, to)
                else:
                    at = lax.bitwise_and(b, CD // 2 - 1) * PR

                    @pl.when(b < CD // 2)
                    def _(at=at, to=to, src=src, out=out):
                        send(src[0], at, out, to)

                    @pl.when(b >= CD // 2)
                    def _(at=at, to=to, src=src, out=out):
                        send(src[1], at, out, to)

    for out in outs:
        pltpu.make_async_copy(out, out, sem).wait()


def pick_call(group, pos, tables, srcs):
    rows = len(group) * CAP * PR
    return pl.pallas_call(
        lambda *refs: pick_kernel(group, *refs),
        out_shape=[sds(rows, D)] * NX,
        in_specs=[sspec()] * (1 + NX) + [vspec()] * len(srcs),
        out_specs=[vspec()] * NX,
        scratch_shapes=[pltpu.SemaphoreType.DMA],
        compiler_params=params(8),
        cost_estimate=cost(0, NX * rows * D * 8),
        name="pick",
    )(pos, *tables, *srcs)


def send_kernel(row, *refs):
    srcs, out, held = refs[:-2], refs[-2], refs[-1]
    at = 0
    for src in srcs:
        held[at:at + src.shape[0], :] = src[...]
        at += src.shape[0]
    for i in range(CD * NE):
        out[i * PR:(i + 1) * PR, :] = held[pl.ds(pl.multiple_of(row[i], PR), PR), :]


def send_call(row, srcs):
    return pl.pallas_call(
        send_kernel,
        out_shape=sds(CD * NE * PR, D),
        in_specs=[sspec()] + [vspec()] * len(srcs),
        out_specs=vspec(),
        scratch_shapes=[pltpu.VMEM((NZ * NX * CAP * PR, D), F32)],
        compiler_params=params(12),
        cost_estimate=cost(0, 6 << 20),
        name="send",
    )(row, *srcs)


def ring(size, step):
    return [(i, (i + step) % size) for i in range(size)]


SWAP = [(0, 1), (1, 0)]


def shards(node_feats, order, node_count, local_blocks, exp_blocks, virt_blocks, virt_feats,
           w_query, w_key, w_value, w_out, w_up, w_down):
    z, x, y, c = (lax.axis_index(a) for a in ("z", "x", "y", "c"))
    head = y * NC + c
    pos = jnp.stack([(z * NX + x) * (CD * CL), head, c, y]).astype(jnp.int32)
    zx = jnp.stack([z, x]).astype(jnp.int32)
    order = order.reshape(CD, CL)

    piece, edge = first_call(pos, order, node_feats)

    half = CL // 2
    tie = lax.optimization_barrier

    def both_z(a, b):
        return lax.ppermute(a, "z", ring(NZ, 1)), lax.ppermute(b, "z", ring(NZ, -1))

    def both_y(a):
        return lax.ppermute(a, "y", ring(NY, 1)), lax.ppermute(a, "y", ring(NY, -1))

    def swap(*arrays):
        return [lax.ppermute(t, "c", SWAP) for t in arrays]

    up, down = both_z(piece, piece)
    *asks, row = index_call(zx, exp_blocks)
    tables = [asks[0]] + [lax.ppermute(asks[k], "x", ring(NX, -k)) for k in range(1, NX)]
    wa, wb = pack_call(w_query.T, w_key.T, w_value.T, w_out.T, w_up, w_down)
    held = {0: (piece,), 7: (up,), 1: (down,)}
    a_up, a_down = both_y(wa)
    up, down, edge, wb, *tables = tie((up, down, edge, wb, *tables))

    e_in = lax.ppermute(edge, ("z", "x", "y", "c"), [
        (i * CD + h, (i + s) * CD + h)
        for s, hs in ((1, (0, 1)), (-1, (6, 7)))
        for i in range(NZ * NX) if 0 <= i + s < NZ * NX for h in hs])
    up, down = both_z(up, down)
    held[6], held[2] = (up,), (down,)
    up, down, a_up, a_down, e_in, *tables = tie((up, down, a_up, a_down, e_in, *tables))

    def exchange(group):
        blocks = pick_call(group, zx, tables, [t for s in group for t in held[s]])
        return [blocks[0]] + [lax.ppermute(blocks[k], "x", ring(NX, k)) for k in (1, 2, 3)]

    near_x = exchange(GROUPS[0])
    up, down = both_z(up, down)
    held[5], held[3] = (up,), (down,)
    first4, second4 = both_z(up[:half], down[half:])
    first4, second4, wb = tie((first4, second4, wb))
    b_up, b_down = both_y(wb)
    first4, second4, *near_x = tie((first4, second4, *near_x))
    held[4] = (first4, second4)
    far_x = exchange(GROUPS[1])

    a_up, a_down, b_up, b_down = tie((a_up, a_down, b_up, b_down))
    a_far = lax.ppermute(a_up, "y", ring(NY, 1))
    b_far = lax.ppermute(b_down, "y", ring(NY, -1))
    e_other, wa_o, a_up_o, a_down_o, wb_o, b_up_o, b_down_o = swap(e_in, wa, a_up, a_down, wb, b_up, b_down)
    e_other, wa_o, a_up_o, a_down_o, wb_o, b_up_o, b_down_o, *far_x = tie(
        (e_other, wa_o, a_up_o, a_down_o, wb_o, b_up_o, b_down_o, *far_x))

    sending = send_call(row, near_x + far_x)
    xe = lax.all_to_all(sending, ("y", "c"), 0, 0, tiled=True)
    a_far_o, b_far_o = swap(a_far, b_far)
    wa = [wa, wa_o, a_up, a_up_o, a_far, a_far_o, a_down, a_down_o]
    wb = [wb, wb_o, b_up, b_up_o, b_far, b_far_o, b_down, b_down_o]

    x_own, q, wv, wo, state = near_call(
        (pos, local_blocks, virt_blocks, node_count), (order, node_feats, e_in, e_other, virt_feats), wa)
    wu, wd = prep_call(wb)
    result = far_call((pos, exp_blocks, node_count), (xe, q, state, wv, x_own, wo, wu, wd))
    received = lax.all_to_all(result, ("y", "c"), 0, 0, tiled=True)
    return place_call(pos, received, order).T


def solution(mesh):
    grid = Mesh(mesh.devices.reshape(NZ, NX, NY, NC), ("z", "x", "y", "c"))
    dom, head = ("z", "x"), ("y", "c")
    return jax.shard_map(
        shards,
        mesh=grid,
        in_specs=(P(dom, None), P(dom), P(), P(dom, None), P(dom, None), P(dom), P(),
                  P(None, head), P(None, head), P(None, head), P(None, head), P(None, head),
                  P(head, None)),
        out_specs=P(dom, head),
        check_vma=False,
    )
```

```python
import math

import jax
import jax.numpy as jnp
from jax import lax
from jax.experimental import pallas as pl
from jax.experimental.pallas import tpu as pltpu
from jax.sharding import Mesh, PartitionSpec as P

D = 512
HD = 64
FF = 1024
CL = 128
CD = 8
NE = 6
NL = 3
CAP = 3
NZ, NX, NY, NC = 8, 4, 4, 2
PR = CL // (NY * NC)
EK = NE * CL
LK = (NL + 1) * CL
NEG = -1e30
VMEM_BYTES = 67043328
BF = jnp.bfloat16
F32 = jnp.float32
NT = (((1,), (1,)), ((), ()))
NN = (((1,), (0,)), ((), ()))

GROUPS = ((0, 1, 7, 2, 6), (3, 5, 4))


def split2(v):
    hi = v.astype(BF)
    return hi, (v - hi.astype(F32)).astype(BF)


def mm(a, b, dims):
    return lax.dot_general(a, b, dims, preferred_element_type=F32)


def dot3(ah, al, bh, bl, dims):
    return mm(ah, bh, dims) + (mm(ah, bl, dims) + mm(al, bh, dims))


def vspec():
    return pl.BlockSpec(memory_space=pltpu.VMEM)


def hspec():
    return pl.BlockSpec(memory_space=pltpu.HBM)


def sspec():
    return pl.BlockSpec(memory_space=pltpu.SMEM)


def params(mb):
    return pltpu.CompilerParams(vmem_limit_bytes=mb << 20)


def cost(flops, bytes_accessed, transcendentals=0):
    return pl.CostEstimate(flops=flops, bytes_accessed=bytes_accessed, transcendentals=transcendentals)


def sds(*shape, dtype=F32):
    return jax.ShapeDtypeStruct(shape, dtype)


def columns(row):
    return jnp.broadcast_to(row, (CL, CL)).T


def one_hot(cols):
    lanes = lax.broadcasted_iota(jnp.int32, cols.shape, 1).astype(F32)
    parts = [jnp.where(cols == lanes + float(j * CL), 1.0, 0.0).astype(BF) for j in range(CD)]
    return jnp.concatenate(parts, 1)


def first_kernel(pos, order_hbm, nodes_hbm, piece_out, edge_out, order_ref, nodes, sems):
    base, head, c = pos[0], pos[1], pos[2]
    step = 2 * CL
    parts = CD * CL // step
    fetch = [pltpu.make_async_copy(order_hbm, order_ref, sems.at[0])] + [
        pltpu.make_async_copy(nodes_hbm.at[i * step:(i + 1) * step, :], nodes.at[i * step:(i + 1) * step, :],
                              sems.at[i + 1]) for i in range(parts)]
    for copy in fetch:
        copy.start()
    fetch[0].wait()
    order = (order_ref[...] - base).astype(F32)
    mine = pltpu.roll(order, lax.rem(CL - head * PR, CL), 1)
    col = jnp.concatenate([mine] + [jnp.zeros((CL - CD, CL), F32)], 0).T
    pieces = [jnp.broadcast_to(col[:PR, k:k + 1], (PR, CL)) for k in range(CD)]
    edge = jnp.where(head < NY, CD - NC + c, c)
    edge_row = (order_ref[pl.ds(edge, 1), :] - base).astype(F32)
    pick = one_hot(jnp.concatenate(pieces + [columns(edge_row)], 0))
    rows = jnp.zeros((2 * CL, D), F32)
    for i in range(parts):
        fetch[i + 1].wait()
        hi, lo = split2(nodes[i * step:(i + 1) * step, :])
        some = pick[:, i * step:(i + 1) * step]
        rows = rows + (mm(some, hi, NN) + mm(some, lo, NN))
    piece_out[...] = rows[:CL]
    edge_out[...] = rows[CL:]


def first_call(pos, order, nodes):
    return pl.pallas_call(
        first_kernel,
        out_shape=[sds(CL, D), sds(CL, D)],
        in_specs=[sspec(), hspec(), hspec()],
        out_specs=[vspec()] * 2,
        scratch_shapes=[pltpu.VMEM((CD, CL), jnp.int32), pltpu.VMEM((CD * CL, D), F32),
                        pltpu.SemaphoreType.DMA((5,))],
        compiler_params=params(60),
        cost_estimate=cost(10**9, 3 << 20),
        name="first",
    )(pos, order, nodes)


def index_kernel(pos, exp_ref, table, row, seen, starts, widths):
    z, x = pos[0], pos[1]
    start = 0
    for group in GROUPS:
        for p, s in enumerate(group):
            starts[s] = start + p * CAP
            widths[s] = len(group) * CAP
        start += NX * len(group) * CAP

    def clear(i, carry):
        table[i] = 0
        seen[lax.bitwise_and(i, NZ * NX - 1)] = 0
        return carry

    lax.fori_loop(0, NX * NZ * CAP, clear, 0)

    def place(i, carry):
        for e in range(NE):
            block = exp_ref[i, e]
            owner = lax.shift_right_logical(block, 3)
            rank = seen[owner]
            seen[owner] = rank + 1
            oz = lax.shift_right_logical(owner, 2)
            back = lax.bitwise_and(x - lax.bitwise_and(owner, NX - 1), NX - 1)
            table[back * (NZ * CAP) + oz * CAP + rank] = lax.bitwise_and(block, CD - 1)
            off = lax.bitwise_and(oz - z, NZ - 1)
            row[i * NE + e] = (starts[off] + back * widths[off] + rank) * PR
        return carry

    lax.fori_loop(0, CD, place, 0)


def index_call(pos, exp_blocks):
    return pl.pallas_call(
        index_kernel,
        out_shape=[sds(NX * NZ * CAP, dtype=jnp.int32), sds(CD * NE, dtype=jnp.int32)],
        in_specs=[sspec()] * 2,
        out_specs=[sspec()] * 2,
        scratch_shapes=[pltpu.SMEM((NZ * NX,), jnp.int32), pltpu.SMEM((NZ,), jnp.int32), pltpu.SMEM((NZ,), jnp.int32)],
        compiler_params=params(2),
        cost_estimate=cost(1000, 4096),
        name="index",
    )(pos, exp_blocks)


def pack_kernel(q, k, v, o, up, down, att, ffw, sems):
    pairs = [(w, att.at[i * HD:(i + 1) * HD, :]) for i, w in enumerate((q, k, v, o))]
    pairs.append((down, ffw.at[:CL, :]))
    pairs += [(up.at[j * CL:(j + 1) * CL, :], ffw.at[CL:, j * CL:(j + 1) * CL]) for j in range(4)]
    copies = [pltpu.make_async_copy(src, dst, sems.at[i]) for i, (src, dst) in enumerate(pairs)]
    for copy in copies:
        copy.start()
    for copy in copies:
        copy.wait()


def pack_call(*w):
    return pl.pallas_call(
        pack_kernel,
        out_shape=[sds(2 * CL, D), sds(2 * CL, D)],
        in_specs=[hspec()] * 6,
        out_specs=[vspec()] * 2,
        scratch_shapes=[pltpu.SemaphoreType.DMA((9,))],
        compiler_params=params(60),
        cost_estimate=cost(0, 2 << 20),
        name="pack",
    )(*w)


def near_kernel(pos, local_ref, virt_ref, count_ref, order_ref, nodes_ref, e_in, e_other, virtual_ref, *rest):
    w = rest[:8]
    x_out, q_out, v_out, o_out, state, kh, kl = rest[8:]
    base, head, c, y = pos[0], pos[1], pos[2], pos[3]
    first = lax.shift_right_logical(base, 7)

    def order_row(r):
        return columns((order_ref[pl.ds(r, 1), :] - base).astype(F32))

    rel = [local_ref[head, j] - first for j in range(NL)]
    rows = [order_row(jnp.clip(r, 0, CD - 1)) for r in rel] + [order_row(head)]
    pick = one_hot(jnp.concatenate(rows, 0))
    nodes = nodes_ref[...]
    hi, lo = split2(nodes)
    got = mm(pick, hi, NN) + mm(pick, lo, NN)
    last = (nodes - hi.astype(F32) - lo.astype(F32)).astype(BF)
    x = got[NL * CL:] + mm(pick[NL * CL:], last, NN)
    x_out[...] = x
    lane = lax.broadcasted_iota(jnp.int32, (1, CL), 1)
    bias = []
    for j in range(NL):
        r = rel[j]
        at = jnp.where(r < 0, r + NC, r - CD)
        edge = jnp.where(at == c, e_in[...], e_other[...])
        keys = jnp.where((r >= 0) & (r < CD), got[j * CL:(j + 1) * CL], edge)
        kh[j * CL:(j + 1) * CL, :], kl[j * CL:(j + 1) * CL, :] = split2(keys)
        bias.append(jnp.where(lane < count_ref[local_ref[head, j]], 0.0, NEG))
    vat = pl.multiple_of(virt_ref[head] * CL, CL)
    kh[NL * CL:, :], kl[NL * CL:, :] = split2(virtual_ref[pl.ds(vat, CL), :])
    bias = jnp.concatenate(bias + [jnp.zeros((1, CL), F32)], 1)

    lanes = lax.broadcasted_iota(jnp.int32, (CL, 2 * HD), 1)
    lowq = lanes < HD
    xh, xl = split2(x)
    for dy in range(NY):
        a, b = w[2 * dy][...], w[2 * dy + 1][...]
        at = lax.rem(y - dy + NY, NY)
        left = jnp.where(c == 0, a, b)
        right = jnp.where(c == 0, b, a)
        wq, wk, wv, wo = (
            split2(jnp.concatenate([left[i * HD:(i + 1) * HD], right[i * HD:(i + 1) * HD]], 0))
            for i in range(4))
        q = dot3(xh, xl, *wq, NT) * (1.0 / math.sqrt(HD))
        both = jnp.concatenate([jnp.where(lowq, q, 0.0), jnp.where(lowq, 0.0, q)], 0)
        q_out[0, at], q_out[1, at] = split2(dot3(*split2(both), *wk, NN))
        v_out[0, at], v_out[1, at] = wv
        rows = pl.ds(pl.multiple_of(at * CL, CL), CL)
        o_out[0, rows, :], o_out[1, rows, :] = wo

    def body(p, carry):
        s = dot3(q_out[0, p], q_out[1, p], kh[...], kl[...], NT) + bias
        m = jnp.max(s, axis=1, keepdims=True)
        e = jnp.exp(s - m)
        l = jnp.sum(e, axis=1, keepdims=True)
        a = dot3(*split2(e), kh[...], kl[...], NN)
        o = dot3(*split2(a), v_out[0, p], v_out[1, p], NT)
        state[p, :CL, :] = jnp.where(lowq, o[:CL], jnp.where(lanes < HD + HD // 2, m[:CL], l[:CL]))
        state[p, CL:, :] = jnp.where(lowq, jnp.where(lanes < HD // 2, m[CL:], l[CL:]), o[CL:])
        return carry

    lax.fori_loop(0, NY, body, 0)


def near_call(scalars, arrays, weights):
    shapes = [
        sds(CL, D), sds(2, NY, 2 * CL, D, dtype=BF), sds(2, NY, 2 * HD, D, dtype=BF),
        sds(2, D, D, dtype=BF), sds(NY, 2 * CL, 2 * HD),
    ]
    return pl.pallas_call(
        near_kernel,
        out_shape=shapes,
        in_specs=[sspec()] * len(scalars) + [vspec()] * len(arrays)
        + [vspec()] * len(weights),
        out_specs=[vspec()] * len(shapes),
        scratch_shapes=[pltpu.VMEM((LK, D), BF), pltpu.VMEM((LK, D), BF)],
        compiler_params=params(60),
        cost_estimate=cost(6 * 10**9, 16 << 20, 1 << 20),
        name="near",
    )(*scalars, *arrays, *weights)


def prep_kernel(*refs):
    w = refs[:8]
    u_out, d_out = refs[8:]
    for i in range(8):
        rows = slice(i * CL, (i + 1) * CL)
        d_out[0, rows, :], d_out[1, rows, :] = split2(w[i][:CL, :])
        hi, lo = split2(w[i][CL:, :])
        for j in range(4):
            cols = slice(j * CL, (j + 1) * CL)
            u_out[0, cols, rows] = hi[:, cols]
            u_out[1, cols, rows] = lo[:, cols]


def prep_call(weights):
    return pl.pallas_call(
        prep_kernel,
        out_shape=[sds(2, D, FF, dtype=BF), sds(2, FF, D, dtype=BF)],
        in_specs=[vspec()] * len(weights),
        out_specs=[vspec()] * 2,
        compiler_params=params(60),
        cost_estimate=cost(10**7, 8 << 20),
        name="prep",
    )(*weights)


def far_kernel(pos, exp_ref, count_ref, xe_ref, q_hbm, s_hbm, v_hbm, x_hbm, o_hbm, u_hbm, d_hbm,
               out_ref, kh, kl, att, q, st, v, x, wo, u, d, sems):
    copies = [pltpu.make_async_copy(src, dst, sems.at[i]) for i, (src, dst) in enumerate(zip(
        (q_hbm, s_hbm, v_hbm, x_hbm, o_hbm, u_hbm, d_hbm), (q, st, v, x, wo, u, d)))]
    for copy in copies[:3]:
        copy.start()
    head = pos[1]
    hi, lo = split2(xe_ref[...])
    kh[...] = hi
    kl[...] = lo
    lowq = lax.broadcasted_iota(jnp.int32, (CL, 2 * HD), 1) < HD
    n = lax.broadcasted_iota(jnp.int32, (1, EK), 1)

    def steps(v, width, count):
        return sum(jnp.where(v >= width * k, 1, 0) for k in range(1, count))

    piece = steps(n, NE * PR, CD)
    r = n - piece * (NE * PR)
    entry = steps(r, PR, NE)
    slot = piece * PR + r - entry * PR
    bias = jnp.zeros((1, EK), F32)
    for e in range(NE):
        bad = (entry == e) & (slot >= count_ref[exp_ref[head, e]])
        bias = jnp.where(bad, NEG, bias)

    def scores(p):
        return dot3(q[0, p], q[1, p], kh[...], kl[...], NT) + bias

    def attend(p, s):
        m_near = jnp.concatenate([st[p, :CL, HD:HD + 1], st[p, CL:, :1]], 0)
        half = HD // 2
        l_near = jnp.concatenate([st[p, :CL, HD + half:HD + half + 1], st[p, CL:, half:half + 1]], 0)
        m = jnp.maximum(m_near, jnp.max(s, axis=1, keepdims=True))
        e = jnp.exp(s - m)
        scale = jnp.exp(m_near - m)
        total = jnp.sum(e, axis=1, keepdims=True) + l_near * scale
        a = dot3(*split2(e), kh[...], kl[...], NN)
        o = (dot3(*split2(a), v[0, p], v[1, p], NT) + st[p] * scale) / total
        att[p] = jnp.where(lowq, o[:CL], o[CL:])

    for copy in copies[:3]:
        copy.wait()
    for copy in copies[3:]:
        copy.start()

    def body(i, carry):
        one, two = scores(2 * i), scores(2 * i + 1)
        attend(2 * i, one)
        attend(2 * i + 1, two)
        return carry

    lax.fori_loop(0, NY // 2, body, 0)
    ah, al = split2(jnp.concatenate([att[p] for p in range(NY)], 1))
    for copy in copies[3:]:
        copy.wait()
    r = x[...] + dot3(ah, al, wo[0], wo[1], NT)
    mean = jnp.sum(r, axis=1, keepdims=True) * (1.0 / D)
    square = jnp.sum(r * r, axis=1, keepdims=True) * (1.0 / D)
    normed = (r - mean) * lax.rsqrt(square - mean * mean + 1e-05)
    hid = dot3(*split2(normed), u[0], u[1], NN)
    act = 0.5 * hid * (1.0 + lax.erf(hid * math.sqrt(0.5)))
    y = r + dot3(*split2(act), d[0], d[1], NN)
    out_ref[...] = y.T


def far_call(scalars, arrays):
    return pl.pallas_call(
        far_kernel,
        out_shape=sds(D, CL),
        in_specs=[sspec()] * len(scalars) + [vspec()] + [hspec()] * (len(arrays) - 1),
        out_specs=vspec(),
        scratch_shapes=[pltpu.VMEM((EK, D), BF), pltpu.VMEM((EK, D), BF), pltpu.VMEM((NY, CL, 2 * HD), F32)]
        + [pltpu.VMEM(a.shape, a.dtype) for a in arrays[1:]] + [pltpu.SemaphoreType.DMA((len(arrays) - 1,))],
        compiler_params=params(60),
        cost_estimate=cost(6 * 10**9, 16 << 20, 1 << 20),
        name="far",
    )(*scalars, *arrays)


def place_kernel(pos, r_ref, order_ref, out_ref):
    full = jnp.concatenate([r_ref[i * HD:(i + 1) * HD, :] for i in range(CD)], 1)
    order = jnp.concatenate([order_ref[i:i + 1, :] for i in range(CD)], 1) - pos[0]
    hi = full.astype(BF)
    rest = full - hi.astype(F32)
    mid = rest.astype(BF)
    low = (rest - mid.astype(F32)).astype(BF)
    parts = jnp.concatenate([hi, mid, low], 0)
    step = 256
    for j in range(CD * CL // step):
        nodes = lax.broadcasted_iota(jnp.int32, (step, CD * CL), 0) + j * step
        pick = jnp.where(nodes == order, 1.0, 0.0).astype(BF)
        t = mm(parts, pick, NT)
        out_ref[:, j * step:(j + 1) * step] = t[:HD] + (t[HD:2 * HD] + t[2 * HD:])


def place_call(pos, received, order):
    return pl.pallas_call(
        place_kernel,
        out_shape=sds(HD, CD * CL),
        in_specs=[sspec(), vspec(), vspec()],
        out_specs=vspec(),
        compiler_params=params(12),
        cost_estimate=cost(4 * 10**8, 1 << 20),
        name="place",
    )(pos, received, order)


def pick_kernel(group, pos, *refs):
    tables, srcs, outs, sem = refs[:NX], refs[NX:-NX - 1], refs[-NX - 1:-1], refs[-1]
    z = pos[0]
    parts, at = [], 0
    for s in group:
        size = 2 if s == NZ // 2 else 1
        parts.append(srcs[at:at + size])
        at += size

    def send(src, at, out, to):
        pltpu.make_async_copy(src.at[pl.ds(pl.multiple_of(at, PR), PR), :], out.at[to:to + PR, :], sem).start()

    for k, out in enumerate(outs):
        for i, s in enumerate(group):
            src = parts[i]
            for j in range(CAP):
                b = tables[k][(k * NZ + lax.bitwise_and(z + s, NZ - 1)) * CAP + j]
                to = (i * CAP + j) * PR
                if len(src) == 1:
                    send(src[0], b * PR, out, to)
                else:
                    at = lax.bitwise_and(b, CD // 2 - 1) * PR

                    @pl.when(b < CD // 2)
                    def _(at=at, to=to, src=src, out=out):
                        send(src[0], at, out, to)

                    @pl.when(b >= CD // 2)
                    def _(at=at, to=to, src=src, out=out):
                        send(src[1], at, out, to)

    for out in outs:
        pltpu.make_async_copy(out, out, sem).wait()


def pick_call(group, pos, tables, srcs):
    rows = len(group) * CAP * PR
    return pl.pallas_call(
        lambda *refs: pick_kernel(group, *refs),
        out_shape=[sds(rows, D)] * NX,
        in_specs=[sspec()] * (1 + NX) + [vspec()] * len(srcs),
        out_specs=[vspec()] * NX,
        scratch_shapes=[pltpu.SemaphoreType.DMA],
        compiler_params=params(8),
        cost_estimate=cost(0, NX * rows * D * 8),
        name="pick",
    )(pos, *tables, *srcs)


def send_kernel(row, *refs):
    srcs, out, held = refs[:-2], refs[-2], refs[-1]
    at = 0
    for src in srcs:
        held[at:at + src.shape[0], :] = src[...]
        at += src.shape[0]
    for i in range(CD * NE):
        out[i * PR:(i + 1) * PR, :] = held[pl.ds(pl.multiple_of(row[i], PR), PR), :]


def send_call(row, srcs):
    return pl.pallas_call(
        send_kernel,
        out_shape=sds(CD * NE * PR, D),
        in_specs=[sspec()] + [vspec()] * len(srcs),
        out_specs=vspec(),
        scratch_shapes=[pltpu.VMEM((NZ * NX * CAP * PR, D), F32)],
        compiler_params=params(12),
        cost_estimate=cost(0, 6 << 20),
        name="send",
    )(row, *srcs)


def ring(size, step):
    return [(i, (i + step) % size) for i in range(size)]


SWAP = [(0, 1), (1, 0)]


def shards(node_feats, order, node_count, local_blocks, exp_blocks, virt_blocks, virt_feats,
           w_query, w_key, w_value, w_out, w_up, w_down):
    z, x, y, c = (lax.axis_index(a) for a in ("z", "x", "y", "c"))
    head = y * NC + c
    pos = jnp.stack([(z * NX + x) * (CD * CL), head, c, y]).astype(jnp.int32)
    zx = jnp.stack([z, x]).astype(jnp.int32)
    order = order.reshape(CD, CL)

    piece, edge = first_call(pos, order, node_feats)

    half = CL // 2
    tie = lax.optimization_barrier

    def both_z(a, b):
        return lax.ppermute(a, "z", ring(NZ, 1)), lax.ppermute(b, "z", ring(NZ, -1))

    def both_y(a):
        return lax.ppermute(a, "y", ring(NY, 1)), lax.ppermute(a, "y", ring(NY, -1))

    def swap(*arrays):
        return [lax.ppermute(t, "c", SWAP) for t in arrays]

    up, down = both_z(piece, piece)
    table, row = index_call(zx, exp_blocks)
    tables = [table] + [lax.ppermute(table, "x", ring(NX, -k)) for k in range(1, NX)]
    wa, wb = pack_call(w_query.T, w_key.T, w_value.T, w_out.T, w_up, w_down)
    held = {0: (piece,), 7: (up,), 1: (down,)}
    wa, wb, *tables = tie((wa, wb, *tables))
    a_up, a_down = both_y(wa)
    up, down, edge, *tables = tie((up, down, edge, *tables))

    e_in = lax.ppermute(edge, ("z", "x", "y", "c"), [
        (i * CD + h, (i + s) * CD + h)
        for s, hs in ((1, (0, 1)), (-1, (6, 7)))
        for i in range(NZ * NX) if 0 <= i + s < NZ * NX for h in hs])
    up, down = both_z(up, down)
    held[6], held[2] = (up,), (down,)
    up, down, a_up, a_down, wa, wb, e_in, *tables = tie((up, down, a_up, a_down, wa, wb, e_in, *tables))

    def exchange(group):
        blocks = pick_call(group, zx, tables, [t for s in group for t in held[s]])
        return [blocks[0]] + [lax.ppermute(blocks[k], "x", ring(NX, k)) for k in (1, 2, 3)]

    near_x = exchange(GROUPS[0])
    up, down = both_z(up, down)
    held[5], held[3] = (up,), (down,)
    first4, second4 = both_z(up[:half], down[half:])
    first4, second4, e_in, wa, wb, a_up, a_down = tie((first4, second4, e_in, wa, wb, a_up, a_down))
    held[4] = (first4, second4)
    b_up, b_down = both_y(wb)
    e_other, wa_o, wb_o, a_up_o, a_down_o = swap(e_in, wa, wb, a_up, a_down)
    a_up, first4, second4, *near_x = tie((a_up, first4, second4, *near_x))
    held[4] = (first4, second4)
    far_x = exchange(GROUPS[1])

    a_far = lax.ppermute(a_up, "y", ring(NY, 1))
    b_far = lax.ppermute(b_down, "y", ring(NY, -1))
    e_other, wa_o, wb_o, a_up_o, a_down_o, *far_x = tie((e_other, wa_o, wb_o, a_up_o, a_down_o, *far_x))

    sending = send_call(row, near_x + far_x)
    xe = lax.all_to_all(sending, ("y", "c"), 0, 0, tiled=True)
    _, a_far_s, b_far_s, b_up_s, b_down_s = tie((row, a_far, b_far, b_up, b_down))
    a_far_o, b_up_o, b_down_o, b_far_o = swap(a_far_s, b_up_s, b_down_s, b_far_s)
    wa = [wa, wa_o, a_up, a_up_o, a_far, a_far_o, a_down, a_down_o]
    wb = [wb, wb_o, b_up, b_up_o, b_far, b_far_o, b_down, b_down_o]

    x_own, q, wv, wo, state = near_call(
        (pos, local_blocks, virt_blocks, node_count), (order, node_feats, e_in, e_other, virt_feats), wa)
    wu, wd = prep_call(wb)
    result = far_call((pos, exp_blocks, node_count), (xe, q, state, wv, x_own, wo, wu, wd))
    received = lax.all_to_all(result, ("y", "c"), 0, 0, tiled=True)
    return place_call(pos, received, order).T


def solution(mesh):
    grid = Mesh(mesh.devices.reshape(NZ, NX, NY, NC), ("z", "x", "y", "c"))
    dom, head = ("z", "x"), ("y", "c")
    return jax.shard_map(
        shards,
        mesh=grid,
        in_specs=(P(dom, None), P(dom), P(), P(dom, None), P(dom, None), P(dom), P(),
                  P(None, head), P(None, head), P(None, head), P(None, head), P(None, head),
                  P(head, None)),
        out_specs=P(dom, head),
        check_vma=False,
    )
```

```python
import math

import jax
import jax.numpy as jnp
from jax import lax
from jax.experimental import pallas as pl
from jax.experimental.pallas import tpu as pltpu
from jax.sharding import Mesh, PartitionSpec as P

D = 512
HD = 64
FF = 1024
CL = 128
CD = 8
NE = 6
NL = 3
CAP = 3
NZ, NX, NY, NC = 8, 4, 4, 2
PR = CL // (NY * NC)
EK = NE * CL
LK = (NL + 1) * CL
NEG = -1e30
VMEM_BYTES = 67043328
BF = jnp.bfloat16
F32 = jnp.float32
NT = (((1,), (1,)), ((), ()))
NN = (((1,), (0,)), ((), ()))

GROUPS = ((0, 1, 7, 2, 6), (3, 5, 4))


def split2(v):
    hi = v.astype(BF)
    return hi, (v - hi.astype(F32)).astype(BF)


def mm(a, b, dims):
    return lax.dot_general(a, b, dims, preferred_element_type=F32)


def dot3(ah, al, bh, bl, dims):
    return mm(ah, bh, dims) + (mm(ah, bl, dims) + mm(al, bh, dims))


def vspec():
    return pl.BlockSpec(memory_space=pltpu.VMEM)


def hspec():
    return pl.BlockSpec(memory_space=pltpu.HBM)


def sspec():
    return pl.BlockSpec(memory_space=pltpu.SMEM)


def params(mb):
    return pltpu.CompilerParams(vmem_limit_bytes=mb << 20)


def cost(flops, bytes_accessed, transcendentals=0):
    return pl.CostEstimate(flops=flops, bytes_accessed=bytes_accessed, transcendentals=transcendentals)


def sds(*shape, dtype=F32):
    return jax.ShapeDtypeStruct(shape, dtype)


def columns(row):
    return jnp.broadcast_to(row, (CL, CL)).T


def one_hot(cols):
    lanes = lax.broadcasted_iota(jnp.int32, cols.shape, 1).astype(F32)
    parts = [jnp.where(cols == lanes + float(j * CL), 1.0, 0.0).astype(BF) for j in range(CD)]
    return jnp.concatenate(parts, 1)


def first_kernel(pos, order_hbm, nodes_hbm, piece_out, edge_out, order_ref, nodes, sems):
    base, head, c = pos[0], pos[1], pos[2]
    step = 2 * CL
    parts = CD * CL // step
    fetch = [pltpu.make_async_copy(order_hbm, order_ref, sems.at[0])] + [
        pltpu.make_async_copy(nodes_hbm.at[i * step:(i + 1) * step, :], nodes.at[i * step:(i + 1) * step, :],
                              sems.at[i + 1]) for i in range(parts)]
    for copy in fetch:
        copy.start()
    fetch[0].wait()
    order = (order_ref[...] - base).astype(F32)
    mine = pltpu.roll(order, lax.rem(CL - head * PR, CL), 1)
    col = jnp.concatenate([mine] + [jnp.zeros((CL - CD, CL), F32)], 0).T
    pieces = [jnp.broadcast_to(col[:PR, k:k + 1], (PR, CL)) for k in range(CD)]
    edge = jnp.where(head < NY, CD - NC + c, c)
    edge_row = (order_ref[pl.ds(edge, 1), :] - base).astype(F32)
    pick = one_hot(jnp.concatenate(pieces + [columns(edge_row)], 0))
    rows = jnp.zeros((2 * CL, D), F32)
    for i in range(parts):
        fetch[i + 1].wait()
        hi, lo = split2(nodes[i * step:(i + 1) * step, :])
        some = pick[:, i * step:(i + 1) * step]
        rows = rows + (mm(some, hi, NN) + mm(some, lo, NN))
    piece_out[...] = rows[:CL]
    edge_out[...] = rows[CL:]


def first_call(pos, order, nodes):
    return pl.pallas_call(
        first_kernel,
        out_shape=[sds(CL, D), sds(CL, D)],
        in_specs=[sspec(), hspec(), hspec()],
        out_specs=[vspec()] * 2,
        scratch_shapes=[pltpu.VMEM((CD, CL), jnp.int32), pltpu.VMEM((CD * CL, D), F32),
                        pltpu.SemaphoreType.DMA((5,))],
        compiler_params=params(60),
        cost_estimate=cost(10**9, 3 << 20),
        name="first",
    )(pos, order, nodes)


def index_kernel(pos, exp_ref, table, row, seen, starts, widths):
    z, x = pos[0], pos[1]
    start = 0
    for group in GROUPS:
        for p, s in enumerate(group):
            starts[s] = start + p * CAP
            widths[s] = len(group) * CAP
        start += NX * len(group) * CAP

    def clear(i, carry):
        table[i] = 0
        seen[lax.bitwise_and(i, NZ * NX - 1)] = 0
        return carry

    lax.fori_loop(0, NX * NZ * CAP, clear, 0)

    def place(i, carry):
        for e in range(NE):
            block = exp_ref[i, e]
            owner = lax.shift_right_logical(block, 3)
            rank = seen[owner]
            seen[owner] = rank + 1
            oz = lax.shift_right_logical(owner, 2)
            back = lax.bitwise_and(x - lax.bitwise_and(owner, NX - 1), NX - 1)
            table[back * (NZ * CAP) + oz * CAP + rank] = lax.bitwise_and(block, CD - 1)
            off = lax.bitwise_and(oz - z, NZ - 1)
            row[i * NE + e] = (starts[off] + back * widths[off] + rank) * PR
        return carry

    lax.fori_loop(0, CD, place, 0)


def index_call(pos, exp_blocks):
    return pl.pallas_call(
        index_kernel,
        out_shape=[sds(NX * NZ * CAP, dtype=jnp.int32), sds(CD * NE, dtype=jnp.int32)],
        in_specs=[sspec()] * 2,
        out_specs=[sspec()] * 2,
        scratch_shapes=[pltpu.SMEM((NZ * NX,), jnp.int32), pltpu.SMEM((NZ,), jnp.int32), pltpu.SMEM((NZ,), jnp.int32)],
        compiler_params=params(2),
        cost_estimate=cost(1000, 4096),
        name="index",
    )(pos, exp_blocks)


def pack_kernel(q, k, v, o, up, down, att, ffw, sems):
    pairs = [(w, att.at[i * HD:(i + 1) * HD, :]) for i, w in enumerate((q, k, v, o))]
    pairs.append((down, ffw.at[:CL, :]))
    pairs += [(up.at[j * CL:(j + 1) * CL, :], ffw.at[CL:, j * CL:(j + 1) * CL]) for j in range(4)]
    copies = [pltpu.make_async_copy(src, dst, sems.at[i]) for i, (src, dst) in enumerate(pairs)]
    for copy in copies:
        copy.start()
    for copy in copies:
        copy.wait()


def pack_call(*w):
    return pl.pallas_call(
        pack_kernel,
        out_shape=[sds(2 * CL, D), sds(2 * CL, D)],
        in_specs=[hspec()] * 6,
        out_specs=[vspec()] * 2,
        scratch_shapes=[pltpu.SemaphoreType.DMA((9,))],
        compiler_params=params(60),
        cost_estimate=cost(0, 2 << 20),
        name="pack",
    )(*w)


def near_kernel(pos, local_ref, virt_ref, count_ref, order_ref, nodes_ref, e_in, e_other, virtual_ref, w_hbm,
                x_out, q_out, v_out, o_out, state, kh, kl, w, sem):
    fetch = pltpu.make_async_copy(w_hbm, w, sem)
    fetch.start()
    base, head, c = pos[0], pos[1], pos[2]
    first = lax.shift_right_logical(base, 7)

    def order_row(r):
        return columns((order_ref[pl.ds(r, 1), :] - base).astype(F32))

    rel = [local_ref[head, j] - first for j in range(NL)]
    rows = [order_row(jnp.clip(r, 0, CD - 1)) for r in rel] + [order_row(head)]
    pick = one_hot(jnp.concatenate(rows, 0))
    nodes = nodes_ref[...]
    hi, lo = split2(nodes)
    got = mm(pick, hi, NN) + mm(pick, lo, NN)
    last = (nodes - hi.astype(F32) - lo.astype(F32)).astype(BF)
    x = got[NL * CL:] + mm(pick[NL * CL:], last, NN)
    x_out[...] = x
    lane = lax.broadcasted_iota(jnp.int32, (1, CL), 1)
    bias = []
    for j in range(NL):
        r = rel[j]
        at = jnp.where(r < 0, r + NC, r - CD)
        edge = jnp.where(at == c, e_in[...], e_other[...])
        keys = jnp.where((r >= 0) & (r < CD), got[j * CL:(j + 1) * CL], edge)
        kh[j * CL:(j + 1) * CL, :], kl[j * CL:(j + 1) * CL, :] = split2(keys)
        bias.append(jnp.where(lane < count_ref[local_ref[head, j]], 0.0, NEG))
    vat = pl.multiple_of(virt_ref[head] * CL, CL)
    kh[NL * CL:, :], kl[NL * CL:, :] = split2(virtual_ref[pl.ds(vat, CL), :])
    bias = jnp.concatenate(bias + [jnp.zeros((1, CL), F32)], 1)

    lanes = lax.broadcasted_iota(jnp.int32, (CL, 2 * HD), 1)
    lowq = lanes < HD
    xh, xl = split2(x)
    fetch.wait()
    for at in range(NY):
        left, right = w[2 * at], w[2 * at + 1]
        wq, wk, wv, wo = (
            split2(jnp.concatenate([left[i * HD:(i + 1) * HD], right[i * HD:(i + 1) * HD]], 0))
            for i in range(4))
        q = dot3(xh, xl, *wq, NT) * (1.0 / math.sqrt(HD))
        both = jnp.concatenate([jnp.where(lowq, q, 0.0), jnp.where(lowq, 0.0, q)], 0)
        q_out[0, at], q_out[1, at] = split2(dot3(*split2(both), *wk, NN))
        v_out[0, at], v_out[1, at] = wv
        rows = slice(at * CL, (at + 1) * CL)
        o_out[0, rows, :], o_out[1, rows, :] = wo

    def body(p, carry):
        s = dot3(q_out[0, p], q_out[1, p], kh[...], kl[...], NT) + bias
        m = jnp.max(s, axis=1, keepdims=True)
        e = jnp.exp(s - m)
        l = jnp.sum(e, axis=1, keepdims=True)
        a = dot3(*split2(e), kh[...], kl[...], NN)
        o = dot3(*split2(a), v_out[0, p], v_out[1, p], NT)
        state[p, :CL, :] = jnp.where(lowq, o[:CL], jnp.where(lanes < HD + HD // 2, m[:CL], l[:CL]))
        state[p, CL:, :] = jnp.where(lowq, jnp.where(lanes < HD // 2, m[CL:], l[CL:]), o[CL:])
        return carry

    lax.fori_loop(0, NY, body, 0)


def near_call(scalars, arrays):
    shapes = [
        sds(CL, D), sds(2, NY, 2 * CL, D, dtype=BF), sds(2, NY, 2 * HD, D, dtype=BF),
        sds(2, D, D, dtype=BF), sds(NY, 2 * CL, 2 * HD),
    ]
    return pl.pallas_call(
        near_kernel,
        out_shape=shapes,
        in_specs=[sspec()] * len(scalars) + [vspec()] * (len(arrays) - 1) + [hspec()],
        out_specs=[vspec()] * len(shapes),
        scratch_shapes=[pltpu.VMEM((LK, D), BF), pltpu.VMEM((LK, D), BF), pltpu.VMEM(arrays[-1].shape, F32),
                        pltpu.SemaphoreType.DMA],
        compiler_params=params(60),
        cost_estimate=cost(6 * 10**9, 16 << 20, 1 << 20),
        name="near",
    )(*scalars, *arrays)


def prep_kernel(w, u_out, d_out):
    for i in range(8):
        rows = slice(i * CL, (i + 1) * CL)
        d_out[0, rows, :], d_out[1, rows, :] = split2(w[i, :CL, :])
        hi, lo = split2(w[i, CL:, :])
        for j in range(4):
            cols = slice(j * CL, (j + 1) * CL)
            u_out[0, cols, rows] = hi[:, cols]
            u_out[1, cols, rows] = lo[:, cols]


def prep_call(weights):
    return pl.pallas_call(
        prep_kernel,
        out_shape=[sds(2, D, FF, dtype=BF), sds(2, FF, D, dtype=BF)],
        in_specs=[vspec()],
        out_specs=[vspec()] * 2,
        compiler_params=params(60),
        cost_estimate=cost(10**7, 8 << 20),
        name="prep",
    )(weights)


def far_kernel(pos, exp_ref, count_ref, xe_ref, q_hbm, s_hbm, v_hbm, x_hbm, o_hbm, u_hbm, d_hbm,
               out_ref, kh, kl, att, q, st, v, x, wo, u, d, sems):
    copies = [pltpu.make_async_copy(src, dst, sems.at[i]) for i, (src, dst) in enumerate(zip(
        (q_hbm, s_hbm, v_hbm, x_hbm, o_hbm, u_hbm, d_hbm), (q, st, v, x, wo, u, d)))]
    for copy in copies[:3]:
        copy.start()
    head = pos[1]
    hi, lo = split2(xe_ref[...])
    kh[...] = hi
    kl[...] = lo
    lowq = lax.broadcasted_iota(jnp.int32, (CL, 2 * HD), 1) < HD
    n = lax.broadcasted_iota(jnp.int32, (1, EK), 1)

    def steps(v, width, count):
        return sum(jnp.where(v >= width * k, 1, 0) for k in range(1, count))

    piece = steps(n, NE * PR, CD)
    r = n - piece * (NE * PR)
    entry = steps(r, PR, NE)
    slot = piece * PR + r - entry * PR
    bias = jnp.zeros((1, EK), F32)
    for e in range(NE):
        bad = (entry == e) & (slot >= count_ref[exp_ref[head, e]])
        bias = jnp.where(bad, NEG, bias)

    def scores(p):
        return dot3(q[0, p], q[1, p], kh[...], kl[...], NT) + bias

    def attend(p, s):
        m_near = jnp.concatenate([st[p, :CL, HD:HD + 1], st[p, CL:, :1]], 0)
        half = HD // 2
        l_near = jnp.concatenate([st[p, :CL, HD + half:HD + half + 1], st[p, CL:, half:half + 1]], 0)
        m = jnp.maximum(m_near, jnp.max(s, axis=1, keepdims=True))
        e = jnp.exp(s - m)
        scale = jnp.exp(m_near - m)
        total = jnp.sum(e, axis=1, keepdims=True) + l_near * scale
        a = dot3(*split2(e), kh[...], kl[...], NN)
        o = (dot3(*split2(a), v[0, p], v[1, p], NT) + st[p] * scale) / total
        att[p] = jnp.where(lowq, o[:CL], o[CL:])

    for copy in copies[:3]:
        copy.wait()
    for copy in copies[3:]:
        copy.start()

    def body(i, carry):
        one, two = scores(2 * i), scores(2 * i + 1)
        attend(2 * i, one)
        attend(2 * i + 1, two)
        return carry

    lax.fori_loop(0, NY // 2, body, 0)
    ah, al = split2(jnp.concatenate([att[p] for p in range(NY)], 1))
    for copy in copies[3:]:
        copy.wait()
    r = x[...] + dot3(ah, al, wo[0], wo[1], NT)
    mean = jnp.sum(r, axis=1, keepdims=True) * (1.0 / D)
    square = jnp.sum(r * r, axis=1, keepdims=True) * (1.0 / D)
    normed = (r - mean) * lax.rsqrt(square - mean * mean + 1e-05)
    hid = dot3(*split2(normed), u[0], u[1], NN)
    act = 0.5 * hid * (1.0 + lax.erf(hid * math.sqrt(0.5)))
    y = r + dot3(*split2(act), d[0], d[1], NN)
    out_ref[...] = y.T


def far_call(scalars, arrays):
    return pl.pallas_call(
        far_kernel,
        out_shape=sds(D, CL),
        in_specs=[sspec()] * len(scalars) + [vspec()] + [hspec()] * (len(arrays) - 1),
        out_specs=vspec(),
        scratch_shapes=[pltpu.VMEM((EK, D), BF), pltpu.VMEM((EK, D), BF), pltpu.VMEM((NY, CL, 2 * HD), F32)]
        + [pltpu.VMEM(a.shape, a.dtype) for a in arrays[1:]] + [pltpu.SemaphoreType.DMA((len(arrays) - 1,))],
        compiler_params=params(60),
        cost_estimate=cost(6 * 10**9, 16 << 20, 1 << 20),
        name="far",
    )(*scalars, *arrays)


def place_kernel(pos, r_ref, order_ref, out_ref):
    full = jnp.concatenate([r_ref[i * HD:(i + 1) * HD, :] for i in range(CD)], 1)
    order = jnp.concatenate([order_ref[i:i + 1, :] for i in range(CD)], 1) - pos[0]
    hi = full.astype(BF)
    rest = full - hi.astype(F32)
    mid = rest.astype(BF)
    low = (rest - mid.astype(F32)).astype(BF)
    parts = jnp.concatenate([hi, mid, low], 0)
    step = 256
    for j in range(CD * CL // step):
        nodes = lax.broadcasted_iota(jnp.int32, (step, CD * CL), 0) + j * step
        pick = jnp.where(nodes == order, 1.0, 0.0).astype(BF)
        t = mm(parts, pick, NT)
        out_ref[:, j * step:(j + 1) * step] = t[:HD] + (t[HD:2 * HD] + t[2 * HD:])


def place_call(pos, received, order):
    return pl.pallas_call(
        place_kernel,
        out_shape=sds(HD, CD * CL),
        in_specs=[sspec(), vspec(), vspec()],
        out_specs=vspec(),
        compiler_params=params(12),
        cost_estimate=cost(4 * 10**8, 1 << 20),
        name="place",
    )(pos, received, order)


def pick_kernel(group, pos, *refs):
    tables, srcs, outs, sem = refs[:NX], refs[NX:-NX - 1], refs[-NX - 1:-1], refs[-1]
    z = pos[0]
    parts, at = [], 0
    for s in group:
        size = 2 if s == NZ // 2 else 1
        parts.append(srcs[at:at + size])
        at += size

    def send(src, at, out, to):
        pltpu.make_async_copy(src.at[pl.ds(pl.multiple_of(at, PR), PR), :], out.at[to:to + PR, :], sem).start()

    for k, out in enumerate(outs):
        for i, s in enumerate(group):
            src = parts[i]
            for j in range(CAP):
                b = tables[k][(k * NZ + lax.bitwise_and(z + s, NZ - 1)) * CAP + j]
                to = (i * CAP + j) * PR
                if len(src) == 1:
                    send(src[0], b * PR, out, to)
                else:
                    at = lax.bitwise_and(b, CD // 2 - 1) * PR

                    @pl.when(b < CD // 2)
                    def _(at=at, to=to, src=src, out=out):
                        send(src[0], at, out, to)

                    @pl.when(b >= CD // 2)
                    def _(at=at, to=to, src=src, out=out):
                        send(src[1], at, out, to)

    for out in outs:
        pltpu.make_async_copy(out, out, sem).wait()


def pick_call(group, pos, tables, srcs):
    rows = len(group) * CAP * PR
    return pl.pallas_call(
        lambda *refs: pick_kernel(group, *refs),
        out_shape=[sds(rows, D)] * NX,
        in_specs=[sspec()] * (1 + NX) + [vspec()] * len(srcs),
        out_specs=[vspec()] * NX,
        scratch_shapes=[pltpu.SemaphoreType.DMA],
        compiler_params=params(8),
        cost_estimate=cost(0, NX * rows * D * 8),
        name="pick",
    )(pos, *tables, *srcs)


def send_kernel(row, *refs):
    srcs, out, held = refs[:-2], refs[-2], refs[-1]
    at = 0
    for src in srcs:
        held[at:at + src.shape[0], :] = src[...]
        at += src.shape[0]
    for i in range(CD * NE):
        out[i * PR:(i + 1) * PR, :] = held[pl.ds(pl.multiple_of(row[i], PR), PR), :]


def send_call(row, srcs):
    return pl.pallas_call(
        send_kernel,
        out_shape=sds(CD * NE * PR, D),
        in_specs=[sspec()] + [vspec()] * len(srcs),
        out_specs=vspec(),
        scratch_shapes=[pltpu.VMEM((NZ * NX * CAP * PR, D), F32)],
        compiler_params=params(12),
        cost_estimate=cost(0, 6 << 20),
        name="send",
    )(row, *srcs)


def ring(size, step):
    return [(i, (i + step) % size) for i in range(size)]


SWAP = [(0, 1), (1, 0)]


def shards(node_feats, order, node_count, local_blocks, exp_blocks, virt_blocks, virt_feats,
           w_query, w_key, w_value, w_out, w_up, w_down):
    z, x, y, c = (lax.axis_index(a) for a in ("z", "x", "y", "c"))
    head = y * NC + c
    pos = jnp.stack([(z * NX + x) * (CD * CL), head, c]).astype(jnp.int32)
    zx = jnp.stack([z, x]).astype(jnp.int32)
    order = order.reshape(CD, CL)

    piece, edge = first_call(pos, order, node_feats)

    half = CL // 2
    tie = lax.optimization_barrier

    def both_z(a, b):
        return lax.ppermute(a, "z", ring(NZ, 1)), lax.ppermute(b, "z", ring(NZ, -1))

    def swap(*arrays):
        return [lax.ppermute(t, "c", SWAP) for t in arrays]

    up, down = both_z(piece, piece)
    table, row = index_call(zx, exp_blocks)
    tables = [table] + [lax.ppermute(table, "x", ring(NX, -k)) for k in range(1, NX)]
    held = {0: (piece,), 7: (up,), 1: (down,)}
    wa, wb = pack_call(w_query.T, w_key.T, w_value.T, w_out.T, w_up, w_down)
    up, down, edge, wa, wb, *tables = tie((up, down, edge, wa, wb, *tables))
    wa = lax.all_gather(wa, ("y", "c"), axis=0, tiled=True).reshape(CD, 2 * CL, D)
    wb = lax.all_gather(wb, ("y", "c"), axis=0, tiled=True).reshape(CD, 2 * CL, D)

    e_in = lax.ppermute(edge, ("z", "x", "y", "c"), [
        (i * CD + h, (i + s) * CD + h)
        for s, hs in ((1, (0, 1)), (-1, (6, 7)))
        for i in range(NZ * NX) if 0 <= i + s < NZ * NX for h in hs])
    up, down = both_z(up, down)
    held[6], held[2] = (up,), (down,)
    up, down, e_in, *tables = tie((up, down, e_in, *tables))

    def exchange(group):
        blocks = pick_call(group, zx, tables, [t for s in group for t in held[s]])
        return [blocks[0]] + [lax.ppermute(blocks[k], "x", ring(NX, k)) for k in (1, 2, 3)]

    up, down = both_z(up, down)
    near_x = exchange(GROUPS[0])
    held[5], held[3] = (up,), (down,)
    held[4] = both_z(up[:half], down[half:])
    far_x = exchange(GROUPS[1])
    (e_other,) = swap(e_in)

    sending = send_call(row, near_x + far_x)
    xe = lax.all_to_all(sending, ("y", "c"), 0, 0, tiled=True)
    _, wa, wb, pos_late = tie((sending, wa, wb, pos))

    x_own, q, wv, wo, state = near_call(
        (pos_late, local_blocks, virt_blocks, node_count), (order, node_feats, e_in, e_other, virt_feats, wa))
    wu, wd = prep_call(wb)
    result = far_call((pos, exp_blocks, node_count), (xe, q, state, wv, x_own, wo, wu, wd))
    received = lax.all_to_all(result, ("y", "c"), 0, 0, tiled=True)
    return place_call(pos, received, order).T


def solution(mesh):
    grid = Mesh(mesh.devices.reshape(NZ, NX, NY, NC), ("z", "x", "y", "c"))
    dom, head = ("z", "x"), ("y", "c")
    return jax.shard_map(
        shards,
        mesh=grid,
        in_specs=(P(dom, None), P(dom), P(), P(dom, None), P(dom, None), P(dom), P(),
                  P(None, head), P(None, head), P(None, head), P(None, head), P(None, head),
                  P(head, None)),
        out_specs=P(dom, head),
        check_vma=False,
    )
```

```python
import math

import jax
import jax.numpy as jnp
from jax import lax
from jax.experimental import pallas as pl
from jax.experimental.pallas import tpu as pltpu
from jax.sharding import Mesh, PartitionSpec as P

D = 512
HD = 64
FF = 1024
CL = 128
CD = 8
NE = 6
NL = 3
CAP = 3
NZ, NX, NY, NC = 8, 4, 4, 2
PR = CL // (NY * NC)
EK = NE * CL
LK = (NL + 1) * CL
NEG = -1e30
VMEM_BYTES = 67043328
BF = jnp.bfloat16
F32 = jnp.float32
NT = (((1,), (1,)), ((), ()))
NN = (((1,), (0,)), ((), ()))

GROUPS = ((0, 1, 7), (2, 6), (3, 5, 4))


def split2(v):
    hi = v.astype(BF)
    return hi, (v - hi.astype(F32)).astype(BF)


def mm(a, b, dims):
    return lax.dot_general(a, b, dims, preferred_element_type=F32)


def dot3(ah, al, bh, bl, dims):
    return mm(ah, bh, dims) + (mm(ah, bl, dims) + mm(al, bh, dims))


def vspec():
    return pl.BlockSpec(memory_space=pltpu.VMEM)


def hspec():
    return pl.BlockSpec(memory_space=pltpu.HBM)


def sspec():
    return pl.BlockSpec(memory_space=pltpu.SMEM)


def params(mb):
    return pltpu.CompilerParams(vmem_limit_bytes=mb << 20)


def cost(flops, bytes_accessed, transcendentals=0):
    return pl.CostEstimate(flops=flops, bytes_accessed=bytes_accessed, transcendentals=transcendentals)


def sds(*shape, dtype=F32):
    return jax.ShapeDtypeStruct(shape, dtype)


def columns(row):
    return jnp.broadcast_to(row, (CL, CL)).T


def one_hot(cols):
    lanes = lax.broadcasted_iota(jnp.int32, cols.shape, 1).astype(F32)
    parts = [jnp.where(cols == lanes + float(j * CL), 1.0, 0.0).astype(BF) for j in range(CD)]
    return jnp.concatenate(parts, 1)


def first_kernel(pos, order_hbm, nodes_hbm, piece_out, edge_out, order_ref, nodes, sems):
    base, head, c = pos[0], pos[1], pos[2]
    step = 2 * CL
    parts = CD * CL // step
    fetch = [pltpu.make_async_copy(order_hbm, order_ref, sems.at[0])] + [
        pltpu.make_async_copy(nodes_hbm.at[i * step:(i + 1) * step, :], nodes.at[i * step:(i + 1) * step, :],
                              sems.at[i + 1]) for i in range(parts)]
    for copy in fetch:
        copy.start()
    fetch[0].wait()
    order = (order_ref[...] - base).astype(F32)
    mine = pltpu.roll(order, lax.rem(CL - head * PR, CL), 1)
    col = jnp.concatenate([mine] + [jnp.zeros((CL - CD, CL), F32)], 0).T
    pieces = [jnp.broadcast_to(col[:PR, k:k + 1], (PR, CL)) for k in range(CD)]
    edge = jnp.where(head < NY, CD - NC + c, c)
    edge_row = (order_ref[pl.ds(edge, 1), :] - base).astype(F32)
    pick = one_hot(jnp.concatenate(pieces + [columns(edge_row)], 0))
    rows = jnp.zeros((2 * CL, D), F32)
    for i in range(parts):
        fetch[i + 1].wait()
        hi, lo = split2(nodes[i * step:(i + 1) * step, :])
        some = pick[:, i * step:(i + 1) * step]
        rows = rows + (mm(some, hi, NN) + mm(some, lo, NN))
    piece_out[...] = rows[:CL]
    edge_out[...] = rows[CL:]


def first_call(pos, order, nodes):
    return pl.pallas_call(
        first_kernel,
        out_shape=[sds(CL, D), sds(CL, D)],
        in_specs=[sspec(), hspec(), hspec()],
        out_specs=[vspec()] * 2,
        scratch_shapes=[pltpu.VMEM((CD, CL), jnp.int32), pltpu.VMEM((CD * CL, D), F32),
                        pltpu.SemaphoreType.DMA((5,))],
        compiler_params=params(60),
        cost_estimate=cost(10**9, 3 << 20),
        name="first",
    )(pos, order, nodes)


def setup_kernel(pos, exp_ref, q, k, v, o, up, down, table, row, att, ffw, seen, starts, widths, sems):
    pairs = [(w, att.at[i * HD:(i + 1) * HD, :]) for i, w in enumerate((q, k, v, o))]
    pairs.append((down, ffw.at[:CL, :]))
    pairs += [(up.at[j * CL:(j + 1) * CL, :], ffw.at[CL:, j * CL:(j + 1) * CL]) for j in range(4)]
    copies = [pltpu.make_async_copy(src, dst, sems.at[i]) for i, (src, dst) in enumerate(pairs)]
    for copy in copies:
        copy.start()
    z, x = pos[0], pos[1]
    start = 0
    for group in GROUPS:
        for p, s in enumerate(group):
            starts[s] = start + p * CAP
            widths[s] = len(group) * CAP
        start += NX * len(group) * CAP
    for i in range(NX * NZ * CAP):
        table[i] = 0
    for i in range(NZ * NX):
        seen[i] = 0

    def place(i, carry):
        for e in range(NE):
            block = exp_ref[i, e]
            owner = lax.shift_right_logical(block, 3)
            rank = seen[owner]
            seen[owner] = rank + 1
            oz = lax.shift_right_logical(owner, 2)
            back = lax.bitwise_and(x - lax.bitwise_and(owner, NX - 1), NX - 1)
            table[back * (NZ * CAP) + oz * CAP + rank] = lax.bitwise_and(block, CD - 1)
            off = lax.bitwise_and(oz - z, NZ - 1)
            row[i * NE + e] = (starts[off] + back * widths[off] + rank) * PR
        return carry

    lax.fori_loop(0, CD, place, 0)
    for copy in copies:
        copy.wait()


def setup_call(pos, exp_blocks, *w):
    return pl.pallas_call(
        setup_kernel,
        out_shape=[sds(NX * NZ * CAP, dtype=jnp.int32), sds(CD * NE, dtype=jnp.int32),
                   sds(2 * CL, D), sds(2 * CL, D)],
        in_specs=[sspec()] * 2 + [hspec()] * 6,
        out_specs=[sspec()] * 2 + [vspec()] * 2,
        scratch_shapes=[pltpu.SMEM((NZ * NX,), jnp.int32), pltpu.SMEM((NZ,), jnp.int32), pltpu.SMEM((NZ,), jnp.int32),
                        pltpu.SemaphoreType.DMA((9,))],
        compiler_params=params(60),
        cost_estimate=cost(1000, 2 << 20),
        name="setup",
    )(pos, exp_blocks, *w)


def near_kernel(pos, local_ref, virt_ref, count_ref, order_ref, nodes_ref, e_in, e_other, virtual_ref, mine_hbm, other_hbm,
                x_out, q_out, v_out, o_out, state, kh, kl, mine, other, sems):
    fetch = [pltpu.make_async_copy(mine_hbm, mine, sems.at[0]), pltpu.make_async_copy(other_hbm, other, sems.at[1])]
    for copy in fetch:
        copy.start()
    base, head, c = pos[0], pos[1], pos[2]
    first = lax.shift_right_logical(base, 7)

    def order_row(r):
        return columns((order_ref[pl.ds(r, 1), :] - base).astype(F32))

    rel = [local_ref[head, j] - first for j in range(NL)]
    rows = [order_row(jnp.clip(r, 0, CD - 1)) for r in rel] + [order_row(head)]
    pick = one_hot(jnp.concatenate(rows, 0))
    nodes = nodes_ref[...]
    hi, lo = split2(nodes)
    got = mm(pick, hi, NN) + mm(pick, lo, NN)
    last = (nodes - hi.astype(F32) - lo.astype(F32)).astype(BF)
    x = got[NL * CL:] + mm(pick[NL * CL:], last, NN)
    x_out[...] = x
    lane = lax.broadcasted_iota(jnp.int32, (1, CL), 1)
    bias = []
    for j in range(NL):
        r = rel[j]
        at = jnp.where(r < 0, r + NC, r - CD)
        edge = jnp.where(at == c, e_in[...], e_other[...])
        keys = jnp.where((r >= 0) & (r < CD), got[j * CL:(j + 1) * CL], edge)
        kh[j * CL:(j + 1) * CL, :], kl[j * CL:(j + 1) * CL, :] = split2(keys)
        bias.append(jnp.where(lane < count_ref[local_ref[head, j]], 0.0, NEG))
    vat = pl.multiple_of(virt_ref[head] * CL, CL)
    kh[NL * CL:, :], kl[NL * CL:, :] = split2(virtual_ref[pl.ds(vat, CL), :])
    bias = jnp.concatenate(bias + [jnp.zeros((1, CL), F32)], 1)

    lanes = lax.broadcasted_iota(jnp.int32, (CL, 2 * HD), 1)
    lowq = lanes < HD
    xh, xl = split2(x)
    for copy in fetch:
        copy.wait()
    for at in range(NY):
        a, b = mine[at * 2 * CL:(at + 1) * 2 * CL, :], other[at * 2 * CL:(at + 1) * 2 * CL, :]
        left, right = jnp.where(c == 0, a, b), jnp.where(c == 0, b, a)
        wq, wk, wv, wo = (
            split2(jnp.concatenate([left[i * HD:(i + 1) * HD], right[i * HD:(i + 1) * HD]], 0))
            for i in range(4))
        q = dot3(xh, xl, *wq, NT) * (1.0 / math.sqrt(HD))
        both = jnp.concatenate([jnp.where(lowq, q, 0.0), jnp.where(lowq, 0.0, q)], 0)
        q_out[0, at], q_out[1, at] = split2(dot3(*split2(both), *wk, NN))
        v_out[0, at], v_out[1, at] = wv
        rows = slice(at * CL, (at + 1) * CL)
        o_out[0, rows, :], o_out[1, rows, :] = wo

    def body(p, carry):
        s = dot3(q_out[0, p], q_out[1, p], kh[...], kl[...], NT) + bias
        m = jnp.max(s, axis=1, keepdims=True)
        e = jnp.exp(s - m)
        l = jnp.sum(e, axis=1, keepdims=True)
        a = dot3(*split2(e), kh[...], kl[...], NN)
        o = dot3(*split2(a), v_out[0, p], v_out[1, p], NT)
        state[p, :CL, :] = jnp.where(lowq, o[:CL], jnp.where(lanes < HD + HD // 2, m[:CL], l[:CL]))
        state[p, CL:, :] = jnp.where(lowq, jnp.where(lanes < HD // 2, m[CL:], l[CL:]), o[CL:])
        return carry

    lax.fori_loop(0, NY, body, 0)


def near_call(scalars, arrays):
    shapes = [
        sds(CL, D), sds(2, NY, 2 * CL, D, dtype=BF), sds(2, NY, 2 * HD, D, dtype=BF),
        sds(2, D, D, dtype=BF), sds(NY, 2 * CL, 2 * HD),
    ]
    return pl.pallas_call(
        near_kernel,
        out_shape=shapes,
        in_specs=[sspec()] * len(scalars) + [vspec()] * (len(arrays) - 2) + [hspec()] * 2,
        out_specs=[vspec()] * len(shapes),
        scratch_shapes=[pltpu.VMEM((LK, D), BF), pltpu.VMEM((LK, D), BF), pltpu.VMEM(arrays[-1].shape, F32),
                        pltpu.VMEM(arrays[-1].shape, F32), pltpu.SemaphoreType.DMA((2,))],
        compiler_params=params(60),
        cost_estimate=cost(6 * 10**9, 16 << 20, 1 << 20),
        name="near",
    )(*scalars, *arrays)


def prep_kernel(mine, other, u_out, d_out):
    for i in range(8):
        w, at = (mine, other)[i // NY], i % NY * 2 * CL
        rows = slice(i * CL, (i + 1) * CL)
        d_out[0, rows, :], d_out[1, rows, :] = split2(w[at:at + CL, :])
        hi, lo = split2(w[at + CL:at + 2 * CL, :])
        for j in range(4):
            cols = slice(j * CL, (j + 1) * CL)
            u_out[0, cols, rows] = hi[:, cols]
            u_out[1, cols, rows] = lo[:, cols]


def prep_call(mine, other):
    return pl.pallas_call(
        prep_kernel,
        out_shape=[sds(2, D, FF, dtype=BF), sds(2, FF, D, dtype=BF)],
        in_specs=[vspec()] * 2,
        out_specs=[vspec()] * 2,
        compiler_params=params(60),
        cost_estimate=cost(10**7, 8 << 20),
        name="prep",
    )(mine, other)


def far_kernel(pos, exp_ref, count_ref, xe_ref, q_hbm, s_hbm, v_hbm, x_hbm, o_hbm, u_hbm, d_hbm,
               out_ref, kh, kl, att, q, st, v, x, wo, u, d, sems):
    copies = [pltpu.make_async_copy(src, dst, sems.at[i]) for i, (src, dst) in enumerate(zip(
        (q_hbm, s_hbm, v_hbm, x_hbm, o_hbm, u_hbm, d_hbm), (q, st, v, x, wo, u, d)))]
    for copy in copies[:3]:
        copy.start()
    head = pos[1]
    hi, lo = split2(xe_ref[...])
    kh[...] = hi
    kl[...] = lo
    lowq = lax.broadcasted_iota(jnp.int32, (CL, 2 * HD), 1) < HD
    n = lax.broadcasted_iota(jnp.int32, (1, EK), 1)

    def steps(v, width, count):
        return sum(jnp.where(v >= width * k, 1, 0) for k in range(1, count))

    piece = steps(n, NE * PR, CD)
    r = n - piece * (NE * PR)
    entry = steps(r, PR, NE)
    slot = piece * PR + r - entry * PR
    bias = jnp.zeros((1, EK), F32)
    for e in range(NE):
        bad = (entry == e) & (slot >= count_ref[exp_ref[head, e]])
        bias = jnp.where(bad, NEG, bias)

    def scores(p):
        return dot3(q[0, p], q[1, p], kh[...], kl[...], NT) + bias

    def attend(p, s):
        m_near = jnp.concatenate([st[p, :CL, HD:HD + 1], st[p, CL:, :1]], 0)
        half = HD // 2
        l_near = jnp.concatenate([st[p, :CL, HD + half:HD + half + 1], st[p, CL:, half:half + 1]], 0)
        m = jnp.maximum(m_near, jnp.max(s, axis=1, keepdims=True))
        e = jnp.exp(s - m)
        scale = jnp.exp(m_near - m)
        total = jnp.sum(e, axis=1, keepdims=True) + l_near * scale
        a = dot3(*split2(e), kh[...], kl[...], NN)
        o = (dot3(*split2(a), v[0, p], v[1, p], NT) + st[p] * scale) / total
        att[p] = jnp.where(lowq, o[:CL], o[CL:])

    for copy in copies[:3]:
        copy.wait()
    for copy in copies[3:]:
        copy.start()

    def body(i, carry):
        one, two = scores(2 * i), scores(2 * i + 1)
        attend(2 * i, one)
        attend(2 * i + 1, two)
        return carry

    lax.fori_loop(0, NY // 2, body, 0)
    ah, al = split2(jnp.concatenate([att[p] for p in range(NY)], 1))
    for copy in copies[3:]:
        copy.wait()
    r = x[...] + dot3(ah, al, wo[0], wo[1], NT)
    mean = jnp.sum(r, axis=1, keepdims=True) * (1.0 / D)
    square = jnp.sum(r * r, axis=1, keepdims=True) * (1.0 / D)
    normed = (r - mean) * lax.rsqrt(square - mean * mean + 1e-05)
    hid = dot3(*split2(normed), u[0], u[1], NN)
    act = 0.5 * hid * (1.0 + lax.erf(hid * math.sqrt(0.5)))
    y = r + dot3(*split2(act), d[0], d[1], NN)
    out_ref[...] = y.T


def far_call(scalars, arrays):
    return pl.pallas_call(
        far_kernel,
        out_shape=sds(D, CL),
        in_specs=[sspec()] * len(scalars) + [vspec()] + [hspec()] * (len(arrays) - 1),
        out_specs=vspec(),
        scratch_shapes=[pltpu.VMEM((EK, D), BF), pltpu.VMEM((EK, D), BF), pltpu.VMEM((NY, CL, 2 * HD), F32)]
        + [pltpu.VMEM(a.shape, a.dtype) for a in arrays[1:]] + [pltpu.SemaphoreType.DMA((len(arrays) - 1,))],
        compiler_params=params(60),
        cost_estimate=cost(6 * 10**9, 16 << 20, 1 << 20),
        name="far",
    )(*scalars, *arrays)


def place_kernel(pos, r_ref, order_ref, out_ref):
    full = jnp.concatenate([r_ref[i * HD:(i + 1) * HD, :] for i in range(CD)], 1)
    order = jnp.concatenate([order_ref[i:i + 1, :] for i in range(CD)], 1) - pos[0]
    hi = full.astype(BF)
    rest = full - hi.astype(F32)
    mid = rest.astype(BF)
    low = (rest - mid.astype(F32)).astype(BF)
    parts = jnp.concatenate([hi, mid, low], 0)
    step = 256
    for j in range(CD * CL // step):
        nodes = lax.broadcasted_iota(jnp.int32, (step, CD * CL), 0) + j * step
        pick = jnp.where(nodes == order, 1.0, 0.0).astype(BF)
        t = mm(parts, pick, NT)
        out_ref[:, j * step:(j + 1) * step] = t[:HD] + (t[HD:2 * HD] + t[2 * HD:])


def place_call(pos, received, order):
    return pl.pallas_call(
        place_kernel,
        out_shape=sds(HD, CD * CL),
        in_specs=[sspec(), vspec(), vspec()],
        out_specs=vspec(),
        compiler_params=params(12),
        cost_estimate=cost(4 * 10**8, 1 << 20),
        name="place",
    )(pos, received, order)


def pick_kernel(group, pos, *refs):
    tables, srcs, outs = refs[:NX], refs[NX:-NX], refs[-NX:]
    z = pos[0]
    parts, at = [], 0
    for s in group:
        size = 2 if s == NZ // 2 else 1
        parts.append(srcs[at:at + size])
        at += size

    for k, out in enumerate(outs):
        for i, s in enumerate(group):
            src = parts[i]
            for j in range(CAP):
                b = tables[k][(k * NZ + lax.bitwise_and(z + s, NZ - 1)) * CAP + j]
                if len(src) == 1:
                    block = src[0][pl.ds(pl.multiple_of(b * PR, PR), PR), :]
                else:
                    at = pl.multiple_of(lax.bitwise_and(b, CD // 2 - 1) * PR, PR)
                    block = jnp.where(b < CD // 2, src[0][pl.ds(at, PR), :], src[1][pl.ds(at, PR), :])
                out[(i * CAP + j) * PR:(i * CAP + j + 1) * PR, :] = block


def pick_call(group, pos, tables, srcs):
    rows = len(group) * CAP * PR
    return pl.pallas_call(
        lambda *refs: pick_kernel(group, *refs),
        out_shape=[sds(rows, D)] * NX,
        in_specs=[sspec()] * (1 + NX) + [vspec()] * len(srcs),
        out_specs=[vspec()] * NX,
        compiler_params=params(8),
        cost_estimate=cost(0, NX * rows * D * 8),
        name="pick",
    )(pos, *tables, *srcs)


def send_kernel(row, *refs):
    srcs, out, held = refs[:-2], refs[-2], refs[-1]
    at = 0
    for src in srcs:
        held[at:at + src.shape[0], :] = src[...]
        at += src.shape[0]
    for i in range(CD * NE):
        out[i * PR:(i + 1) * PR, :] = held[pl.ds(pl.multiple_of(row[i], PR), PR), :]


def send_call(row, srcs):
    return pl.pallas_call(
        send_kernel,
        out_shape=sds(CD * NE * PR, D),
        in_specs=[sspec()] + [vspec()] * len(srcs),
        out_specs=vspec(),
        scratch_shapes=[pltpu.VMEM((NZ * NX * CAP * PR, D), F32)],
        compiler_params=params(12),
        cost_estimate=cost(0, 6 << 20),
        name="send",
    )(row, *srcs)


def ring(size, step):
    return [(i, (i + step) % size) for i in range(size)]


SWAP = [(0, 1), (1, 0)]


def shards(node_feats, order, node_count, local_blocks, exp_blocks, virt_blocks, virt_feats,
           w_query, w_key, w_value, w_out, w_up, w_down):
    z, x, y, c = (lax.axis_index(a) for a in ("z", "x", "y", "c"))
    head = y * NC + c
    pos = jnp.stack([(z * NX + x) * (CD * CL), head, c]).astype(jnp.int32)
    zx = jnp.stack([z, x]).astype(jnp.int32)
    order = order.reshape(CD, CL)

    piece, edge = first_call(pos, order, node_feats)

    half = CL // 2
    tie = lax.optimization_barrier

    def both_z(a, b):
        return lax.ppermute(a, "z", ring(NZ, 1)), lax.ppermute(b, "z", ring(NZ, -1))

    def swap(*arrays):
        return [lax.ppermute(t, "c", SWAP) for t in arrays]

    up, down = both_z(piece, piece)
    table, row, wa, wb = setup_call(zx, exp_blocks, w_query.T, w_key.T, w_value.T, w_out.T, w_up, w_down)
    tables = [table] + [lax.ppermute(table, "x", ring(NX, -k)) for k in range(1, NX)]
    held = {0: (piece,), 7: (up,), 1: (down,)}
    up, down, edge, wa, wb, *tables = tie((up, down, edge, wa, wb, *tables))
    wa = lax.all_gather(wa, "y", axis=0, tiled=True)
    wb = lax.all_gather(wb, "y", axis=0, tiled=True)

    def pick(group):
        return pick_call(group, zx, tables, [t for s in group for t in held[s]])

    def exchange(blocks):
        return [blocks[0]] + [lax.ppermute(blocks[k], "x", ring(NX, k)) for k in (1, 2, 3)]

    one = pick(GROUPS[0])
    up, down = both_z(up, down)
    held[6], held[2] = (up,), (down,)
    up, down, *_ = tie((up, down, *one))
    one = exchange(one)
    two = pick(GROUPS[1])
    up, down = both_z(up, down)
    held[5], held[3] = (up,), (down,)
    up, down, *_ = tie((up, down, *one, *two))
    held[4] = both_z(up[:half], down[half:])
    arrived = one + exchange(two) + exchange(pick(GROUPS[2]))

    sending = send_call(row, arrived)
    xe = lax.all_to_all(sending, ("y", "c"), 0, 0, tiled=True)

    _, wa, wb, edge, pos_late = tie((sending, wa, wb, edge, pos))
    e_in = lax.ppermute(edge, ("z", "x", "y", "c"), [
        (i * CD + h, (i + s) * CD + h)
        for s, hs in ((1, (0, 1)), (-1, (6, 7)))
        for i in range(NZ * NX) if 0 <= i + s < NZ * NX for h in hs])
    e_other, wa_other, wb_other = swap(e_in, wa, wb)
    x_own, q, wv, wo, state = near_call(
        (pos_late, local_blocks, virt_blocks, node_count),
        (order, node_feats, e_in, e_other, virt_feats, wa, wa_other))
    state, wb, wb_other = tie((state, wb, wb_other))
    wu, wd = prep_call(wb, wb_other)
    result = far_call((pos, exp_blocks, node_count), (xe, q, state, wv, x_own, wo, wu, wd))
    received = lax.all_to_all(result, ("y", "c"), 0, 0, tiled=True)
    return place_call(pos, received, order).T


def solution(mesh):
    grid = Mesh(mesh.devices.reshape(NZ, NX, NY, NC), ("z", "x", "y", "c"))
    dom, head = ("z", "x"), ("y", "c")
    return jax.shard_map(
        shards,
        mesh=grid,
        in_specs=(P(dom, None), P(dom), P(), P(dom, None), P(dom, None), P(dom), P(),
                  P(None, head), P(None, head), P(None, head), P(None, head), P(None, head),
                  P(head, None)),
        out_specs=P(dom, head),
        check_vma=False,
    )
```

```python
import math

import jax
import jax.numpy as jnp
from jax import lax
from jax.experimental import pallas as pl
from jax.experimental.pallas import tpu as pltpu
from jax.sharding import Mesh, PartitionSpec as P

D = 512
HD = 64
FF = 1024
CL = 128
CD = 8
NE = 6
NL = 3
CAP = 3
NZ, NX, NY, NC = 8, 4, 4, 2
PR = CL // (NY * NC)
EK = NE * CL
LK = (NL + 1) * CL
NEG = -1e30
VMEM_BYTES = 67043328
BF = jnp.bfloat16
F32 = jnp.float32
NT = (((1,), (1,)), ((), ()))
NN = (((1,), (0,)), ((), ()))

GROUPS = ((0, 1, 7), (2, 6, 3, 5, 4))


def split2(v):
    hi = v.astype(BF)
    return hi, (v - hi.astype(F32)).astype(BF)


def mm(a, b, dims):
    return lax.dot_general(a, b, dims, preferred_element_type=F32)


def dot3(ah, al, bh, bl, dims):
    return mm(ah, bh, dims) + (mm(ah, bl, dims) + mm(al, bh, dims))


def vspec():
    return pl.BlockSpec(memory_space=pltpu.VMEM)


def hspec():
    return pl.BlockSpec(memory_space=pltpu.HBM)


def sspec():
    return pl.BlockSpec(memory_space=pltpu.SMEM)


def params(mb):
    return pltpu.CompilerParams(vmem_limit_bytes=mb << 20)


def cost(flops, bytes_accessed, transcendentals=0):
    return pl.CostEstimate(flops=flops, bytes_accessed=bytes_accessed, transcendentals=transcendentals)


def sds(*shape, dtype=F32):
    return jax.ShapeDtypeStruct(shape, dtype)


def columns(row):
    return jnp.broadcast_to(row, (CL, CL)).T


def one_hot(cols):
    lanes = lax.broadcasted_iota(jnp.int32, cols.shape, 1).astype(F32)
    parts = [jnp.where(cols == lanes + float(j * CL), 1.0, 0.0).astype(BF) for j in range(CD)]
    return jnp.concatenate(parts, 1)


def first_kernel(pos, order_hbm, nodes_hbm, piece_out, edge_out, order_ref, nodes, sems):
    base, head, c = pos[0], pos[1], pos[2]
    step = 2 * CL
    parts = CD * CL // step
    fetch = [pltpu.make_async_copy(order_hbm, order_ref, sems.at[0])] + [
        pltpu.make_async_copy(nodes_hbm.at[i * step:(i + 1) * step, :], nodes.at[i * step:(i + 1) * step, :],
                              sems.at[i + 1]) for i in range(parts)]
    for copy in fetch:
        copy.start()
    fetch[0].wait()
    order = (order_ref[...] - base).astype(F32)
    mine = pltpu.roll(order, lax.rem(CL - head * PR, CL), 1)
    col = jnp.concatenate([mine] + [jnp.zeros((CL - CD, CL), F32)], 0).T
    pieces = [jnp.broadcast_to(col[:PR, k:k + 1], (PR, CL)) for k in range(CD)]
    edge = jnp.where(head < NY, CD - NC + c, c)
    edge_row = (order_ref[pl.ds(edge, 1), :] - base).astype(F32)
    pick = one_hot(jnp.concatenate(pieces + [columns(edge_row)], 0))
    rows = jnp.zeros((2 * CL, D), F32)
    for i in range(parts):
        fetch[i + 1].wait()
        hi, lo = split2(nodes[i * step:(i + 1) * step, :])
        some = pick[:, i * step:(i + 1) * step]
        rows = rows + (mm(some, hi, NN) + mm(some, lo, NN))
    piece_out[...] = rows[:CL]
    edge_out[...] = rows[CL:]


def first_call(pos, order, nodes):
    return pl.pallas_call(
        first_kernel,
        out_shape=[sds(CL, D), sds(CL, D)],
        in_specs=[sspec(), hspec(), hspec()],
        out_specs=[vspec()] * 2,
        scratch_shapes=[pltpu.VMEM((CD, CL), jnp.int32), pltpu.VMEM((CD * CL, D), F32),
                        pltpu.SemaphoreType.DMA((5,))],
        compiler_params=params(60),
        cost_estimate=cost(10**9, 3 << 20),
        name="first",
    )(pos, order, nodes)


def setup_kernel(pos, exp_ref, q, k, v, o, up, down, table, row, out, seen, starts, widths, sems):
    pairs = [(w, out.at[i * HD:(i + 1) * HD, :]) for i, w in enumerate((q, k, v, o))]
    pairs.append((down, out.at[2 * CL:3 * CL, :]))
    pairs += [(up.at[j * CL:(j + 1) * CL, :], out.at[3 * CL:, j * CL:(j + 1) * CL]) for j in range(4)]
    copies = [pltpu.make_async_copy(src, dst, sems.at[i]) for i, (src, dst) in enumerate(pairs)]
    for copy in copies:
        copy.start()
    z, x = pos[3], pos[4]
    start = 0
    for group in GROUPS:
        for p, s in enumerate(group):
            starts[s] = start + p * CAP
            widths[s] = len(group) * CAP
        start += NX * len(group) * CAP
    for i in range(NX * NZ * CAP):
        table[i] = 0
    for i in range(NZ * NX):
        seen[i] = 0

    def place(i, carry):
        for e in range(NE):
            block = exp_ref[i, e]
            owner = lax.shift_right_logical(block, 3)
            rank = seen[owner]
            seen[owner] = rank + 1
            oz = lax.shift_right_logical(owner, 2)
            back = lax.bitwise_and(x - lax.bitwise_and(owner, NX - 1), NX - 1)
            table[back * (NZ * CAP) + oz * CAP + rank] = lax.bitwise_and(block, CD - 1)
            off = lax.bitwise_and(oz - z, NZ - 1)
            row[i * NE + e] = (starts[off] + back * widths[off] + rank) * PR
        return carry

    lax.fori_loop(0, CD, place, 0)
    for copy in copies:
        copy.wait()


def setup_call(pos, exp_blocks, *w):
    return pl.pallas_call(
        setup_kernel,
        out_shape=[sds(NX * NZ * CAP, dtype=jnp.int32), sds(CD * NE, dtype=jnp.int32),
                   sds(D, D)],
        in_specs=[sspec()] * 2 + [hspec()] * 6,
        out_specs=[sspec()] * 2 + [vspec()],
        scratch_shapes=[pltpu.SMEM((NZ * NX,), jnp.int32), pltpu.SMEM((NZ,), jnp.int32), pltpu.SMEM((NZ,), jnp.int32),
                        pltpu.SemaphoreType.DMA((9,))],
        compiler_params=params(60),
        cost_estimate=cost(1000, 2 << 20),
        name="setup",
    )(pos, exp_blocks, *w)


def near_kernel(pos, local_ref, virt_ref, count_ref, order_ref, nodes_ref, e_in, e_other, virtual_ref, w_hbm,
                x_out, q_out, v_out, o_out, state, kh, kl, w, sem):
    fetch = pltpu.make_async_copy(w_hbm.at[:, :2 * CL, :], w, sem)
    fetch.start()
    base, head, c = pos[0], pos[1], pos[2]
    first = lax.shift_right_logical(base, 7)

    def order_row(r):
        return columns((order_ref[pl.ds(r, 1), :] - base).astype(F32))

    rel = [local_ref[head, j] - first for j in range(NL)]
    rows = [order_row(jnp.clip(r, 0, CD - 1)) for r in rel] + [order_row(head)]
    pick = one_hot(jnp.concatenate(rows, 0))
    nodes = nodes_ref[...]
    hi, lo = split2(nodes)
    got = mm(pick, hi, NN) + mm(pick, lo, NN)
    last = (nodes - hi.astype(F32) - lo.astype(F32)).astype(BF)
    x = got[NL * CL:] + mm(pick[NL * CL:], last, NN)
    x_out[...] = x
    lane = lax.broadcasted_iota(jnp.int32, (1, CL), 1)
    bias = []
    for j in range(NL):
        r = rel[j]
        at = jnp.where(r < 0, r + NC, r - CD)
        edge = jnp.where(at == c, e_in[...], e_other[...])
        keys = jnp.where((r >= 0) & (r < CD), got[j * CL:(j + 1) * CL], edge)
        kh[j * CL:(j + 1) * CL, :], kl[j * CL:(j + 1) * CL, :] = split2(keys)
        bias.append(jnp.where(lane < count_ref[local_ref[head, j]], 0.0, NEG))
    vat = pl.multiple_of(virt_ref[head] * CL, CL)
    kh[NL * CL:, :], kl[NL * CL:, :] = split2(virtual_ref[pl.ds(vat, CL), :])
    bias = jnp.concatenate(bias + [jnp.zeros((1, CL), F32)], 1)

    lanes = lax.broadcasted_iota(jnp.int32, (CL, 2 * HD), 1)
    lowq = lanes < HD
    xh, xl = split2(x)
    fetch.wait()
    for at in range(NY):
        left, right = w[2 * at], w[2 * at + 1]
        wq, wk, wv, wo = (
            split2(jnp.concatenate([left[i * HD:(i + 1) * HD], right[i * HD:(i + 1) * HD]], 0))
            for i in range(4))
        q = dot3(xh, xl, *wq, NT) * (1.0 / math.sqrt(HD))
        both = jnp.concatenate([jnp.where(lowq, q, 0.0), jnp.where(lowq, 0.0, q)], 0)
        q_out[0, at], q_out[1, at] = split2(dot3(*split2(both), *wk, NN))
        v_out[0, at], v_out[1, at] = wv
        rows = slice(at * CL, (at + 1) * CL)
        o_out[0, rows, :], o_out[1, rows, :] = wo

    def body(p, carry):
        s = dot3(q_out[0, p], q_out[1, p], kh[...], kl[...], NT) + bias
        m = jnp.max(s, axis=1, keepdims=True)
        e = jnp.exp(s - m)
        l = jnp.sum(e, axis=1, keepdims=True)
        a = dot3(*split2(e), kh[...], kl[...], NN)
        o = dot3(*split2(a), v_out[0, p], v_out[1, p], NT)
        state[p, :CL, :] = jnp.where(lowq, o[:CL], jnp.where(lanes < HD + HD // 2, m[:CL], l[:CL]))
        state[p, CL:, :] = jnp.where(lowq, jnp.where(lanes < HD // 2, m[CL:], l[CL:]), o[CL:])
        return carry

    lax.fori_loop(0, NY, body, 0)


def near_call(scalars, arrays):
    shapes = [
        sds(CL, D), sds(2, NY, 2 * CL, D, dtype=BF), sds(2, NY, 2 * HD, D, dtype=BF),
        sds(2, D, D, dtype=BF), sds(NY, 2 * CL, 2 * HD),
    ]
    return pl.pallas_call(
        near_kernel,
        out_shape=shapes,
        in_specs=[sspec()] * len(scalars) + [vspec()] * (len(arrays) - 1) + [hspec()],
        out_specs=[vspec()] * len(shapes),
        scratch_shapes=[pltpu.VMEM((LK, D), BF), pltpu.VMEM((LK, D), BF), pltpu.VMEM((CD, 2 * CL, D), F32),
                        pltpu.SemaphoreType.DMA],
        compiler_params=params(60),
        cost_estimate=cost(6 * 10**9, 16 << 20, 1 << 20),
        name="near",
    )(*scalars, *arrays)


def prep_kernel(w_hbm, u_out, d_out, w, sems):
    fetch = [pltpu.make_async_copy(w_hbm.at[i, 2 * CL:, :], w.at[i], sems.at[i]) for i in range(CD)]
    for copy in fetch:
        copy.start()
    for i in range(CD):
        fetch[i].wait()
        rows = slice(i * CL, (i + 1) * CL)
        d_out[0, rows, :], d_out[1, rows, :] = split2(w[i, :CL, :])
        hi, lo = split2(w[i, CL:, :])
        for j in range(4):
            cols = slice(j * CL, (j + 1) * CL)
            u_out[0, cols, rows] = hi[:, cols]
            u_out[1, cols, rows] = lo[:, cols]


def prep_call(weights):
    return pl.pallas_call(
        prep_kernel,
        out_shape=[sds(2, D, FF, dtype=BF), sds(2, FF, D, dtype=BF)],
        in_specs=[hspec()],
        out_specs=[vspec()] * 2,
        scratch_shapes=[pltpu.VMEM((CD, 2 * CL, D), F32), pltpu.SemaphoreType.DMA((CD,))],
        compiler_params=params(60),
        cost_estimate=cost(10**7, 8 << 20),
        name="prep",
    )(weights)


def far_kernel(pos, exp_ref, count_ref, xe_ref, q_hbm, s_hbm, v_hbm, x_hbm, o_hbm, u_hbm, d_hbm,
               out_ref, kh, kl, att, q, st, v, x, wo, u, d, sems):
    copies = [pltpu.make_async_copy(src, dst, sems.at[i]) for i, (src, dst) in enumerate(zip(
        (q_hbm, s_hbm, v_hbm, x_hbm, o_hbm, u_hbm, d_hbm), (q, st, v, x, wo, u, d)))]
    for copy in copies[:3]:
        copy.start()
    head = pos[1]
    hi, lo = split2(xe_ref[...])
    kh[...] = hi
    kl[...] = lo
    lowq = lax.broadcasted_iota(jnp.int32, (CL, 2 * HD), 1) < HD
    n = lax.broadcasted_iota(jnp.int32, (1, EK), 1)

    def steps(v, width, count):
        return sum(jnp.where(v >= width * k, 1, 0) for k in range(1, count))

    piece = steps(n, NE * PR, CD)
    r = n - piece * (NE * PR)
    entry = steps(r, PR, NE)
    slot = piece * PR + r - entry * PR
    bias = jnp.zeros((1, EK), F32)
    for e in range(NE):
        bad = (entry == e) & (slot >= count_ref[exp_ref[head, e]])
        bias = jnp.where(bad, NEG, bias)

    def scores(p):
        return dot3(q[0, p], q[1, p], kh[...], kl[...], NT) + bias

    def attend(p, s):
        m_near = jnp.concatenate([st[p, :CL, HD:HD + 1], st[p, CL:, :1]], 0)
        half = HD // 2
        l_near = jnp.concatenate([st[p, :CL, HD + half:HD + half + 1], st[p, CL:, half:half + 1]], 0)
        m = jnp.maximum(m_near, jnp.max(s, axis=1, keepdims=True))
        e = jnp.exp(s - m)
        scale = jnp.exp(m_near - m)
        total = jnp.sum(e, axis=1, keepdims=True) + l_near * scale
        a = dot3(*split2(e), kh[...], kl[...], NN)
        o = (dot3(*split2(a), v[0, p], v[1, p], NT) + st[p] * scale) / total
        att[p] = jnp.where(lowq, o[:CL], o[CL:])

    for copy in copies[:3]:
        copy.wait()
    for copy in copies[3:]:
        copy.start()

    def body(i, carry):
        one, two = scores(2 * i), scores(2 * i + 1)
        attend(2 * i, one)
        attend(2 * i + 1, two)
        return carry

    lax.fori_loop(0, NY // 2, body, 0)
    ah, al = split2(jnp.concatenate([att[p] for p in range(NY)], 1))
    for copy in copies[3:]:
        copy.wait()
    r = x[...] + dot3(ah, al, wo[0], wo[1], NT)
    mean = jnp.sum(r, axis=1, keepdims=True) * (1.0 / D)
    square = jnp.sum(r * r, axis=1, keepdims=True) * (1.0 / D)
    normed = (r - mean) * lax.rsqrt(square - mean * mean + 1e-05)
    hid = dot3(*split2(normed), u[0], u[1], NN)
    act = 0.5 * hid * (1.0 + lax.erf(hid * math.sqrt(0.5)))
    y = r + dot3(*split2(act), d[0], d[1], NN)
    out_ref[...] = y.T


def far_call(scalars, arrays):
    return pl.pallas_call(
        far_kernel,
        out_shape=sds(D, CL),
        in_specs=[sspec()] * len(scalars) + [vspec()] + [hspec()] * (len(arrays) - 1),
        out_specs=vspec(),
        scratch_shapes=[pltpu.VMEM((EK, D), BF), pltpu.VMEM((EK, D), BF), pltpu.VMEM((NY, CL, 2 * HD), F32)]
        + [pltpu.VMEM(a.shape, a.dtype) for a in arrays[1:]] + [pltpu.SemaphoreType.DMA((len(arrays) - 1,))],
        compiler_params=params(60),
        cost_estimate=cost(6 * 10**9, 16 << 20, 1 << 20),
        name="far",
    )(*scalars, *arrays)


def place_kernel(pos, r_ref, order_ref, out_ref):
    full = jnp.concatenate([r_ref[i * HD:(i + 1) * HD, :] for i in range(CD)], 1)
    order = jnp.concatenate([order_ref[i:i + 1, :] for i in range(CD)], 1) - pos[0]
    hi = full.astype(BF)
    rest = full - hi.astype(F32)
    mid = rest.astype(BF)
    low = (rest - mid.astype(F32)).astype(BF)
    parts = jnp.concatenate([hi, mid, low], 0)
    step = 256
    for j in range(CD * CL // step):
        nodes = lax.broadcasted_iota(jnp.int32, (step, CD * CL), 0) + j * step
        pick = jnp.where(nodes == order, 1.0, 0.0).astype(BF)
        t = mm(parts, pick, NT)
        out_ref[:, j * step:(j + 1) * step] = t[:HD] + (t[HD:2 * HD] + t[2 * HD:])


def place_call(pos, received, order):
    return pl.pallas_call(
        place_kernel,
        out_shape=sds(HD, CD * CL),
        in_specs=[sspec(), vspec(), vspec()],
        out_specs=vspec(),
        compiler_params=params(12),
        cost_estimate=cost(4 * 10**8, 1 << 20),
        name="place",
    )(pos, received, order)


def pick_kernel(group, pos, *refs):
    tables, srcs, outs = refs[:NX], refs[NX:-NX], refs[-NX:]
    z = pos[3]
    parts, at = [], 0
    for s in group:
        size = 2 if s == NZ // 2 else 1
        parts.append(srcs[at:at + size])
        at += size

    for k, out in enumerate(outs):
        for i, s in enumerate(group):
            src = parts[i]
            for j in range(CAP):
                b = tables[k][(k * NZ + lax.bitwise_and(z + s, NZ - 1)) * CAP + j]
                if len(src) == 1:
                    block = src[0][pl.ds(pl.multiple_of(b * PR, PR), PR), :]
                else:
                    at = pl.multiple_of(lax.bitwise_and(b, CD // 2 - 1) * PR, PR)
                    block = jnp.where(b < CD // 2, src[0][pl.ds(at, PR), :], src[1][pl.ds(at, PR), :])
                out[(i * CAP + j) * PR:(i * CAP + j + 1) * PR, :] = block


def pick_call(group, pos, tables, srcs):
    rows = len(group) * CAP * PR
    return pl.pallas_call(
        lambda *refs: pick_kernel(group, *refs),
        out_shape=[sds(rows, D)] * NX,
        in_specs=[sspec()] * (1 + NX) + [vspec()] * len(srcs),
        out_specs=[vspec()] * NX,
        compiler_params=params(8),
        cost_estimate=cost(0, NX * rows * D * 8),
        name="pick",
    )(pos, *tables, *srcs)


def send_kernel(row, *refs):
    srcs, out, held = refs[:-2], refs[-2], refs[-1]
    at = 0
    for src in srcs:
        held[at:at + src.shape[0], :] = src[...]
        at += src.shape[0]
    for i in range(CD * NE):
        out[i * PR:(i + 1) * PR, :] = held[pl.ds(pl.multiple_of(row[i], PR), PR), :]


def send_call(row, srcs):
    return pl.pallas_call(
        send_kernel,
        out_shape=sds(CD * NE * PR, D),
        in_specs=[sspec()] + [vspec()] * len(srcs),
        out_specs=vspec(),
        scratch_shapes=[pltpu.VMEM((NZ * NX * CAP * PR, D), F32)],
        compiler_params=params(12),
        cost_estimate=cost(0, 6 << 20),
        name="send",
    )(row, *srcs)


def ring(size, step):
    return [(i, (i + step) % size) for i in range(size)]


SWAP = [(0, 1), (1, 0)]


def shards(node_feats, order, node_count, local_blocks, exp_blocks, virt_blocks, virt_feats,
           w_query, w_key, w_value, w_out, w_up, w_down):
    z, x, y, c = (lax.axis_index(a) for a in ("z", "x", "y", "c"))
    head = y * NC + c
    pos = jnp.stack([(z * NX + x) * (CD * CL), head, c, z, x]).astype(jnp.int32)
    order = order.reshape(CD, CL)

    piece, edge = first_call(pos, order, node_feats)

    half = CL // 2
    tie = lax.optimization_barrier

    def both_z(a, b):
        return lax.ppermute(a, "z", ring(NZ, 1)), lax.ppermute(b, "z", ring(NZ, -1))

    def swap(*arrays):
        return [lax.ppermute(t, "c", SWAP) for t in arrays]

    up, down = both_z(piece, piece)
    table, row, w = setup_call(pos, exp_blocks, w_query.T, w_key.T, w_value.T, w_out.T, w_up, w_down)
    tables = [table] + [lax.ppermute(table, "x", ring(NX, -k)) for k in range(1, NX)]
    held = {0: (piece,), 7: (up,), 1: (down,)}
    up, down, w, edge, *tables = tie((up, down, w, edge, *tables))
    w = lax.all_gather(w, ("y", "c"), axis=0, tiled=True).reshape(CD, D, D)

    def pick(group):
        return pick_call(group, pos, tables, [t for s in group for t in held[s]])

    def exchange(blocks):
        return [blocks[0]] + [lax.ppermute(blocks[k], "x", ring(NX, k)) for k in (1, 2, 3)]

    one = pick(GROUPS[0])
    e_in = lax.ppermute(edge, ("z", "x", "y", "c"), [
        (i * CD + h, (i + s) * CD + h)
        for s, hs in ((1, (0, 1)), (-1, (6, 7)))
        for i in range(NZ * NX) if 0 <= i + s < NZ * NX for h in hs])
    up, down = both_z(up, down)
    held[6], held[2] = (up,), (down,)
    up, down, *_ = tie((up, down, *one))
    one = exchange(one)
    up, down = both_z(up, down)
    held[5], held[3] = (up,), (down,)
    up, down, e_in, *_ = tie((up, down, e_in, *one))
    held[4] = both_z(up[:half], down[half:])
    two = pick(GROUPS[1])
    (e_other,) = swap(tie((e_in, *two))[0])
    arrived = one + exchange(two)
    arrived = tie((e_other, *arrived))
    e_other, arrived = arrived[0], arrived[1:]

    sending = send_call(row, arrived)
    xe = lax.all_to_all(sending, ("y", "c"), 0, 0, tiled=True)

    _, w, pos_late = tie((sending, w, pos))
    x_own, q, wv, wo, state = near_call(
        (pos_late, local_blocks, virt_blocks, node_count), (order, node_feats, e_in, e_other, virt_feats, w))
    state, w = tie((state, w))
    wu, wd = prep_call(w)
    result = far_call((pos, exp_blocks, node_count), (xe, q, state, wv, x_own, wo, wu, wd))
    received = lax.all_to_all(result, ("y", "c"), 0, 0, tiled=True)
    return place_call(pos, received, order).T


def solution(mesh):
    grid = Mesh(mesh.devices.reshape(NZ, NX, NY, NC), ("z", "x", "y", "c"))
    dom, head = ("z", "x"), ("y", "c")
    return jax.shard_map(
        shards,
        mesh=grid,
        in_specs=(P(dom, None), P(dom), P(), P(dom, None), P(dom, None), P(dom), P(),
                  P(None, head), P(None, head), P(None, head), P(None, head), P(None, head),
                  P(head, None)),
        out_specs=P(dom, head),
        check_vma=False,
    )
```

```python
import math

import jax
import jax.numpy as jnp
from jax import lax
from jax.experimental import pallas as pl
from jax.experimental.pallas import tpu as pltpu
from jax.sharding import Mesh, PartitionSpec as P

D = 512
HD = 64
FF = 1024
CL = 128
CD = 8
NE = 6
NL = 3
CAP = 3
NZ, NX, NY, NC = 8, 4, 4, 2
PR = CL // (NY * NC)
EK = NE * CL
LK = (NL + 1) * CL
NEG = -1e30
VMEM_BYTES = 67043328
BF = jnp.bfloat16
F32 = jnp.float32
NT = (((1,), (1,)), ((), ()))
NN = (((1,), (0,)), ((), ()))

GROUPS = ((0, 1, 7), (2, 6, 3, 5, 4))


def split2(v):
    hi = v.astype(BF)
    return hi, (v - hi.astype(F32)).astype(BF)


def mm(a, b, dims):
    return lax.dot_general(a, b, dims, preferred_element_type=F32)


def dot3(ah, al, bh, bl, dims):
    return mm(ah, bh, dims) + (mm(ah, bl, dims) + mm(al, bh, dims))


def vspec():
    return pl.BlockSpec(memory_space=pltpu.VMEM)


def hspec():
    return pl.BlockSpec(memory_space=pltpu.HBM)


def sspec():
    return pl.BlockSpec(memory_space=pltpu.SMEM)


def params(mb):
    return pltpu.CompilerParams(vmem_limit_bytes=mb << 20)


def cost(flops, bytes_accessed, transcendentals=0):
    return pl.CostEstimate(flops=flops, bytes_accessed=bytes_accessed, transcendentals=transcendentals)


def sds(*shape, dtype=F32):
    return jax.ShapeDtypeStruct(shape, dtype)


def columns(row):
    return jnp.broadcast_to(row, (CL, CL)).T


def one_hot(cols):
    lanes = lax.broadcasted_iota(jnp.int32, cols.shape, 1).astype(F32)
    parts = [jnp.where(cols == lanes + float(j * CL), 1.0, 0.0).astype(BF) for j in range(CD)]
    return jnp.concatenate(parts, 1)


def first_kernel(pos, exp_ref, order_hbm, nodes_hbm, piece_out, edge_out, table, row,
                 order_ref, nodes, seen, starts, widths, sems):
    base, head, c = pos[0], pos[1], pos[2]
    step = 2 * CL
    parts = CD * CL // step
    fetch = [pltpu.make_async_copy(order_hbm, order_ref, sems.at[0])] + [
        pltpu.make_async_copy(nodes_hbm.at[i * step:(i + 1) * step, :], nodes.at[i * step:(i + 1) * step, :],
                              sems.at[i + 1]) for i in range(parts)]
    for copy in fetch:
        copy.start()
    z, x = pos[3], pos[4]
    start = 0
    for group in GROUPS:
        for p, s in enumerate(group):
            starts[s] = start + p * CAP
            widths[s] = len(group) * CAP
        start += NX * len(group) * CAP
    for i in range(NX * NZ * CAP):
        table[i] = 0
    for i in range(NZ * NX):
        seen[i] = 0

    def place(i, carry):
        for e in range(NE):
            block = exp_ref[i, e]
            owner = lax.shift_right_logical(block, 3)
            rank = seen[owner]
            seen[owner] = rank + 1
            oz = lax.shift_right_logical(owner, 2)
            back = lax.bitwise_and(x - lax.bitwise_and(owner, NX - 1), NX - 1)
            table[back * (NZ * CAP) + oz * CAP + rank] = lax.bitwise_and(block, CD - 1)
            off = lax.bitwise_and(oz - z, NZ - 1)
            row[i * NE + e] = (starts[off] + back * widths[off] + rank) * PR
        return carry

    lax.fori_loop(0, CD, place, 0)
    fetch[0].wait()
    order = (order_ref[...] - base).astype(F32)
    mine = pltpu.roll(order, lax.rem(CL - head * PR, CL), 1)
    col = jnp.concatenate([mine] + [jnp.zeros((CL - CD, CL), F32)], 0).T
    pieces = [jnp.broadcast_to(col[:PR, k:k + 1], (PR, CL)) for k in range(CD)]
    edge = jnp.where(head < NY, CD - NC + c, c)
    edge_row = (order_ref[pl.ds(edge, 1), :] - base).astype(F32)
    pick = one_hot(jnp.concatenate(pieces + [columns(edge_row)], 0))
    rows = jnp.zeros((2 * CL, D), F32)
    for i in range(parts):
        fetch[i + 1].wait()
        hi, lo = split2(nodes[i * step:(i + 1) * step, :])
        some = pick[:, i * step:(i + 1) * step]
        rows = rows + (mm(some, hi, NN) + mm(some, lo, NN))
    piece_out[...] = rows[:CL]
    edge_out[...] = rows[CL:]


def first_call(pos, exp_blocks, order, nodes):
    return pl.pallas_call(
        first_kernel,
        out_shape=[sds(CL, D), sds(CL, D), sds(NX * NZ * CAP, dtype=jnp.int32), sds(CD * NE, dtype=jnp.int32)],
        in_specs=[sspec(), sspec(), hspec(), hspec()],
        out_specs=[vspec()] * 2 + [sspec()] * 2,
        scratch_shapes=[pltpu.VMEM((CD, CL), jnp.int32), pltpu.VMEM((CD * CL, D), F32),
                        pltpu.SMEM((NZ * NX,), jnp.int32), pltpu.SMEM((NZ,), jnp.int32),
                        pltpu.SMEM((NZ,), jnp.int32), pltpu.SemaphoreType.DMA((5,))],
        compiler_params=params(60),
        cost_estimate=cost(10**9, 3 << 20),
        name="first",
    )(pos, exp_blocks, order, nodes)


def pack_kernel(q, k, v, o, up, down, out, sems):
    pairs = [(w, out.at[i * HD:(i + 1) * HD, :]) for i, w in enumerate((q, k, v, o))]
    pairs.append((down, out.at[2 * CL:3 * CL, :]))
    pairs += [(up.at[j * CL:(j + 1) * CL, :], out.at[3 * CL:, j * CL:(j + 1) * CL]) for j in range(4)]
    copies = [pltpu.make_async_copy(src, dst, sems.at[i]) for i, (src, dst) in enumerate(pairs)]
    for copy in copies:
        copy.start()
    for copy in copies:
        copy.wait()


def pack_call(*w):
    return pl.pallas_call(
        pack_kernel,
        out_shape=sds(D, D),
        in_specs=[hspec()] * 6,
        out_specs=vspec(),
        scratch_shapes=[pltpu.SemaphoreType.DMA((9,))],
        compiler_params=params(60),
        cost_estimate=cost(1000, 2 << 20),
        name="pack",
    )(*w)


def near_kernel(pos, local_ref, virt_ref, count_ref, order_ref, nodes_ref, e_in, e_other, virtual_ref, w_hbm,
                x_out, q_out, v_out, o_out, state, kh, kl, w, sem):
    fetch = pltpu.make_async_copy(w_hbm.at[:, :2 * CL, :], w, sem)
    fetch.start()
    base, head, c = pos[0], pos[1], pos[2]
    first = lax.shift_right_logical(base, 7)

    def order_row(r):
        return columns((order_ref[pl.ds(r, 1), :] - base).astype(F32))

    rel = [local_ref[head, j] - first for j in range(NL)]
    rows = [order_row(jnp.clip(r, 0, CD - 1)) for r in rel] + [order_row(head)]
    pick = one_hot(jnp.concatenate(rows, 0))
    nodes = nodes_ref[...]
    hi, lo = split2(nodes)
    got = mm(pick, hi, NN) + mm(pick, lo, NN)
    last = (nodes - hi.astype(F32) - lo.astype(F32)).astype(BF)
    x = got[NL * CL:] + mm(pick[NL * CL:], last, NN)
    x_out[...] = x
    lane = lax.broadcasted_iota(jnp.int32, (1, CL), 1)
    bias = []
    for j in range(NL):
        r = rel[j]
        at = jnp.where(r < 0, r + NC, r - CD)
        edge = jnp.where(at == c, e_in[...], e_other[...])
        keys = jnp.where((r >= 0) & (r < CD), got[j * CL:(j + 1) * CL], edge)
        kh[j * CL:(j + 1) * CL, :], kl[j * CL:(j + 1) * CL, :] = split2(keys)
        bias.append(jnp.where(lane < count_ref[local_ref[head, j]], 0.0, NEG))
    vat = pl.multiple_of(virt_ref[head] * CL, CL)
    kh[NL * CL:, :], kl[NL * CL:, :] = split2(virtual_ref[pl.ds(vat, CL), :])
    bias = jnp.concatenate(bias + [jnp.zeros((1, CL), F32)], 1)

    lanes = lax.broadcasted_iota(jnp.int32, (CL, 2 * HD), 1)
    lowq = lanes < HD
    xh, xl = split2(x)
    fetch.wait()
    for at in range(NY):
        left, right = w[2 * at], w[2 * at + 1]
        wq, wk, wv, wo = (
            split2(jnp.concatenate([left[i * HD:(i + 1) * HD], right[i * HD:(i + 1) * HD]], 0))
            for i in range(4))
        q = dot3(xh, xl, *wq, NT) * (1.0 / math.sqrt(HD))
        both = jnp.concatenate([jnp.where(lowq, q, 0.0), jnp.where(lowq, 0.0, q)], 0)
        q_out[0, at], q_out[1, at] = split2(dot3(*split2(both), *wk, NN))
        v_out[0, at], v_out[1, at] = wv
        rows = slice(at * CL, (at + 1) * CL)
        o_out[0, rows, :], o_out[1, rows, :] = wo

    def body(p, carry):
        s = dot3(q_out[0, p], q_out[1, p], kh[...], kl[...], NT) + bias
        m = jnp.max(s, axis=1, keepdims=True)
        e = jnp.exp(s - m)
        l = jnp.sum(e, axis=1, keepdims=True)
        a = dot3(*split2(e), kh[...], kl[...], NN)
        o = dot3(*split2(a), v_out[0, p], v_out[1, p], NT)
        state[p, :CL, :] = jnp.where(lowq, o[:CL], jnp.where(lanes < HD + HD // 2, m[:CL], l[:CL]))
        state[p, CL:, :] = jnp.where(lowq, jnp.where(lanes < HD // 2, m[CL:], l[CL:]), o[CL:])
        return carry

    lax.fori_loop(0, NY, body, 0)


def near_call(scalars, arrays):
    shapes = [
        sds(CL, D), sds(2, NY, 2 * CL, D, dtype=BF), sds(2, NY, 2 * HD, D, dtype=BF),
        sds(2, D, D, dtype=BF), sds(NY, 2 * CL, 2 * HD),
    ]
    return pl.pallas_call(
        near_kernel,
        out_shape=shapes,
        in_specs=[sspec()] * len(scalars) + [vspec()] * (len(arrays) - 1) + [hspec()],
        out_specs=[vspec()] * len(shapes),
        scratch_shapes=[pltpu.VMEM((LK, D), BF), pltpu.VMEM((LK, D), BF), pltpu.VMEM((CD, 2 * CL, D), F32),
                        pltpu.SemaphoreType.DMA],
        compiler_params=params(60),
        cost_estimate=cost(6 * 10**9, 16 << 20, 1 << 20),
        name="near",
    )(*scalars, *arrays)


def prep_kernel(w_hbm, u_out, d_out, w, sems):
    fetch = [pltpu.make_async_copy(w_hbm.at[i, 2 * CL:, :], w.at[i], sems.at[i]) for i in range(CD)]
    for copy in fetch:
        copy.start()
    for i in range(CD):
        fetch[i].wait()
        rows = slice(i * CL, (i + 1) * CL)
        d_out[0, rows, :], d_out[1, rows, :] = split2(w[i, :CL, :])
        hi, lo = split2(w[i, CL:, :])
        for j in range(4):
            cols = slice(j * CL, (j + 1) * CL)
            u_out[0, cols, rows] = hi[:, cols]
            u_out[1, cols, rows] = lo[:, cols]


def prep_call(weights):
    return pl.pallas_call(
        prep_kernel,
        out_shape=[sds(2, D, FF, dtype=BF), sds(2, FF, D, dtype=BF)],
        in_specs=[hspec()],
        out_specs=[vspec()] * 2,
        scratch_shapes=[pltpu.VMEM((CD, 2 * CL, D), F32), pltpu.SemaphoreType.DMA((CD,))],
        compiler_params=params(60),
        cost_estimate=cost(10**7, 8 << 20),
        name="prep",
    )(weights)


def far_kernel(pos, exp_ref, count_ref, xe_ref, q_hbm, s_hbm, v_hbm, x_hbm, o_hbm, u_hbm, d_hbm,
               out_ref, kh, kl, att, q, st, v, x, wo, u, d, sems):
    first = [pltpu.make_async_copy(q_hbm.at[:, p], q.at[:, p], sems.at[p]) for p in range(NY)]
    later = [pltpu.make_async_copy(src, dst, sems.at[NY + i]) for i, (src, dst) in enumerate(zip(
        (s_hbm, v_hbm, x_hbm, o_hbm, u_hbm, d_hbm), (st, v, x, wo, u, d)))]
    for copy in first:
        copy.start()
    head = pos[1]
    hi, lo = split2(xe_ref[...])
    kh[...] = hi
    kl[...] = lo
    lowq = lax.broadcasted_iota(jnp.int32, (CL, 2 * HD), 1) < HD
    n = lax.broadcasted_iota(jnp.int32, (1, EK), 1)

    def steps(v, width, count):
        return sum(jnp.where(v >= width * k, 1, 0) for k in range(1, count))

    piece = steps(n, NE * PR, CD)
    r = n - piece * (NE * PR)
    entry = steps(r, PR, NE)
    slot = piece * PR + r - entry * PR
    bias = jnp.zeros((1, EK), F32)
    for e in range(NE):
        bad = (entry == e) & (slot >= count_ref[exp_ref[head, e]])
        bias = jnp.where(bad, NEG, bias)

    def scores(p):
        return dot3(q[0, p], q[1, p], kh[...], kl[...], NT) + bias

    def attend(p, s):
        m_near = jnp.concatenate([st[p, :CL, HD:HD + 1], st[p, CL:, :1]], 0)
        half = HD // 2
        l_near = jnp.concatenate([st[p, :CL, HD + half:HD + half + 1], st[p, CL:, half:half + 1]], 0)
        m = jnp.maximum(m_near, jnp.max(s, axis=1, keepdims=True))
        e = jnp.exp(s - m)
        scale = jnp.exp(m_near - m)
        total = jnp.sum(e, axis=1, keepdims=True) + l_near * scale
        a = dot3(*split2(e), kh[...], kl[...], NN)
        o = (dot3(*split2(a), v[0, p], v[1, p], NT) + st[p] * scale) / total
        att[p] = jnp.where(lowq, o[:CL], o[CL:])

    first[0].wait()
    ahead = scores(0)
    for copy in later:
        copy.start()
    for p in range(NY):
        s = ahead
        if p + 1 < NY:
            first[p + 1].wait()
            ahead = scores(p + 1)
        if p == 0:
            later[0].wait()
            later[1].wait()
        attend(p, s)

    ah, al = split2(jnp.concatenate([att[p] for p in range(NY)], 1))
    for copy in later[2:]:
        copy.wait()
    r = x[...] + dot3(ah, al, wo[0], wo[1], NT)
    mean = jnp.sum(r, axis=1, keepdims=True) * (1.0 / D)
    square = jnp.sum(r * r, axis=1, keepdims=True) * (1.0 / D)
    normed = (r - mean) * lax.rsqrt(square - mean * mean + 1e-05)
    hid = dot3(*split2(normed), u[0], u[1], NN)
    act = 0.5 * hid * (1.0 + lax.erf(hid * math.sqrt(0.5)))
    y = r + dot3(*split2(act), d[0], d[1], NN)
    out_ref[...] = y.T


def far_call(scalars, arrays):
    return pl.pallas_call(
        far_kernel,
        out_shape=sds(D, CL),
        in_specs=[sspec()] * len(scalars) + [vspec()] + [hspec()] * (len(arrays) - 1),
        out_specs=vspec(),
        scratch_shapes=[pltpu.VMEM((EK, D), BF), pltpu.VMEM((EK, D), BF), pltpu.VMEM((NY, CL, 2 * HD), F32)]
        + [pltpu.VMEM(a.shape, a.dtype) for a in arrays[1:]] + [pltpu.SemaphoreType.DMA((NY + len(arrays) - 2,))],
        compiler_params=params(50),
        cost_estimate=cost(6 * 10**9, 16 << 20, 1 << 20),
        name="far",
    )(*scalars, *arrays)


def place_kernel(pos, r_ref, order_ref, out_ref):
    full = jnp.concatenate([r_ref[i * HD:(i + 1) * HD, :] for i in range(CD)], 1)
    order = jnp.concatenate([order_ref[i:i + 1, :] for i in range(CD)], 1) - pos[0]
    hi = full.astype(BF)
    rest = full - hi.astype(F32)
    mid = rest.astype(BF)
    low = (rest - mid.astype(F32)).astype(BF)
    parts = jnp.concatenate([hi, mid, low], 0)
    step = 256
    for j in range(CD * CL // step):
        nodes = lax.broadcasted_iota(jnp.int32, (step, CD * CL), 0) + j * step
        pick = jnp.where(nodes == order, 1.0, 0.0).astype(BF)
        t = mm(parts, pick, NT)
        out_ref[:, j * step:(j + 1) * step] = t[:HD] + (t[HD:2 * HD] + t[2 * HD:])


def place_call(pos, received, order):
    return pl.pallas_call(
        place_kernel,
        out_shape=sds(HD, CD * CL),
        in_specs=[sspec(), vspec(), vspec()],
        out_specs=vspec(),
        compiler_params=params(12),
        cost_estimate=cost(4 * 10**8, 1 << 20),
        name="place",
    )(pos, received, order)


def pick_kernel(group, pos, *refs):
    tables, srcs, outs = refs[:NX], refs[NX:-NX], refs[-NX:]
    z = pos[3]
    parts, at = [], 0
    for s in group:
        size = 2 if s == NZ // 2 else 1
        parts.append(srcs[at:at + size])
        at += size

    for k, out in enumerate(outs):
        for i, s in enumerate(group):
            src = parts[i]
            for j in range(CAP):
                b = tables[k][(k * NZ + lax.bitwise_and(z + s, NZ - 1)) * CAP + j]
                if len(src) == 1:
                    block = src[0][pl.ds(pl.multiple_of(b * PR, PR), PR), :]
                else:
                    at = pl.multiple_of(lax.bitwise_and(b, CD // 2 - 1) * PR, PR)
                    block = jnp.where(b < CD // 2, src[0][pl.ds(at, PR), :], src[1][pl.ds(at, PR), :])
                out[(i * CAP + j) * PR:(i * CAP + j + 1) * PR, :] = block


def pick_call(group, pos, tables, srcs):
    rows = len(group) * CAP * PR
    return pl.pallas_call(
        lambda *refs: pick_kernel(group, *refs),
        out_shape=[sds(rows, D)] * NX,
        in_specs=[sspec()] * (1 + NX) + [vspec()] * len(srcs),
        out_specs=[vspec()] * NX,
        compiler_params=params(8),
        cost_estimate=cost(0, NX * rows * D * 8),
        name="pick",
    )(pos, *tables, *srcs)


def send_kernel(row, *refs):
    srcs, out, held = refs[:-2], refs[-2], refs[-1]
    at = 0
    for src in srcs:
        held[at:at + src.shape[0], :] = src[...]
        at += src.shape[0]
    for i in range(CD * NE):
        out[i * PR:(i + 1) * PR, :] = held[pl.ds(pl.multiple_of(row[i], PR), PR), :]


def send_call(row, srcs):
    return pl.pallas_call(
        send_kernel,
        out_shape=sds(CD * NE * PR, D),
        in_specs=[sspec()] + [vspec()] * len(srcs),
        out_specs=vspec(),
        scratch_shapes=[pltpu.VMEM((NZ * NX * CAP * PR, D), F32)],
        compiler_params=params(12),
        cost_estimate=cost(0, 6 << 20),
        name="send",
    )(row, *srcs)


def ring(size, step):
    return [(i, (i + step) % size) for i in range(size)]


SWAP = [(0, 1), (1, 0)]


def shards(node_feats, order, node_count, local_blocks, exp_blocks, virt_blocks, virt_feats,
           w_query, w_key, w_value, w_out, w_up, w_down):
    z, x, y, c = (lax.axis_index(a) for a in ("z", "x", "y", "c"))
    head = y * NC + c
    pos = jnp.stack([(z * NX + x) * (CD * CL), head, c, z, x]).astype(jnp.int32)
    order = order.reshape(CD, CL)

    piece, edge, table, row = first_call(pos, exp_blocks, order, node_feats)

    half = CL // 2
    tie = lax.optimization_barrier

    def both_z(a, b):
        return lax.ppermute(a, "z", ring(NZ, 1)), lax.ppermute(b, "z", ring(NZ, -1))

    def swap(*arrays):
        return [lax.ppermute(t, "c", SWAP) for t in arrays]

    up, down = both_z(piece, piece)
    w = pack_call(w_query.T, w_key.T, w_value.T, w_out.T, w_up, w_down)
    tables = [table] + [lax.ppermute(table, "x", ring(NX, -k)) for k in range(1, NX)]
    held = {0: (piece,), 7: (up,), 1: (down,)}
    up, down, w, edge, *tables = tie((up, down, w, edge, *tables))
    w = lax.all_gather(w, ("y", "c"), axis=0, tiled=True).reshape(CD, D, D)

    def pick(group):
        return pick_call(group, pos, tables, [t for s in group for t in held[s]])

    def exchange(blocks):
        return [blocks[0]] + [lax.ppermute(blocks[k], "x", ring(NX, k)) for k in (1, 2, 3)]

    one = pick(GROUPS[0])
    e_in = lax.ppermute(edge, ("z", "x", "y", "c"), [
        (i * CD + h, (i + s) * CD + h)
        for s, hs in ((1, (0, 1)), (-1, (6, 7)))
        for i in range(NZ * NX) if 0 <= i + s < NZ * NX for h in hs])
    up, down = both_z(up, down)
    held[6], held[2] = (up,), (down,)
    up, down, *_ = tie((up, down, *one))
    one = exchange(one)
    up, down = both_z(up, down)
    held[5], held[3] = (up,), (down,)
    up, down, e_in, *_ = tie((up, down, e_in, *one))
    held[4] = both_z(up[:half], down[half:])
    two = pick(GROUPS[1])
    (e_other,) = swap(tie((e_in, *two))[0])
    arrived = one + exchange(two)
    arrived = tie((e_other, *arrived))
    e_other, arrived = arrived[0], arrived[1:]

    sending = send_call(row, arrived)
    xe = lax.all_to_all(sending, ("y", "c"), 0, 0, tiled=True)

    _, w, pos_late = tie((sending, w, pos))
    x_own, q, wv, wo, state = near_call(
        (pos_late, local_blocks, virt_blocks, node_count), (order, node_feats, e_in, e_other, virt_feats, w))
    state, w = tie((state, w))
    wu, wd = prep_call(w)
    result = far_call((pos, exp_blocks, node_count), (xe, q, state, wv, x_own, wo, wu, wd))
    received = lax.all_to_all(result, ("y", "c"), 0, 0, tiled=True)
    return place_call(pos, received, order).T


def solution(mesh):
    grid = Mesh(mesh.devices.reshape(NZ, NX, NY, NC), ("z", "x", "y", "c"))
    dom, head = ("z", "x"), ("y", "c")
    return jax.shard_map(
        shards,
        mesh=grid,
        in_specs=(P(dom, None), P(dom), P(), P(dom, None), P(dom, None), P(dom), P(),
                  P(None, head), P(None, head), P(None, head), P(None, head), P(None, head),
                  P(head, None)),
        out_specs=P(dom, head),
        check_vma=False,
    )
```

```python
import math

import jax
import jax.numpy as jnp
from jax import lax
from jax.experimental import pallas as pl
from jax.experimental.pallas import tpu as pltpu
from jax.sharding import Mesh, PartitionSpec as P

D = 512
HD = 64
FF = 1024
CL = 128
CD = 8
NE = 6
NL = 3
CAP = 3
NZ, NX, NY, NC = 8, 4, 4, 2
PR = CL // (NY * NC)
EK = NE * CL
LK = (NL + 1) * CL
NEG = -1e30
VMEM_BYTES = 67043328
BF = jnp.bfloat16
F32 = jnp.float32
NT = (((1,), (1,)), ((), ()))
NN = (((1,), (0,)), ((), ()))

GROUPS = ((0, 1, 7), (2, 6), (3, 5, 4))


def split2(v):
    hi = v.astype(BF)
    return hi, (v - hi.astype(F32)).astype(BF)


def mm(a, b, dims):
    return lax.dot_general(a, b, dims, preferred_element_type=F32)


def dot3(ah, al, bh, bl, dims):
    return mm(ah, bh, dims) + (mm(ah, bl, dims) + mm(al, bh, dims))


def vspec():
    return pl.BlockSpec(memory_space=pltpu.VMEM)


def hspec():
    return pl.BlockSpec(memory_space=pltpu.HBM)


def sspec():
    return pl.BlockSpec(memory_space=pltpu.SMEM)


def params(mb):
    return pltpu.CompilerParams(vmem_limit_bytes=mb << 20)


def cost(flops, bytes_accessed, transcendentals=0):
    return pl.CostEstimate(flops=flops, bytes_accessed=bytes_accessed, transcendentals=transcendentals)


def sds(*shape, dtype=F32):
    return jax.ShapeDtypeStruct(shape, dtype)


def columns(row):
    return jnp.broadcast_to(row, (CL, CL)).T


def one_hot(cols):
    lanes = lax.broadcasted_iota(jnp.int32, cols.shape, 1).astype(F32)
    parts = [jnp.where(cols == lanes + float(j * CL), 1.0, 0.0).astype(BF) for j in range(CD)]
    return jnp.concatenate(parts, 1)


def first_kernel(pos, exp_ref, order_hbm, nodes_hbm, piece_out, edge_out, table, row,
                 order_ref, nodes, seen, starts, widths, sems):
    base, head, c = pos[0], pos[1], pos[2]
    step = 2 * CL
    parts = CD * CL // step
    fetch = [pltpu.make_async_copy(order_hbm, order_ref, sems.at[0])] + [
        pltpu.make_async_copy(nodes_hbm.at[i * step:(i + 1) * step, :], nodes.at[i * step:(i + 1) * step, :],
                              sems.at[i + 1]) for i in range(parts)]
    for copy in fetch:
        copy.start()
    z, x = pos[3], pos[4]
    start = 0
    for group in GROUPS:
        for p, s in enumerate(group):
            starts[s] = start + p * CAP
            widths[s] = len(group) * CAP
        start += NX * len(group) * CAP
    for i in range(NX * NZ * CAP):
        table[i] = 0
    for i in range(NZ * NX):
        seen[i] = 0

    def place(i, carry):
        for e in range(NE):
            block = exp_ref[i, e]
            owner = lax.shift_right_logical(block, 3)
            rank = seen[owner]
            seen[owner] = rank + 1
            oz = lax.shift_right_logical(owner, 2)
            back = lax.bitwise_and(x - lax.bitwise_and(owner, NX - 1), NX - 1)
            table[back * (NZ * CAP) + oz * CAP + rank] = lax.bitwise_and(block, CD - 1)
            off = lax.bitwise_and(oz - z, NZ - 1)
            row[i * NE + e] = (starts[off] + back * widths[off] + rank) * PR
        return carry

    lax.fori_loop(0, CD, place, 0)
    fetch[0].wait()
    order = (order_ref[...] - base).astype(F32)
    mine = pltpu.roll(order, lax.rem(CL - head * PR, CL), 1)
    col = jnp.concatenate([mine] + [jnp.zeros((CL - CD, CL), F32)], 0).T
    pieces = [jnp.broadcast_to(col[:PR, k:k + 1], (PR, CL)) for k in range(CD)]
    edge = jnp.where(head < NY, CD - NC + c, c)
    edge_row = (order_ref[pl.ds(edge, 1), :] - base).astype(F32)
    pick = one_hot(jnp.concatenate(pieces + [columns(edge_row)], 0))
    rows = jnp.zeros((2 * CL, D), F32)
    for i in range(parts):
        fetch[i + 1].wait()
        hi, lo = split2(nodes[i * step:(i + 1) * step, :])
        some = pick[:, i * step:(i + 1) * step]
        rows = rows + (mm(some, hi, NN) + mm(some, lo, NN))
    piece_out[...] = rows[:CL]
    edge_out[...] = rows[CL:]


def first_call(pos, exp_blocks, order, nodes):
    return pl.pallas_call(
        first_kernel,
        out_shape=[sds(CL, D), sds(CL, D), sds(NX * NZ * CAP, dtype=jnp.int32), sds(CD * NE, dtype=jnp.int32)],
        in_specs=[sspec(), sspec(), hspec(), hspec()],
        out_specs=[vspec()] * 2 + [sspec()] * 2,
        scratch_shapes=[pltpu.VMEM((CD, CL), jnp.int32), pltpu.VMEM((CD * CL, D), F32),
                        pltpu.SMEM((NZ * NX,), jnp.int32), pltpu.SMEM((NZ,), jnp.int32),
                        pltpu.SMEM((NZ,), jnp.int32), pltpu.SemaphoreType.DMA((5,))],
        compiler_params=params(60),
        cost_estimate=cost(10**9, 3 << 20),
        name="first",
    )(pos, exp_blocks, order, nodes)


def pack_kernel(q, k, v, o, up, down, out, sems):
    pairs = [(w, out.at[i * HD:(i + 1) * HD, :]) for i, w in enumerate((q, k, v, o))]
    pairs.append((down, out.at[2 * CL:3 * CL, :]))
    pairs += [(up.at[j * CL:(j + 1) * CL, :], out.at[3 * CL:, j * CL:(j + 1) * CL]) for j in range(4)]
    copies = [pltpu.make_async_copy(src, dst, sems.at[i]) for i, (src, dst) in enumerate(pairs)]
    for copy in copies:
        copy.start()
    for copy in copies:
        copy.wait()


def pack_call(*w):
    return pl.pallas_call(
        pack_kernel,
        out_shape=sds(D, D),
        in_specs=[hspec()] * 6,
        out_specs=vspec(),
        scratch_shapes=[pltpu.SemaphoreType.DMA((9,))],
        compiler_params=params(60),
        cost_estimate=cost(1000, 2 << 20),
        name="pack",
    )(*w)


def near_kernel(pos, local_ref, virt_ref, count_ref, order_ref, nodes_ref, e_in, e_other, virtual_ref, w_hbm,
                x_out, q_out, v_out, o_out, state, kh, kl, w, sem):
    fetch = pltpu.make_async_copy(w_hbm.at[:, :2 * CL, :], w, sem)
    fetch.start()
    base, head, c = pos[0], pos[1], pos[2]
    first = lax.shift_right_logical(base, 7)

    def order_row(r):
        return columns((order_ref[pl.ds(r, 1), :] - base).astype(F32))

    rel = [local_ref[head, j] - first for j in range(NL)]
    rows = [order_row(jnp.clip(r, 0, CD - 1)) for r in rel] + [order_row(head)]
    pick = one_hot(jnp.concatenate(rows, 0))
    nodes = nodes_ref[...]
    hi, lo = split2(nodes)
    got = mm(pick, hi, NN) + mm(pick, lo, NN)
    last = (nodes - hi.astype(F32) - lo.astype(F32)).astype(BF)
    x = got[NL * CL:] + mm(pick[NL * CL:], last, NN)
    x_out[...] = x
    lane = lax.broadcasted_iota(jnp.int32, (1, CL), 1)
    bias = []
    for j in range(NL):
        r = rel[j]
        at = jnp.where(r < 0, r + NC, r - CD)
        edge = jnp.where(at == c, e_in[...], e_other[...])
        keys = jnp.where((r >= 0) & (r < CD), got[j * CL:(j + 1) * CL], edge)
        kh[j * CL:(j + 1) * CL, :], kl[j * CL:(j + 1) * CL, :] = split2(keys)
        bias.append(jnp.where(lane < count_ref[local_ref[head, j]], 0.0, NEG))
    vat = pl.multiple_of(virt_ref[head] * CL, CL)
    kh[NL * CL:, :], kl[NL * CL:, :] = split2(virtual_ref[pl.ds(vat, CL), :])
    bias = jnp.concatenate(bias + [jnp.zeros((1, CL), F32)], 1)

    lanes = lax.broadcasted_iota(jnp.int32, (CL, 2 * HD), 1)
    lowq = lanes < HD
    xh, xl = split2(x)
    fetch.wait()
    for at in range(NY):
        left, right = w[2 * at], w[2 * at + 1]
        wq, wk, wv, wo = (
            split2(jnp.concatenate([left[i * HD:(i + 1) * HD], right[i * HD:(i + 1) * HD]], 0))
            for i in range(4))
        q = dot3(xh, xl, *wq, NT) * (1.0 / math.sqrt(HD))
        both = jnp.concatenate([jnp.where(lowq, q, 0.0), jnp.where(lowq, 0.0, q)], 0)
        q_out[0, at], q_out[1, at] = split2(dot3(*split2(both), *wk, NN))
        v_out[0, at], v_out[1, at] = wv
        rows = slice(at * CL, (at + 1) * CL)
        o_out[0, rows, :], o_out[1, rows, :] = wo

    def body(p, carry):
        s = dot3(q_out[0, p], q_out[1, p], kh[...], kl[...], NT) + bias
        m = jnp.max(s, axis=1, keepdims=True)
        e = jnp.exp(s - m)
        l = jnp.sum(e, axis=1, keepdims=True)
        a = dot3(*split2(e), kh[...], kl[...], NN)
        o = dot3(*split2(a), v_out[0, p], v_out[1, p], NT)
        state[p, :CL, :] = jnp.where(lowq, o[:CL], jnp.where(lanes < HD + HD // 2, m[:CL], l[:CL]))
        state[p, CL:, :] = jnp.where(lowq, jnp.where(lanes < HD // 2, m[CL:], l[CL:]), o[CL:])
        return carry

    lax.fori_loop(0, NY, body, 0)


def near_call(scalars, arrays):
    shapes = [
        sds(CL, D), sds(2, NY, 2 * CL, D, dtype=BF), sds(2, NY, 2 * HD, D, dtype=BF),
        sds(2, D, D, dtype=BF), sds(NY, 2 * CL, 2 * HD),
    ]
    return pl.pallas_call(
        near_kernel,
        out_shape=shapes,
        in_specs=[sspec()] * len(scalars) + [vspec()] * (len(arrays) - 1) + [hspec()],
        out_specs=[vspec()] * len(shapes),
        scratch_shapes=[pltpu.VMEM((LK, D), BF), pltpu.VMEM((LK, D), BF), pltpu.VMEM((CD, 2 * CL, D), F32),
                        pltpu.SemaphoreType.DMA],
        compiler_params=params(60),
        cost_estimate=cost(6 * 10**9, 16 << 20, 1 << 20),
        name="near",
    )(*scalars, *arrays)


def prep_kernel(w_hbm, u_out, d_out, w, sems):
    fetch = [pltpu.make_async_copy(w_hbm.at[i, 2 * CL:, :], w.at[i], sems.at[i]) for i in range(CD)]
    for copy in fetch:
        copy.start()
    for i in range(CD):
        fetch[i].wait()
        rows = slice(i * CL, (i + 1) * CL)
        d_out[0, rows, :], d_out[1, rows, :] = split2(w[i, :CL, :])
        hi, lo = split2(w[i, CL:, :])
        for j in range(4):
            cols = slice(j * CL, (j + 1) * CL)
            u_out[0, cols, rows] = hi[:, cols]
            u_out[1, cols, rows] = lo[:, cols]


def prep_call(weights):
    return pl.pallas_call(
        prep_kernel,
        out_shape=[sds(2, D, FF, dtype=BF), sds(2, FF, D, dtype=BF)],
        in_specs=[hspec()],
        out_specs=[vspec()] * 2,
        scratch_shapes=[pltpu.VMEM((CD, 2 * CL, D), F32), pltpu.SemaphoreType.DMA((CD,))],
        compiler_params=params(60),
        cost_estimate=cost(10**7, 8 << 20),
        name="prep",
    )(weights)


def far_kernel(pos, exp_ref, count_ref, xe_ref, q_hbm, s_hbm, v_hbm, x_hbm, o_hbm, u_hbm, d_hbm,
               out_ref, kh, kl, att, q, st, v, x, wo, u, d, sems):
    first = [pltpu.make_async_copy(q_hbm.at[:, p], q.at[:, p], sems.at[p]) for p in range(NY)]
    later = [pltpu.make_async_copy(src, dst, sems.at[NY + i]) for i, (src, dst) in enumerate(zip(
        (s_hbm, v_hbm, x_hbm, o_hbm, u_hbm, d_hbm), (st, v, x, wo, u, d)))]
    for copy in first:
        copy.start()
    head = pos[1]
    hi, lo = split2(xe_ref[...])
    kh[...] = hi
    kl[...] = lo
    lowq = lax.broadcasted_iota(jnp.int32, (CL, 2 * HD), 1) < HD
    n = lax.broadcasted_iota(jnp.int32, (1, EK), 1)

    def steps(v, width, count):
        return sum(jnp.where(v >= width * k, 1, 0) for k in range(1, count))

    piece = steps(n, NE * PR, CD)
    r = n - piece * (NE * PR)
    entry = steps(r, PR, NE)
    slot = piece * PR + r - entry * PR
    bias = jnp.zeros((1, EK), F32)
    for e in range(NE):
        bad = (entry == e) & (slot >= count_ref[exp_ref[head, e]])
        bias = jnp.where(bad, NEG, bias)

    def scores(p):
        return dot3(q[0, p], q[1, p], kh[...], kl[...], NT) + bias

    def attend(p, s):
        m_near = jnp.concatenate([st[p, :CL, HD:HD + 1], st[p, CL:, :1]], 0)
        half = HD // 2
        l_near = jnp.concatenate([st[p, :CL, HD + half:HD + half + 1], st[p, CL:, half:half + 1]], 0)
        m = jnp.maximum(m_near, jnp.max(s, axis=1, keepdims=True))
        e = jnp.exp(s - m)
        scale = jnp.exp(m_near - m)
        total = jnp.sum(e, axis=1, keepdims=True) + l_near * scale
        a = dot3(*split2(e), kh[...], kl[...], NN)
        o = (dot3(*split2(a), v[0, p], v[1, p], NT) + st[p] * scale) / total
        att[p] = jnp.where(lowq, o[:CL], o[CL:])

    for copy in first:
        copy.wait()
    for copy in later:
        copy.start()
    later[0].wait()
    later[1].wait()

    def body(i, carry):
        one, two = scores(2 * i), scores(2 * i + 1)
        attend(2 * i, one)
        attend(2 * i + 1, two)
        return carry

    lax.fori_loop(0, NY // 2, body, 0)
    ah, al = split2(jnp.concatenate([att[p] for p in range(NY)], 1))
    for copy in later[2:]:
        copy.wait()
    r = x[...] + dot3(ah, al, wo[0], wo[1], NT)
    mean = jnp.sum(r, axis=1, keepdims=True) * (1.0 / D)
    square = jnp.sum(r * r, axis=1, keepdims=True) * (1.0 / D)
    normed = (r - mean) * lax.rsqrt(square - mean * mean + 1e-05)
    hid = dot3(*split2(normed), u[0], u[1], NN)
    act = 0.5 * hid * (1.0 + lax.erf(hid * math.sqrt(0.5)))
    y = r + dot3(*split2(act), d[0], d[1], NN)
    out_ref[...] = y.T


def far_call(scalars, arrays):
    return pl.pallas_call(
        far_kernel,
        out_shape=sds(D, CL),
        in_specs=[sspec()] * len(scalars) + [vspec()] + [hspec()] * (len(arrays) - 1),
        out_specs=vspec(),
        scratch_shapes=[pltpu.VMEM((EK, D), BF), pltpu.VMEM((EK, D), BF), pltpu.VMEM((NY, CL, 2 * HD), F32)]
        + [pltpu.VMEM(a.shape, a.dtype) for a in arrays[1:]] + [pltpu.SemaphoreType.DMA((NY + len(arrays) - 2,))],
        compiler_params=params(50),
        cost_estimate=cost(6 * 10**9, 16 << 20, 1 << 20),
        name="far",
    )(*scalars, *arrays)


def place_kernel(pos, r_ref, order_ref, out_ref):
    full = jnp.concatenate([r_ref[i * HD:(i + 1) * HD, :] for i in range(CD)], 1)
    order = jnp.concatenate([order_ref[i:i + 1, :] for i in range(CD)], 1) - pos[0]
    hi = full.astype(BF)
    rest = full - hi.astype(F32)
    mid = rest.astype(BF)
    low = (rest - mid.astype(F32)).astype(BF)
    parts = jnp.concatenate([hi, mid, low], 0)
    step = 256
    for j in range(CD * CL // step):
        nodes = lax.broadcasted_iota(jnp.int32, (step, CD * CL), 0) + j * step
        pick = jnp.where(nodes == order, 1.0, 0.0).astype(BF)
        t = mm(parts, pick, NT)
        out_ref[:, j * step:(j + 1) * step] = t[:HD] + (t[HD:2 * HD] + t[2 * HD:])


def place_call(pos, received, order):
    return pl.pallas_call(
        place_kernel,
        out_shape=sds(HD, CD * CL),
        in_specs=[sspec(), vspec(), vspec()],
        out_specs=vspec(),
        compiler_params=params(12),
        cost_estimate=cost(4 * 10**8, 1 << 20),
        name="place",
    )(pos, received, order)


def pick_kernel(group, pos, *refs):
    tables, srcs, outs = refs[:NX], refs[NX:-NX], refs[-NX:]
    z = pos[3]
    parts, at = [], 0
    for s in group:
        size = 2 if s == NZ // 2 else 1
        parts.append(srcs[at:at + size])
        at += size

    for k, out in enumerate(outs):
        for i, s in enumerate(group):
            src = parts[i]
            for j in range(CAP):
                b = tables[k][(k * NZ + lax.bitwise_and(z + s, NZ - 1)) * CAP + j]
                if len(src) == 1:
                    block = src[0][pl.ds(pl.multiple_of(b * PR, PR), PR), :]
                else:
                    at = pl.multiple_of(lax.bitwise_and(b, CD // 2 - 1) * PR, PR)
                    block = jnp.where(b < CD // 2, src[0][pl.ds(at, PR), :], src[1][pl.ds(at, PR), :])
                out[(i * CAP + j) * PR:(i * CAP + j + 1) * PR, :] = block


def pick_call(group, pos, tables, srcs):
    rows = len(group) * CAP * PR
    return pl.pallas_call(
        lambda *refs: pick_kernel(group, *refs),
        out_shape=[sds(rows, D)] * NX,
        in_specs=[sspec()] * (1 + NX) + [vspec()] * len(srcs),
        out_specs=[vspec()] * NX,
        compiler_params=params(8),
        cost_estimate=cost(0, NX * rows * D * 8),
        name="pick",
    )(pos, *tables, *srcs)


def send_kernel(row, *refs):
    srcs, out, held = refs[:-2], refs[-2], refs[-1]
    at = 0
    for src in srcs:
        held[at:at + src.shape[0], :] = src[...]
        at += src.shape[0]
    for i in range(CD * NE):
        out[i * PR:(i + 1) * PR, :] = held[pl.ds(pl.multiple_of(row[i], PR), PR), :]


def send_call(row, srcs):
    return pl.pallas_call(
        send_kernel,
        out_shape=sds(CD * NE * PR, D),
        in_specs=[sspec()] + [vspec()] * len(srcs),
        out_specs=vspec(),
        scratch_shapes=[pltpu.VMEM((NZ * NX * CAP * PR, D), F32)],
        compiler_params=params(12),
        cost_estimate=cost(0, 6 << 20),
        name="send",
    )(row, *srcs)


def ring(size, step):
    return [(i, (i + step) % size) for i in range(size)]


SWAP = [(0, 1), (1, 0)]


def shards(node_feats, order, node_count, local_blocks, exp_blocks, virt_blocks, virt_feats,
           w_query, w_key, w_value, w_out, w_up, w_down):
    z, x, y, c = (lax.axis_index(a) for a in ("z", "x", "y", "c"))
    head = y * NC + c
    pos = jnp.stack([(z * NX + x) * (CD * CL), head, c, z, x]).astype(jnp.int32)
    order = order.reshape(CD, CL)

    piece, edge, table, row = first_call(pos, exp_blocks, order, node_feats)

    half = CL // 2
    tie = lax.optimization_barrier

    def both_z(a, b):
        return lax.ppermute(a, "z", ring(NZ, 1)), lax.ppermute(b, "z", ring(NZ, -1))

    def swap(*arrays):
        return [lax.ppermute(t, "c", SWAP) for t in arrays]

    up, down = both_z(piece, piece)
    w = pack_call(w_query.T, w_key.T, w_value.T, w_out.T, w_up, w_down)
    tables = [table] + [lax.ppermute(table, "x", ring(NX, -k)) for k in range(1, NX)]
    held = {0: (piece,), 7: (up,), 1: (down,)}
    up, down, w, edge, *tables = tie((up, down, w, edge, *tables))
    w = lax.all_gather(w, ("y", "c"), axis=0, tiled=True).reshape(CD, D, D)

    def pick(group):
        return pick_call(group, pos, tables, [t for s in group for t in held[s]])

    def exchange(blocks):
        return [blocks[0]] + [lax.ppermute(blocks[k], "x", ring(NX, k)) for k in (1, 2, 3)]

    one = pick(GROUPS[0])
    e_in = lax.ppermute(edge, ("z", "x", "y", "c"), [
        (i * CD + h, (i + s) * CD + h)
        for s, hs in ((1, (0, 1)), (-1, (6, 7)))
        for i in range(NZ * NX) if 0 <= i + s < NZ * NX for h in hs])
    up, down = both_z(up, down)
    held[6], held[2] = (up,), (down,)
    up, down, *_ = tie((up, down, *one))
    one = exchange(one)
    two = pick(GROUPS[1])
    up, down = both_z(up, down)
    held[5], held[3] = (up,), (down,)
    up, down, e_in, *_ = tie((up, down, e_in, *one, *two))
    held[4] = both_z(up[:half], down[half:])
    three = pick(GROUPS[2])
    (e_other,) = swap(tie((e_in, *three))[0])
    e_other, *arrived = tie((e_other, *one, *exchange(two), *exchange(three)))

    sending = send_call(row, arrived)
    xe = lax.all_to_all(sending, ("y", "c"), 0, 0, tiled=True)

    _, w, pos_late = tie((sending, w, pos))
    x_own, q, wv, wo, state = near_call(
        (pos_late, local_blocks, virt_blocks, node_count), (order, node_feats, e_in, e_other, virt_feats, w))
    state, w = tie((state, w))
    wu, wd = prep_call(w)
    result = far_call((pos, exp_blocks, node_count), (xe, q, state, wv, x_own, wo, wu, wd))
    received = lax.all_to_all(result, ("y", "c"), 0, 0, tiled=True)
    return place_call(pos, received, order).T


def solution(mesh):
    grid = Mesh(mesh.devices.reshape(NZ, NX, NY, NC), ("z", "x", "y", "c"))
    dom, head = ("z", "x"), ("y", "c")
    return jax.shard_map(
        shards,
        mesh=grid,
        in_specs=(P(dom, None), P(dom), P(), P(dom, None), P(dom, None), P(dom), P(),
                  P(None, head), P(None, head), P(None, head), P(None, head), P(None, head),
                  P(head, None)),
        out_specs=P(dom, head),
        check_vma=False,
    )
```

```python
import math

import jax
import jax.numpy as jnp
from jax import lax
from jax.experimental import pallas as pl
from jax.experimental.pallas import tpu as pltpu
from jax.sharding import Mesh, PartitionSpec as P

D = 512
HD = 64
FF = 1024
CL = 128
CD = 8
NE = 6
NL = 3
CAP = 3
NZ, NX, NY, NC = 8, 4, 4, 2
PR = CL // (NY * NC)
EK = NE * CL
LK = (NL + 1) * CL
NEG = -1e30
VMEM_BYTES = 67043328
BF = jnp.bfloat16
F32 = jnp.float32
NT = (((1,), (1,)), ((), ()))
NN = (((1,), (0,)), ((), ()))

GROUPS = ((0, 1, 7), (2, 6), (3, 5, 4))


def split2(v):
    hi = v.astype(BF)
    return hi, (v - hi.astype(F32)).astype(BF)


def mm(a, b, dims):
    return lax.dot_general(a, b, dims, preferred_element_type=F32)


def dot3(ah, al, bh, bl, dims):
    return mm(ah, bh, dims) + (mm(ah, bl, dims) + mm(al, bh, dims))


def vspec():
    return pl.BlockSpec(memory_space=pltpu.VMEM)


def hspec():
    return pl.BlockSpec(memory_space=pltpu.HBM)


def sspec():
    return pl.BlockSpec(memory_space=pltpu.SMEM)


def params(mb):
    return pltpu.CompilerParams(vmem_limit_bytes=mb << 20)


def cost(flops, bytes_accessed, transcendentals=0):
    return pl.CostEstimate(flops=flops, bytes_accessed=bytes_accessed, transcendentals=transcendentals)


def sds(*shape, dtype=F32):
    return jax.ShapeDtypeStruct(shape, dtype)


def columns(row):
    return jnp.broadcast_to(row, (CL, CL)).T


def one_hot(cols):
    lanes = lax.broadcasted_iota(jnp.int32, cols.shape, 1).astype(F32)
    parts = [jnp.where(cols == lanes + float(j * CL), 1.0, 0.0).astype(BF) for j in range(CD)]
    return jnp.concatenate(parts, 1)


def first_kernel(pos, exp_ref, order_hbm, nodes_hbm, piece_out, edge_out, table, row,
                 order_ref, nodes, seen, starts, widths, sems):
    base, head, c = pos[0], pos[1], pos[2]
    step = 2 * CL
    parts = CD * CL // step
    fetch = [pltpu.make_async_copy(order_hbm, order_ref, sems.at[0])] + [
        pltpu.make_async_copy(nodes_hbm.at[i * step:(i + 1) * step, :], nodes.at[i * step:(i + 1) * step, :],
                              sems.at[i + 1]) for i in range(parts)]
    for copy in fetch:
        copy.start()
    z, x = pos[3], pos[4]
    start = 0
    for group in GROUPS:
        for p, s in enumerate(group):
            starts[s] = start + p * CAP
            widths[s] = len(group) * CAP
        start += NX * len(group) * CAP
    for i in range(NX * NZ * CAP):
        table[i] = 0
    for i in range(NZ * NX):
        seen[i] = 0

    def place(i, carry):
        for e in range(NE):
            block = exp_ref[i, e]
            owner = lax.shift_right_logical(block, 3)
            rank = seen[owner]
            seen[owner] = rank + 1
            oz = lax.shift_right_logical(owner, 2)
            back = lax.bitwise_and(x - lax.bitwise_and(owner, NX - 1), NX - 1)
            table[back * (NZ * CAP) + oz * CAP + rank] = lax.bitwise_and(block, CD - 1)
            off = lax.bitwise_and(oz - z, NZ - 1)
            row[i * NE + e] = (starts[off] + back * widths[off] + rank) * PR
        return carry

    lax.fori_loop(0, CD, place, 0)
    fetch[0].wait()
    order = (order_ref[...] - base).astype(F32)
    mine = pltpu.roll(order, lax.rem(CL - head * PR, CL), 1)
    col = jnp.concatenate([mine] + [jnp.zeros((CL - CD, CL), F32)], 0).T
    pieces = [jnp.broadcast_to(col[:PR, k:k + 1], (PR, CL)) for k in range(CD)]
    edge = jnp.where(head < NY, CD - NC + c, c)
    edge_row = (order_ref[pl.ds(edge, 1), :] - base).astype(F32)
    pick = one_hot(jnp.concatenate(pieces + [columns(edge_row)], 0))
    rows = jnp.zeros((2 * CL, D), F32)
    for i in range(parts):
        fetch[i + 1].wait()
        hi, lo = split2(nodes[i * step:(i + 1) * step, :])
        some = pick[:, i * step:(i + 1) * step]
        rows = rows + (mm(some, hi, NN) + mm(some, lo, NN))
    piece_out[...] = rows[:CL]
    edge_out[...] = rows[CL:]


def first_call(pos, exp_blocks, order, nodes):
    return pl.pallas_call(
        first_kernel,
        out_shape=[sds(CL, D), sds(CL, D), sds(NX * NZ * CAP, dtype=jnp.int32), sds(CD * NE, dtype=jnp.int32)],
        in_specs=[sspec(), sspec(), hspec(), hspec()],
        out_specs=[vspec()] * 2 + [sspec()] * 2,
        scratch_shapes=[pltpu.VMEM((CD, CL), jnp.int32), pltpu.VMEM((CD * CL, D), F32),
                        pltpu.SMEM((NZ * NX,), jnp.int32), pltpu.SMEM((NZ,), jnp.int32),
                        pltpu.SMEM((NZ,), jnp.int32), pltpu.SemaphoreType.DMA((5,))],
        compiler_params=params(60),
        cost_estimate=cost(10**9, 3 << 20),
        name="first",
    )(pos, exp_blocks, order, nodes)


def pack_kernel(q, k, v, o, up, down, out, sems):
    pairs = [(w, out.at[i * HD:(i + 1) * HD, :]) for i, w in enumerate((q, k, v, o))]
    pairs.append((down, out.at[2 * CL:3 * CL, :]))
    pairs += [(up.at[j * CL:(j + 1) * CL, :], out.at[3 * CL:, j * CL:(j + 1) * CL]) for j in range(4)]
    copies = [pltpu.make_async_copy(src, dst, sems.at[i]) for i, (src, dst) in enumerate(pairs)]
    for copy in copies:
        copy.start()
    for copy in copies:
        copy.wait()


def pack_call(*w):
    return pl.pallas_call(
        pack_kernel,
        out_shape=sds(D, D),
        in_specs=[hspec()] * 6,
        out_specs=vspec(),
        scratch_shapes=[pltpu.SemaphoreType.DMA((9,))],
        compiler_params=params(60),
        cost_estimate=cost(1000, 2 << 20),
        name="pack",
    )(*w)


def near_kernel(pos, local_ref, virt_ref, count_ref, order_ref, nodes_ref, e_in, e_other, virtual_ref, w_hbm,
                x_out, q_out, v_out, o_out, state, kh, kl, w, sem):
    fetch = pltpu.make_async_copy(w_hbm.at[:, :2 * CL, :], w, sem)
    fetch.start()
    base, head, c = pos[0], pos[1], pos[2]
    first = lax.shift_right_logical(base, 7)

    def order_row(r):
        return columns((order_ref[pl.ds(r, 1), :] - base).astype(F32))

    rel = [local_ref[head, j] - first for j in range(NL)]
    rows = [order_row(jnp.clip(r, 0, CD - 1)) for r in rel] + [order_row(head)]
    pick = one_hot(jnp.concatenate(rows, 0))
    nodes = nodes_ref[...]
    hi, lo = split2(nodes)
    got = mm(pick, hi, NN) + mm(pick, lo, NN)
    last = (nodes - hi.astype(F32) - lo.astype(F32)).astype(BF)
    x = got[NL * CL:] + mm(pick[NL * CL:], last, NN)
    x_out[...] = x
    lane = lax.broadcasted_iota(jnp.int32, (1, CL), 1)
    bias = []
    for j in range(NL):
        r = rel[j]
        at = jnp.where(r < 0, r + NC, r - CD)
        edge = jnp.where(at == c, e_in[...], e_other[...])
        keys = jnp.where((r >= 0) & (r < CD), got[j * CL:(j + 1) * CL], edge)
        kh[j * CL:(j + 1) * CL, :], kl[j * CL:(j + 1) * CL, :] = split2(keys)
        bias.append(jnp.where(lane < count_ref[local_ref[head, j]], 0.0, NEG))
    vat = pl.multiple_of(virt_ref[head] * CL, CL)
    kh[NL * CL:, :], kl[NL * CL:, :] = split2(virtual_ref[pl.ds(vat, CL), :])
    bias = jnp.concatenate(bias + [jnp.zeros((1, CL), F32)], 1)

    lanes = lax.broadcasted_iota(jnp.int32, (CL, 2 * HD), 1)
    lowq = lanes < HD
    xh, xl = split2(x)
    fetch.wait()
    for at in range(NY):
        left, right = w[2 * at], w[2 * at + 1]
        wq, wk, wv, wo = (
            split2(jnp.concatenate([left[i * HD:(i + 1) * HD], right[i * HD:(i + 1) * HD]], 0))
            for i in range(4))
        q = dot3(xh, xl, *wq, NT) * (1.0 / math.sqrt(HD))
        both = jnp.concatenate([jnp.where(lowq, q, 0.0), jnp.where(lowq, 0.0, q)], 0)
        q_out[0, at], q_out[1, at] = split2(dot3(*split2(both), *wk, NN))
        v_out[0, at], v_out[1, at] = wv
        rows = slice(at * CL, (at + 1) * CL)
        o_out[0, rows, :], o_out[1, rows, :] = wo

    def body(p, carry):
        s = dot3(q_out[0, p], q_out[1, p], kh[...], kl[...], NT) + bias
        m = jnp.max(s, axis=1, keepdims=True)
        e = jnp.exp(s - m)
        l = jnp.sum(e, axis=1, keepdims=True)
        a = dot3(*split2(e), kh[...], kl[...], NN)
        o = dot3(*split2(a), v_out[0, p], v_out[1, p], NT)
        state[p, :CL, :] = jnp.where(lowq, o[:CL], jnp.where(lanes < HD + HD // 2, m[:CL], l[:CL]))
        state[p, CL:, :] = jnp.where(lowq, jnp.where(lanes < HD // 2, m[CL:], l[CL:]), o[CL:])
        return carry

    lax.fori_loop(0, NY, body, 0)


def near_call(scalars, arrays):
    shapes = [
        sds(CL, D), sds(2, NY, 2 * CL, D, dtype=BF), sds(2, NY, 2 * HD, D, dtype=BF),
        sds(2, D, D, dtype=BF), sds(NY, 2 * CL, 2 * HD),
    ]
    return pl.pallas_call(
        near_kernel,
        out_shape=shapes,
        in_specs=[sspec()] * len(scalars) + [vspec()] * (len(arrays) - 1) + [hspec()],
        out_specs=[vspec()] * len(shapes),
        scratch_shapes=[pltpu.VMEM((LK, D), BF), pltpu.VMEM((LK, D), BF), pltpu.VMEM((CD, 2 * CL, D), F32),
                        pltpu.SemaphoreType.DMA],
        compiler_params=params(60),
        cost_estimate=cost(6 * 10**9, 16 << 20, 1 << 20),
        name="near",
    )(*scalars, *arrays)


def prep_kernel(w_hbm, u_out, d_out, w, sems):
    fetch = [pltpu.make_async_copy(w_hbm.at[i, 2 * CL:, :], w.at[i], sems.at[i]) for i in range(CD)]
    for copy in fetch:
        copy.start()
    for i in range(CD):
        fetch[i].wait()
        rows = slice(i * CL, (i + 1) * CL)
        d_out[0, rows, :], d_out[1, rows, :] = split2(w[i, :CL, :])
        hi, lo = split2(w[i, CL:, :])
        for j in range(4):
            cols = slice(j * CL, (j + 1) * CL)
            u_out[0, cols, rows] = hi[:, cols]
            u_out[1, cols, rows] = lo[:, cols]


def prep_call(weights):
    return pl.pallas_call(
        prep_kernel,
        out_shape=[sds(2, D, FF, dtype=BF), sds(2, FF, D, dtype=BF)],
        in_specs=[hspec()],
        out_specs=[vspec()] * 2,
        scratch_shapes=[pltpu.VMEM((CD, 2 * CL, D), F32), pltpu.SemaphoreType.DMA((CD,))],
        compiler_params=params(60),
        cost_estimate=cost(10**7, 8 << 20),
        name="prep",
    )(weights)


def far_kernel(pos, exp_ref, count_ref, xe_ref, q_hbm, s_hbm, v_hbm, x_hbm, o_hbm, u_hbm, d_hbm,
               out_ref, kh, kl, att, q, st, v, x, wo, u, d, sems):
    first = [pltpu.make_async_copy(q_hbm.at[:, p], q.at[:, p], sems.at[p]) for p in range(NY)]
    later = [pltpu.make_async_copy(src, dst, sems.at[NY + i]) for i, (src, dst) in enumerate(zip(
        (s_hbm, v_hbm, x_hbm, o_hbm, u_hbm, d_hbm), (st, v, x, wo, u, d)))]
    for copy in first:
        copy.start()
    head = pos[1]
    hi, lo = split2(xe_ref[...])
    kh[...] = hi
    kl[...] = lo
    lowq = lax.broadcasted_iota(jnp.int32, (CL, 2 * HD), 1) < HD
    n = lax.broadcasted_iota(jnp.int32, (1, EK), 1)

    def steps(v, width, count):
        return sum(jnp.where(v >= width * k, 1, 0) for k in range(1, count))

    piece = steps(n, NE * PR, CD)
    r = n - piece * (NE * PR)
    entry = steps(r, PR, NE)
    slot = piece * PR + r - entry * PR
    bias = jnp.zeros((1, EK), F32)
    for e in range(NE):
        bad = (entry == e) & (slot >= count_ref[exp_ref[head, e]])
        bias = jnp.where(bad, NEG, bias)

    def scores(p):
        return dot3(q[0, p], q[1, p], kh[...], kl[...], NT) + bias

    def attend(p, s):
        m_near = jnp.concatenate([st[p, :CL, HD:HD + 1], st[p, CL:, :1]], 0)
        half = HD // 2
        l_near = jnp.concatenate([st[p, :CL, HD + half:HD + half + 1], st[p, CL:, half:half + 1]], 0)
        m = jnp.maximum(m_near, jnp.max(s, axis=1, keepdims=True))
        e = jnp.exp(s - m)
        scale = jnp.exp(m_near - m)
        total = jnp.sum(e, axis=1, keepdims=True) + l_near * scale
        a = dot3(*split2(e), kh[...], kl[...], NN)
        o = (dot3(*split2(a), v[0, p], v[1, p], NT) + st[p] * scale) / total
        att[p] = jnp.where(lowq, o[:CL], o[CL:])

    for copy in first:
        copy.wait()
    for copy in later:
        copy.start()
    later[0].wait()
    later[1].wait()

    def body(i, carry):
        one, two = scores(2 * i), scores(2 * i + 1)
        attend(2 * i, one)
        attend(2 * i + 1, two)
        return carry

    lax.fori_loop(0, NY // 2, body, 0)
    ah, al = split2(jnp.concatenate([att[p] for p in range(NY)], 1))
    for copy in later[2:]:
        copy.wait()
    r = x[...] + dot3(ah, al, wo[0], wo[1], NT)
    mean = jnp.sum(r, axis=1, keepdims=True) * (1.0 / D)
    square = jnp.sum(r * r, axis=1, keepdims=True) * (1.0 / D)
    normed = (r - mean) * lax.rsqrt(square - mean * mean + 1e-05)
    hid = dot3(*split2(normed), u[0], u[1], NN)
    act = 0.5 * hid * (1.0 + lax.erf(hid * math.sqrt(0.5)))
    y = r + dot3(*split2(act), d[0], d[1], NN)
    out_ref[...] = y.T


def far_call(scalars, arrays):
    return pl.pallas_call(
        far_kernel,
        out_shape=sds(D, CL),
        in_specs=[sspec()] * len(scalars) + [vspec()] + [hspec()] * (len(arrays) - 1),
        out_specs=vspec(),
        scratch_shapes=[pltpu.VMEM((EK, D), BF), pltpu.VMEM((EK, D), BF), pltpu.VMEM((NY, CL, 2 * HD), F32)]
        + [pltpu.VMEM(a.shape, a.dtype) for a in arrays[1:]] + [pltpu.SemaphoreType.DMA((NY + len(arrays) - 2,))],
        compiler_params=params(50),
        cost_estimate=cost(6 * 10**9, 16 << 20, 1 << 20),
        name="far",
    )(*scalars, *arrays)


def place_kernel(pos, r_ref, order_ref, out_ref):
    full = jnp.concatenate([r_ref[i * HD:(i + 1) * HD, :] for i in range(CD)], 1)
    order = jnp.concatenate([order_ref[i:i + 1, :] for i in range(CD)], 1) - pos[0]
    hi = full.astype(BF)
    rest = full - hi.astype(F32)
    mid = rest.astype(BF)
    low = (rest - mid.astype(F32)).astype(BF)
    parts = jnp.concatenate([hi, mid, low], 0)
    step = 256
    for j in range(CD * CL // step):
        nodes = lax.broadcasted_iota(jnp.int32, (step, CD * CL), 0) + j * step
        pick = jnp.where(nodes == order, 1.0, 0.0).astype(BF)
        t = mm(parts, pick, NT)
        out_ref[:, j * step:(j + 1) * step] = t[:HD] + (t[HD:2 * HD] + t[2 * HD:])


def place_call(pos, received, order):
    return pl.pallas_call(
        place_kernel,
        out_shape=sds(HD, CD * CL),
        in_specs=[sspec(), vspec(), vspec()],
        out_specs=vspec(),
        compiler_params=params(12),
        cost_estimate=cost(4 * 10**8, 1 << 20),
        name="place",
    )(pos, received, order)


def pick_kernel(group, pos, *refs):
    tables, srcs, outs = refs[:NX], refs[NX:-NX], refs[-NX:]
    z = pos[3]
    parts, at = [], 0
    for s in group:
        size = 2 if s == NZ // 2 else 1
        parts.append(srcs[at:at + size])
        at += size

    for k, out in enumerate(outs):
        for i, s in enumerate(group):
            src = parts[i]
            for j in range(CAP):
                b = tables[k][(k * NZ + lax.bitwise_and(z + s, NZ - 1)) * CAP + j]
                if len(src) == 1:
                    block = src[0][pl.ds(pl.multiple_of(b * PR, PR), PR), :]
                else:
                    at = pl.multiple_of(lax.bitwise_and(b, CD // 2 - 1) * PR, PR)
                    block = jnp.where(b < CD // 2, src[0][pl.ds(at, PR), :], src[1][pl.ds(at, PR), :])
                out[(i * CAP + j) * PR:(i * CAP + j + 1) * PR, :] = block


def pick_call(group, pos, tables, srcs):
    rows = len(group) * CAP * PR
    return pl.pallas_call(
        lambda *refs: pick_kernel(group, *refs),
        out_shape=[sds(rows, D)] * NX,
        in_specs=[sspec()] * (1 + NX) + [vspec()] * len(srcs),
        out_specs=[vspec()] * NX,
        compiler_params=params(8),
        cost_estimate=cost(0, NX * rows * D * 8),
        name="pick",
    )(pos, *tables, *srcs)


def send_kernel(row, *refs):
    srcs, out, held = refs[:-2], refs[-2], refs[-1]
    at = 0
    for src in srcs:
        held[at:at + src.shape[0], :] = src[...]
        at += src.shape[0]
    for i in range(CD * NE):
        out[i * PR:(i + 1) * PR, :] = held[pl.ds(pl.multiple_of(row[i], PR), PR), :]


def send_call(row, srcs):
    return pl.pallas_call(
        send_kernel,
        out_shape=sds(CD * NE * PR, D),
        in_specs=[sspec()] + [vspec()] * len(srcs),
        out_specs=vspec(),
        scratch_shapes=[pltpu.VMEM((NZ * NX * CAP * PR, D), F32)],
        compiler_params=params(12),
        cost_estimate=cost(0, 6 << 20),
        name="send",
    )(row, *srcs)


def ring(size, step):
    return [(i, (i + step) % size) for i in range(size)]


SWAP = [(0, 1), (1, 0)]


def shards(node_feats, order, node_count, local_blocks, exp_blocks, virt_blocks, virt_feats,
           w_query, w_key, w_value, w_out, w_up, w_down):
    z, x, y, c = (lax.axis_index(a) for a in ("z", "x", "y", "c"))
    head = y * NC + c
    pos = jnp.stack([(z * NX + x) * (CD * CL), head, c, z, x]).astype(jnp.int32)
    order = order.reshape(CD, CL)

    piece, edge, table, row = first_call(pos, exp_blocks, order, node_feats)

    half = CL // 2
    tie = lax.optimization_barrier

    def both_z(a, b):
        return lax.ppermute(a, "z", ring(NZ, 1)), lax.ppermute(b, "z", ring(NZ, -1))

    def swap(*arrays):
        return [lax.ppermute(t, "c", SWAP) for t in arrays]

    up, down = both_z(piece, piece)
    w = pack_call(w_query.T, w_key.T, w_value.T, w_out.T, w_up, w_down)
    tables = [table] + [lax.ppermute(table, "x", ring(NX, -k)) for k in range(1, NX)]
    held = {0: (piece,), 7: (up,), 1: (down,)}
    up, down, w, edge, *tables = tie((up, down, w, edge, *tables))
    w = lax.all_gather(w, ("y", "c"), axis=0, tiled=True).reshape(CD, D, D)

    def pick(group):
        return pick_call(group, pos, tables, [t for s in group for t in held[s]])

    def exchange(blocks):
        return [blocks[0]] + [lax.ppermute(blocks[k], "x", ring(NX, k)) for k in (1, 2, 3)]

    one = pick(GROUPS[0])
    e_in = lax.ppermute(edge, ("z", "x", "y", "c"), [
        (i * CD + h, (i + s) * CD + h)
        for s, hs in ((1, (0, 1)), (-1, (6, 7)))
        for i in range(NZ * NX) if 0 <= i + s < NZ * NX for h in hs])
    up, down = both_z(up, down)
    held[6], held[2] = (up,), (down,)
    up, down, *_ = tie((up, down, *one))
    one = exchange(one)
    two = pick(GROUPS[1])
    up, down = both_z(up, down)
    held[5], held[3] = (up,), (down,)
    up, down, e_in, *_ = tie((up, down, e_in, *one, *two))
    held[4] = both_z(up[:half], down[half:])
    three = pick(GROUPS[2])
    two, three = exchange(two), exchange(three)
    (e_other,) = swap(tie((e_in, *two))[0])
    e_other, *arrived = tie((e_other, *one, *two, *three))

    sending = send_call(row, arrived)
    xe = lax.all_to_all(sending, ("y", "c"), 0, 0, tiled=True)

    _, w, pos_late = tie((sending, w, pos))
    x_own, q, wv, wo, state = near_call(
        (pos_late, local_blocks, virt_blocks, node_count), (order, node_feats, e_in, e_other, virt_feats, w))
    state, w = tie((state, w))
    wu, wd = prep_call(w)
    result = far_call((pos, exp_blocks, node_count), (xe, q, state, wv, x_own, wo, wu, wd))
    received = lax.all_to_all(result, ("y", "c"), 0, 0, tiled=True)
    return place_call(pos, received, order).T


def solution(mesh):
    grid = Mesh(mesh.devices.reshape(NZ, NX, NY, NC), ("z", "x", "y", "c"))
    dom, head = ("z", "x"), ("y", "c")
    return jax.shard_map(
        shards,
        mesh=grid,
        in_specs=(P(dom, None), P(dom), P(), P(dom, None), P(dom, None), P(dom), P(),
                  P(None, head), P(None, head), P(None, head), P(None, head), P(None, head),
                  P(head, None)),
        out_specs=P(dom, head),
        check_vma=False,
    )
```

```python
import math

import jax
import jax.numpy as jnp
from jax import lax
from jax.experimental import pallas as pl
from jax.experimental.pallas import tpu as pltpu
from jax.sharding import Mesh, PartitionSpec as P

D = 512
HD = 64
FF = 1024
CL = 128
CD = 8
NE = 6
NL = 3
CAP = 3
NZ, NX, NY, NC = 8, 4, 4, 2
PR = CL // (NY * NC)
EK = NE * CL
LK = (NL + 1) * CL
NEG = -1e30
VMEM_BYTES = 67043328
BF = jnp.bfloat16
F32 = jnp.float32
NT = (((1,), (1,)), ((), ()))
NN = (((1,), (0,)), ((), ()))

GROUPS = ((0, 1, 7), (2, 6), (3, 5, 4))


def split2(v):
    hi = v.astype(BF)
    return hi, (v - hi.astype(F32)).astype(BF)


def mm(a, b, dims):
    return lax.dot_general(a, b, dims, preferred_element_type=F32)


def dot3(ah, al, bh, bl, dims):
    return mm(ah, bh, dims) + (mm(ah, bl, dims) + mm(al, bh, dims))


def vspec():
    return pl.BlockSpec(memory_space=pltpu.VMEM)


def hspec():
    return pl.BlockSpec(memory_space=pltpu.HBM)


def sspec():
    return pl.BlockSpec(memory_space=pltpu.SMEM)


def params(mb):
    return pltpu.CompilerParams(vmem_limit_bytes=mb << 20)


def cost(flops, bytes_accessed, transcendentals=0):
    return pl.CostEstimate(flops=flops, bytes_accessed=bytes_accessed, transcendentals=transcendentals)


def sds(*shape, dtype=F32):
    return jax.ShapeDtypeStruct(shape, dtype)


def columns(row):
    return jnp.broadcast_to(row, (CL, CL)).T


def one_hot(cols):
    lanes = lax.broadcasted_iota(jnp.int32, cols.shape, 1).astype(F32)
    parts = [jnp.where(cols == lanes + float(j * CL), 1.0, 0.0).astype(BF) for j in range(CD)]
    return jnp.concatenate(parts, 1)


def first_kernel(pos, exp_ref, order_hbm, nodes_hbm, piece_out, edge_out, table, row,
                 order_ref, nodes, seen, starts, widths, sems):
    base, head, c = pos[0], pos[1], pos[2]
    step = 2 * CL
    parts = CD * CL // step
    fetch = [pltpu.make_async_copy(order_hbm, order_ref, sems.at[0])] + [
        pltpu.make_async_copy(nodes_hbm.at[i * step:(i + 1) * step, :], nodes.at[i * step:(i + 1) * step, :],
                              sems.at[i + 1]) for i in range(parts)]
    for copy in fetch:
        copy.start()
    z, x = pos[3], pos[4]
    start = 0
    for group in GROUPS:
        for p, s in enumerate(group):
            starts[s] = start + p * CAP
            widths[s] = len(group) * CAP
        start += NX * len(group) * CAP
    for i in range(NX * NZ * CAP):
        table[i] = 0
    for i in range(NZ * NX):
        seen[i] = 0

    def place(i, carry):
        for e in range(NE):
            block = exp_ref[i, e]
            owner = lax.shift_right_logical(block, 3)
            rank = seen[owner]
            seen[owner] = rank + 1
            oz = lax.shift_right_logical(owner, 2)
            back = lax.bitwise_and(x - lax.bitwise_and(owner, NX - 1), NX - 1)
            table[back * (NZ * CAP) + oz * CAP + rank] = lax.bitwise_and(block, CD - 1)
            off = lax.bitwise_and(oz - z, NZ - 1)
            row[i * NE + e] = (starts[off] + back * widths[off] + rank) * PR
        return carry

    lax.fori_loop(0, CD, place, 0)
    fetch[0].wait()
    order = (order_ref[...] - base).astype(F32)
    mine = pltpu.roll(order, lax.rem(CL - head * PR, CL), 1)
    col = jnp.concatenate([mine] + [jnp.zeros((CL - CD, CL), F32)], 0).T
    pieces = [jnp.broadcast_to(col[:PR, k:k + 1], (PR, CL)) for k in range(CD)]
    edge = jnp.where(head < NY, CD - NC + c, c)
    edge_row = (order_ref[pl.ds(edge, 1), :] - base).astype(F32)
    pick = one_hot(jnp.concatenate(pieces + [columns(edge_row)], 0))
    rows = jnp.zeros((2 * CL, D), F32)
    for i in range(parts):
        fetch[i + 1].wait()
        hi, lo = split2(nodes[i * step:(i + 1) * step, :])
        some = pick[:, i * step:(i + 1) * step]
        rows = rows + (mm(some, hi, NN) + mm(some, lo, NN))
    piece_out[...] = rows[:CL]
    edge_out[...] = rows[CL:]


def first_call(pos, exp_blocks, order, nodes):
    return pl.pallas_call(
        first_kernel,
        out_shape=[sds(CL, D), sds(CL, D), sds(NX * NZ * CAP, dtype=jnp.int32), sds(CD * NE, dtype=jnp.int32)],
        in_specs=[sspec(), sspec(), hspec(), hspec()],
        out_specs=[vspec()] * 2 + [sspec()] * 2,
        scratch_shapes=[pltpu.VMEM((CD, CL), jnp.int32), pltpu.VMEM((CD * CL, D), F32),
                        pltpu.SMEM((NZ * NX,), jnp.int32), pltpu.SMEM((NZ,), jnp.int32),
                        pltpu.SMEM((NZ,), jnp.int32), pltpu.SemaphoreType.DMA((5,))],
        compiler_params=params(60),
        cost_estimate=cost(10**9, 3 << 20),
        name="first",
    )(pos, exp_blocks, order, nodes)


def pack_kernel(q, k, v, o, up, down, out, sems):
    pairs = [(w, out.at[i * HD:(i + 1) * HD, :]) for i, w in enumerate((q, k, v, o))]
    pairs.append((down, out.at[2 * CL:3 * CL, :]))
    pairs += [(up.at[j * CL:(j + 1) * CL, :], out.at[3 * CL:, j * CL:(j + 1) * CL]) for j in range(4)]
    copies = [pltpu.make_async_copy(src, dst, sems.at[i]) for i, (src, dst) in enumerate(pairs)]
    for copy in copies:
        copy.start()
    for copy in copies:
        copy.wait()


def pack_call(*w):
    return pl.pallas_call(
        pack_kernel,
        out_shape=sds(D, D),
        in_specs=[hspec()] * 6,
        out_specs=vspec(),
        scratch_shapes=[pltpu.SemaphoreType.DMA((9,))],
        compiler_params=params(60),
        cost_estimate=cost(1000, 2 << 20),
        name="pack",
    )(*w)


def near_kernel(pos, local_ref, virt_ref, count_ref, order_ref, nodes_ref, e_in, e_other, virtual_ref, w_hbm,
                x_out, q_out, v_out, o_out, state, kh, kl, w, sem):
    fetch = pltpu.make_async_copy(w_hbm.at[:, :2 * CL, :], w, sem)
    fetch.start()
    base, head, c = pos[0], pos[1], pos[2]
    first = lax.shift_right_logical(base, 7)

    def order_row(r):
        return columns((order_ref[pl.ds(r, 1), :] - base).astype(F32))

    rel = [local_ref[head, j] - first for j in range(NL)]
    rows = [order_row(jnp.clip(r, 0, CD - 1)) for r in rel] + [order_row(head)]
    pick = one_hot(jnp.concatenate(rows, 0))
    nodes = nodes_ref[...]
    hi, lo = split2(nodes)
    got = mm(pick, hi, NN) + mm(pick, lo, NN)
    last = (nodes - hi.astype(F32) - lo.astype(F32)).astype(BF)
    x = got[NL * CL:] + mm(pick[NL * CL:], last, NN)
    x_out[...] = x
    lane = lax.broadcasted_iota(jnp.int32, (1, CL), 1)
    bias = []
    for j in range(NL):
        r = rel[j]
        at = jnp.where(r < 0, r + NC, r - CD)
        edge = jnp.where(at == c, e_in[...], e_other[...])
        keys = jnp.where((r >= 0) & (r < CD), got[j * CL:(j + 1) * CL], edge)
        kh[j * CL:(j + 1) * CL, :], kl[j * CL:(j + 1) * CL, :] = split2(keys)
        bias.append(jnp.where(lane < count_ref[local_ref[head, j]], 0.0, NEG))
    vat = pl.multiple_of(virt_ref[head] * CL, CL)
    kh[NL * CL:, :], kl[NL * CL:, :] = split2(virtual_ref[pl.ds(vat, CL), :])
    bias = jnp.concatenate(bias + [jnp.zeros((1, CL), F32)], 1)

    lanes = lax.broadcasted_iota(jnp.int32, (CL, 2 * HD), 1)
    lowq = lanes < HD
    xh, xl = split2(x)
    fetch.wait()
    for at in range(NY):
        left, right = w[2 * at], w[2 * at + 1]
        wq, wk, wv, wo = (
            split2(jnp.concatenate([left[i * HD:(i + 1) * HD], right[i * HD:(i + 1) * HD]], 0))
            for i in range(4))
        q = dot3(xh, xl, *wq, NT) * (1.0 / math.sqrt(HD))
        both = jnp.concatenate([jnp.where(lowq, q, 0.0), jnp.where(lowq, 0.0, q)], 0)
        q_out[0, at], q_out[1, at] = split2(dot3(*split2(both), *wk, NN))
        v_out[0, at], v_out[1, at] = wv
        rows = slice(at * CL, (at + 1) * CL)
        o_out[0, rows, :], o_out[1, rows, :] = wo

    def body(p, carry):
        s = dot3(q_out[0, p], q_out[1, p], kh[...], kl[...], NT) + bias
        m = jnp.max(s, axis=1, keepdims=True)
        e = jnp.exp(s - m)
        l = jnp.sum(e, axis=1, keepdims=True)
        a = dot3(*split2(e), kh[...], kl[...], NN)
        o = dot3(*split2(a), v_out[0, p], v_out[1, p], NT)
        state[p, :CL, :] = jnp.where(lowq, o[:CL], jnp.where(lanes < HD + HD // 2, m[:CL], l[:CL]))
        state[p, CL:, :] = jnp.where(lowq, jnp.where(lanes < HD // 2, m[CL:], l[CL:]), o[CL:])
        return carry

    lax.fori_loop(0, NY, body, 0)


def near_call(scalars, arrays):
    shapes = [
        sds(CL, D), sds(2, NY, 2 * CL, D, dtype=BF), sds(2, NY, 2 * HD, D, dtype=BF),
        sds(2, D, D, dtype=BF), sds(NY, 2 * CL, 2 * HD),
    ]
    return pl.pallas_call(
        near_kernel,
        out_shape=shapes,
        in_specs=[sspec()] * len(scalars) + [vspec()] * (len(arrays) - 1) + [hspec()],
        out_specs=[vspec()] * len(shapes),
        scratch_shapes=[pltpu.VMEM((LK, D), BF), pltpu.VMEM((LK, D), BF), pltpu.VMEM((CD, 2 * CL, D), F32),
                        pltpu.SemaphoreType.DMA],
        compiler_params=params(60),
        cost_estimate=cost(6 * 10**9, 16 << 20, 1 << 20),
        name="near",
    )(*scalars, *arrays)


def prep_kernel(w_hbm, u_out, d_out, w, sems):
    fetch = [pltpu.make_async_copy(w_hbm.at[i, 2 * CL:, :], w.at[i], sems.at[i]) for i in range(CD)]
    for copy in fetch:
        copy.start()
    for i in range(CD):
        fetch[i].wait()
        rows = slice(i * CL, (i + 1) * CL)
        d_out[0, rows, :], d_out[1, rows, :] = split2(w[i, :CL, :])
        hi, lo = split2(w[i, CL:, :])
        for j in range(4):
            cols = slice(j * CL, (j + 1) * CL)
            u_out[0, cols, rows] = hi[:, cols]
            u_out[1, cols, rows] = lo[:, cols]


def prep_call(weights):
    return pl.pallas_call(
        prep_kernel,
        out_shape=[sds(2, D, FF, dtype=BF), sds(2, FF, D, dtype=BF)],
        in_specs=[hspec()],
        out_specs=[vspec()] * 2,
        scratch_shapes=[pltpu.VMEM((CD, 2 * CL, D), F32), pltpu.SemaphoreType.DMA((CD,))],
        compiler_params=params(60),
        cost_estimate=cost(10**7, 8 << 20),
        name="prep",
    )(weights)


def far_kernel(pos, exp_ref, count_ref, xe_ref, q_hbm, s_hbm, v_hbm, x_hbm, o_hbm, u_hbm, d_hbm,
               out_ref, kh, kl, att, q, st, v, x, wo, u, d, sems):
    first = [pltpu.make_async_copy(q_hbm.at[:, p], q.at[:, p], sems.at[p]) for p in range(NY)]
    later = [pltpu.make_async_copy(src, dst, sems.at[NY + i]) for i, (src, dst) in enumerate(zip(
        (s_hbm, v_hbm, x_hbm, o_hbm, u_hbm, d_hbm), (st, v, x, wo, u, d)))]
    for copy in first:
        copy.start()
    head = pos[1]
    hi, lo = split2(xe_ref[...])
    kh[...] = hi
    kl[...] = lo
    lowq = lax.broadcasted_iota(jnp.int32, (CL, 2 * HD), 1) < HD
    n = lax.broadcasted_iota(jnp.int32, (1, EK), 1)

    def steps(v, width, count):
        return sum(jnp.where(v >= width * k, 1, 0) for k in range(1, count))

    piece = steps(n, NE * PR, CD)
    r = n - piece * (NE * PR)
    entry = steps(r, PR, NE)
    slot = piece * PR + r - entry * PR
    bias = jnp.zeros((1, EK), F32)
    for e in range(NE):
        bad = (entry == e) & (slot >= count_ref[exp_ref[head, e]])
        bias = jnp.where(bad, NEG, bias)

    def scores(p):
        return dot3(q[0, p], q[1, p], kh[...], kl[...], NT) + bias

    def attend(p, s):
        m_near = jnp.concatenate([st[p, :CL, HD:HD + 1], st[p, CL:, :1]], 0)
        half = HD // 2
        l_near = jnp.concatenate([st[p, :CL, HD + half:HD + half + 1], st[p, CL:, half:half + 1]], 0)
        m = jnp.maximum(m_near, jnp.max(s, axis=1, keepdims=True))
        e = jnp.exp(s - m)
        scale = jnp.exp(m_near - m)
        total = jnp.sum(e, axis=1, keepdims=True) + l_near * scale
        a = dot3(*split2(e), kh[...], kl[...], NN)
        o = (dot3(*split2(a), v[0, p], v[1, p], NT) + st[p] * scale) / total
        att[p] = jnp.where(lowq, o[:CL], o[CL:])

    for copy in first:
        copy.wait()
    for copy in later:
        copy.start()
    later[0].wait()
    later[1].wait()

    def body(i, carry):
        one, two = scores(2 * i), scores(2 * i + 1)
        attend(2 * i, one)
        attend(2 * i + 1, two)
        return carry

    lax.fori_loop(0, NY // 2, body, 0)
    ah, al = split2(jnp.concatenate([att[p] for p in range(NY)], 1))
    for copy in later[2:]:
        copy.wait()
    r = x[...] + dot3(ah, al, wo[0], wo[1], NT)
    mean = jnp.sum(r, axis=1, keepdims=True) * (1.0 / D)
    square = jnp.sum(r * r, axis=1, keepdims=True) * (1.0 / D)
    normed = (r - mean) * lax.rsqrt(square - mean * mean + 1e-05)
    hid = dot3(*split2(normed), u[0], u[1], NN)
    act = 0.5 * hid * (1.0 + lax.erf(hid * math.sqrt(0.5)))
    y = r + dot3(*split2(act), d[0], d[1], NN)
    out_ref[...] = y.T


def far_call(scalars, arrays):
    return pl.pallas_call(
        far_kernel,
        out_shape=sds(D, CL),
        in_specs=[sspec()] * len(scalars) + [vspec()] + [hspec()] * (len(arrays) - 1),
        out_specs=vspec(),
        scratch_shapes=[pltpu.VMEM((EK, D), BF), pltpu.VMEM((EK, D), BF), pltpu.VMEM((NY, CL, 2 * HD), F32)]
        + [pltpu.VMEM(a.shape, a.dtype) for a in arrays[1:]] + [pltpu.SemaphoreType.DMA((NY + len(arrays) - 2,))],
        compiler_params=params(50),
        cost_estimate=cost(6 * 10**9, 16 << 20, 1 << 20),
        name="far",
    )(*scalars, *arrays)


def place_kernel(pos, r_ref, order_ref, out_ref):
    full = jnp.concatenate([r_ref[i * HD:(i + 1) * HD, :] for i in range(CD)], 1)
    order = jnp.concatenate([order_ref[i:i + 1, :] for i in range(CD)], 1) - pos[0]
    hi = full.astype(BF)
    rest = full - hi.astype(F32)
    mid = rest.astype(BF)
    low = (rest - mid.astype(F32)).astype(BF)
    parts = jnp.concatenate([hi, mid, low], 0)
    step = 256
    for j in range(CD * CL // step):
        nodes = lax.broadcasted_iota(jnp.int32, (step, CD * CL), 0) + j * step
        pick = jnp.where(nodes == order, 1.0, 0.0).astype(BF)
        t = mm(parts, pick, NT)
        out_ref[:, j * step:(j + 1) * step] = t[:HD] + (t[HD:2 * HD] + t[2 * HD:])


def place_call(pos, received, order):
    return pl.pallas_call(
        place_kernel,
        out_shape=sds(HD, CD * CL),
        in_specs=[sspec(), vspec(), vspec()],
        out_specs=vspec(),
        compiler_params=params(12),
        cost_estimate=cost(4 * 10**8, 1 << 20),
        name="place",
    )(pos, received, order)


def pick_kernel(group, pos, *refs):
    tables, srcs, outs = refs[:NX], refs[NX:-NX], refs[-NX:]
    z = pos[3]
    parts, at = [], 0
    for s in group:
        size = 2 if s == NZ // 2 else 1
        parts.append(srcs[at:at + size])
        at += size

    for k, out in enumerate(outs):
        for i, s in enumerate(group):
            src = parts[i]
            for j in range(CAP):
                b = tables[k][(k * NZ + lax.bitwise_and(z + s, NZ - 1)) * CAP + j]
                if len(src) == 1:
                    block = src[0][pl.ds(pl.multiple_of(b * PR, PR), PR), :]
                else:
                    at = pl.multiple_of(lax.bitwise_and(b, CD // 2 - 1) * PR, PR)
                    block = jnp.where(b < CD // 2, src[0][pl.ds(at, PR), :], src[1][pl.ds(at, PR), :])
                out[(i * CAP + j) * PR:(i * CAP + j + 1) * PR, :] = block


def pick_call(group, pos, tables, srcs):
    rows = len(group) * CAP * PR
    return pl.pallas_call(
        lambda *refs: pick_kernel(group, *refs),
        out_shape=[sds(rows, D)] * NX,
        in_specs=[sspec()] * (1 + NX) + [vspec()] * len(srcs),
        out_specs=[vspec()] * NX,
        compiler_params=params(8),
        cost_estimate=cost(0, NX * rows * D * 8),
        name="pick",
    )(pos, *tables, *srcs)


def send_kernel(row, *refs):
    srcs, out, held = refs[:-2], refs[-2], refs[-1]
    at = 0
    for src in srcs:
        held[at:at + src.shape[0], :] = src[...]
        at += src.shape[0]
    for i in range(CD * NE):
        out[i * PR:(i + 1) * PR, :] = held[pl.ds(pl.multiple_of(row[i], PR), PR), :]


def send_call(row, srcs):
    return pl.pallas_call(
        send_kernel,
        out_shape=sds(CD * NE * PR, D),
        in_specs=[sspec()] + [vspec()] * len(srcs),
        out_specs=vspec(),
        scratch_shapes=[pltpu.VMEM((NZ * NX * CAP * PR, D), F32)],
        compiler_params=params(12),
        cost_estimate=cost(0, 6 << 20),
        name="send",
    )(row, *srcs)


def ring(size, step):
    return [(i, (i + step) % size) for i in range(size)]


SWAP = [(0, 1), (1, 0)]


def shards(node_feats, order, node_count, local_blocks, exp_blocks, virt_blocks, virt_feats,
           w_query, w_key, w_value, w_out, w_up, w_down):
    z, x, y, c = (lax.axis_index(a) for a in ("z", "x", "y", "c"))
    head = y * NC + c
    pos = jnp.stack([(z * NX + x) * (CD * CL), head, c, z, x]).astype(jnp.int32)
    order = order.reshape(CD, CL)

    piece, edge, table, row = first_call(pos, exp_blocks, order, node_feats)

    half = CL // 2
    tie = lax.optimization_barrier

    def both_z(a, b):
        return lax.ppermute(a, "z", ring(NZ, 1)), lax.ppermute(b, "z", ring(NZ, -1))

    def swap(*arrays):
        return [lax.ppermute(t, "c", SWAP) for t in arrays]

    up, down = both_z(piece, piece)
    w = pack_call(w_query.T, w_key.T, w_value.T, w_out.T, w_up, w_down)
    tables = [table] + [lax.ppermute(table, "x", ring(NX, -k)) for k in range(1, NX)]
    held = {0: (piece,), 7: (up,), 1: (down,)}
    up, down, w, edge, *tables = tie((up, down, w, edge, *tables))
    w = lax.all_gather(w, ("y", "c"), axis=0, tiled=True).reshape(CD, D, D)

    def pick(group):
        return pick_call(group, pos, tables, [t for s in group for t in held[s]])

    def exchange(blocks):
        return [blocks[0]] + [lax.ppermute(blocks[k], "x", ring(NX, k)) for k in (1, 2, 3)]

    one = pick(GROUPS[0])
    up, down = both_z(up, down)
    held[6], held[2] = (up,), (down,)
    up, down, edge, *_ = tie((up, down, edge, *one))
    e_in = lax.ppermute(edge, ("z", "x", "y", "c"), [
        (i * CD + h, (i + s) * CD + h)
        for s, hs in ((1, (0, 1)), (-1, (6, 7)))
        for i in range(NZ * NX) if 0 <= i + s < NZ * NX for h in hs])
    one = exchange(one)
    two = pick(GROUPS[1])
    up, down = both_z(up, down)
    held[5], held[3] = (up,), (down,)
    up, down, e_in, *_ = tie((up, down, e_in, *one, *two))
    held[4] = both_z(up[:half], down[half:])
    three = pick(GROUPS[2])
    (e_other,) = swap(tie((e_in, *three))[0])
    e_other, *arrived = tie((e_other, *one, *exchange(two), *exchange(three)))

    sending = send_call(row, arrived)
    xe = lax.all_to_all(sending, ("y", "c"), 0, 0, tiled=True)

    _, w, pos_late = tie((sending, w, pos))
    x_own, q, wv, wo, state = near_call(
        (pos_late, local_blocks, virt_blocks, node_count), (order, node_feats, e_in, e_other, virt_feats, w))
    state, w = tie((state, w))
    wu, wd = prep_call(w)
    result = far_call((pos, exp_blocks, node_count), (xe, q, state, wv, x_own, wo, wu, wd))
    received = lax.all_to_all(result, ("y", "c"), 0, 0, tiled=True)
    return place_call(pos, received, order).T


def solution(mesh):
    grid = Mesh(mesh.devices.reshape(NZ, NX, NY, NC), ("z", "x", "y", "c"))
    dom, head = ("z", "x"), ("y", "c")
    return jax.shard_map(
        shards,
        mesh=grid,
        in_specs=(P(dom, None), P(dom), P(), P(dom, None), P(dom, None), P(dom), P(),
                  P(None, head), P(None, head), P(None, head), P(None, head), P(None, head),
                  P(head, None)),
        out_specs=P(dom, head),
        check_vma=False,
    )
```
